32 devices in a mesh: dp: 16 (over z, y, x), fsdp: 2 (over core).
Axes of the slice: x: 2, y: 2, z: 4, core: 2. Of those that a mesh axis runs over, the one named last changes fastest.
Arguments:
- tokens: bfloat16 [2, 18432, 1024], P(None, ('dp', 'fsdp')), may hold values from -6 to 6
- cotangent: bfloat16 [2, 18432, 1024], P(None, ('dp', 'fsdp')), may hold values from -6 to 6
- images: int32 [2, 16, 3], P(None, 'dp'), may hold values from 0 to 4, as said below
- attention_weight: float32 [4096, 1024], P(('dp', 'fsdp')), may hold values from -1 to 1
- attention_first: float32 [4096, 1024], P(('dp', 'fsdp')), may hold values from -0.00048828125 to 0.00048828125
- attention_second: float32 [4096, 1024], P(('dp', 'fsdp')), may hold values from 7.7838555e-11 to 3.1135422e-10
- widen_weight: float32 [1024, 5632], P(None, ('dp', 'fsdp')), may hold values from -0.1875 to 0.1875
- widen_first: float32 [1024, 5632], P(None, ('dp', 'fsdp')), may hold values from -0.00048828125 to 0.00048828125
- widen_second: float32 [1024, 5632], P(None, ('dp', 'fsdp')), may hold values from 7.7838555e-11 to 3.1135422e-10
- narrow_weight: float32 [2816, 1024], P(('dp', 'fsdp')), may hold values from -0.109375 to 0.109375
- narrow_first: float32 [2816, 1024], P(('dp', 'fsdp')), may hold values from -0.00048828125 to 0.00048828125
- narrow_second: float32 [2816, 1024], P(('dp', 'fsdp')), may hold values from 7.7838555e-11 to 3.1135422e-10
- norm_gains: float32 [2048], P(('dp', 'fsdp')), may hold values from 0.5 to 1.5
- gains_first: float32 [2048], P(('dp', 'fsdp')), may hold values from -0.0014648438 to 0.0014648438
- gains_second: float32 [2048], P(('dp', 'fsdp')), may hold values from 7.00547e-10 to 2.802188e-09
Outputs:
- block_output: float32 [2, 18432, 1024], P(None, ('dp', 'fsdp'))
- input_grad: float32 [2, 18432, 1024], P(None, ('dp', 'fsdp'))
- attention_master: float32 [4096, 1024], P(('dp', 'fsdp'))
- attention_mean: float32 [4096, 1024], P(('dp', 'fsdp'))
- attention_square: float32 [4096, 1024], P(('dp', 'fsdp'))
- widen_master: float32 [1024, 5632], P(None, ('dp', 'fsdp'))
- widen_mean: float32 [1024, 5632], P(None, ('dp', 'fsdp'))
- widen_square: float32 [1024, 5632], P(None, ('dp', 'fsdp'))
- narrow_master: float32 [2816, 1024], P(('dp', 'fsdp'))
- narrow_mean: float32 [2816, 1024], P(('dp', 'fsdp'))
- narrow_square: float32 [2816, 1024], P(('dp', 'fsdp'))
- gains_master: float32 [2048], P(('dp', 'fsdp'))
- gains_mean: float32 [2048], P(('dp', 'fsdp'))
- gains_square: float32 [2048], P(('dp', 'fsdp'))
- grad_norm: float32 [], replicated
The draws below stay inside these ranges and needn't reach their ends.
Inputs may be any that keep to these rules, and one draw needn't show every extreme that they name: Each packed row's 3 slots are one of (4, 0, 0), (1, 1, 1), (2, 1, 0), (1, 2, 0): the images of the row's items in order, a 0 marking an empty slot.
All inputs are finite; a program needn't handle non-finite values.
Results may differ from the reference program's by a relative error of at most 0.014.
The reference program's roundings to bfloat16 on the way count: a program that leaves them out, or rounds other values in their place, can miss the bound.
Values may be sent and summed in bfloat16 or wider, within the bound.
A program may use at most 320 MiB of HBM per device.

```python
import math
import jax
import jax.numpy as jnp
from jax import lax

D = 1024
H = 16
HD = 64
FF = 2816
TEXT = 128
PATCH = 256
SLOTS = 3
MICRO = 2
ROW = 1152
TOKENS = 18432
N_DP = 16


def draw_images(key, part):
    pattern_table = jnp.array([[4, 0, 0], [1, 1, 1], [2, 1, 0], [1, 2, 0]], dtype=jnp.int32)
    picked = jax.random.randint(key, (MICRO, N_DP), 0, 4)
    return pattern_table[picked]


def draw_attention_weight(key, part):
    base_draw = jnp.clip(jax.random.normal(key, (4 * D, D), jnp.float32), -2.5, 2.5)
    block_index = jnp.arange(4 * D) // D
    row_scale = jnp.where(block_index < 2, (4.0 * D) ** (-0.5), jnp.where(block_index == 2, D ** (-0.5), (D / 16.0) ** (-0.5)))
    return base_draw * row_scale[:, None].astype(jnp.float32)


def levels(key, extent, split, smallest, top_value):
    factor_of, own = 1.0, jax.random.fold_in(key, 6)
    for axis_at, parts in split:
        draws = jnp.exp(jax.random.uniform(jax.random.fold_in(own, axis_at), (parts,), jnp.float32, smallest / len(split), top_value / len(split)))
        factor_of = factor_of * jnp.repeat(draws, extent[axis_at] // parts).reshape([-1 if axis == axis_at else 1 for axis in range(len(extent))])
    return factor_of


def gaussian(rng, shape, width, most, cuts=(), held_as=jnp.bfloat16):
    loudness = levels(rng, shape, cuts, -0.22, 0.18) if cuts else 1.0
    values = jax.random.normal(rng, shape, jnp.float32) * width * loudness
    return jnp.minimum(jnp.maximum(values, -most), most).astype(held_as)


def setup_inputs(seed: int = 0) -> dict:
    keys = jax.random.split(jax.random.key(seed), 16)
    tokens = gaussian(keys[0], (MICRO, TOKENS, D), 1.0, 6.0, ((1, 32),))
    cotangent = gaussian(keys[1], (MICRO, TOKENS, D), 1.0, 6.0, ((1, 32),))
    images = draw_images(jax.random.fold_in(keys[15], 71), 0)
    attention_weight = draw_attention_weight(jax.random.fold_in(keys[15], 71), 0)
    attention_first = gaussian(keys[4], (4 * D, D), (0.111 / (4 * D * D + 3 * D * FF + 2 * D) ** 0.5), 0.00048828125, ((0, 32),), jnp.float32)
    attention_second = jnp.clip(jnp.exp(math.log(3.1135422018380154e-10) - 1.3862944 * jax.random.uniform(keys[5], (4 * D, D), jnp.float32) ** levels(keys[5], (4 * D, D), ((0, 32),), -0.2, 0.2)), 7.783855504595039e-11, 3.1135422018380154e-10)
    widen_weight = gaussian(keys[6], (D, 2 * FF), D ** -0.5, 0.1875, ((1, 32),), jnp.float32)
    widen_first = gaussian(keys[7], (D, 2 * FF), (0.111 / (4 * D * D + 3 * D * FF + 2 * D) ** 0.5), 0.00048828125, ((1, 32),), jnp.float32)
    widen_second = jnp.clip(jnp.exp(math.log(3.1135422018380154e-10) - 1.3862944 * jax.random.uniform(keys[8], (D, 2 * FF), jnp.float32) ** levels(keys[8], (D, 2 * FF), ((1, 32),), -0.2, 0.2)), 7.783855504595039e-11, 3.1135422018380154e-10)
    narrow_weight = gaussian(keys[9], (FF, D), FF ** -0.5, 0.109375, ((0, 32),), jnp.float32)
    narrow_first = gaussian(keys[10], (FF, D), (0.111 / (4 * D * D + 3 * D * FF + 2 * D) ** 0.5), 0.00048828125, ((0, 32),), jnp.float32)
    narrow_second = jnp.clip(jnp.exp(math.log(3.1135422018380154e-10) - 1.3862944 * jax.random.uniform(keys[11], (FF, D), jnp.float32) ** levels(keys[11], (FF, D), ((0, 32),), -0.2, 0.2)), 7.783855504595039e-11, 3.1135422018380154e-10)
    norm_gains = jnp.clip(1.0 + 0.1 * jax.random.normal(keys[12], (2 * D,), jnp.float32), 0.5, 1.5)
    gains_first = gaussian(keys[13], (2 * D,), (0.333 / (4 * D * D + 3 * D * FF + 2 * D) ** 0.5), 0.0014648438, ((0, 32),), jnp.float32)
    gains_second = jnp.clip(jnp.exp(math.log(2.802188037165365e-09) - 1.3862944 * jax.random.uniform(keys[14], (2 * D,), jnp.float32) ** levels(keys[14], (2 * D,), ((0, 32),), -0.2, 0.2)), 7.005470092913413e-10, 2.802188037165365e-09)
    return dict(tokens=tokens, cotangent=cotangent, images=images, attention_weight=attention_weight, attention_first=attention_first, attention_second=attention_second, widen_weight=widen_weight, widen_first=widen_first, widen_second=widen_second, narrow_weight=narrow_weight, narrow_first=narrow_first, narrow_second=narrow_second, norm_gains=norm_gains, gains_first=gains_first, gains_second=gains_second)


NORM_EPS = 1e-06
MASKED = -1000000000.0
BETA_FIRST = 0.9
BETA_SECOND = 0.999
ADAM_EPS = 1e-08
MATRIX_RATE = 0.05
GAIN_RATE = 0.3
DECAY = 0.1
CLIP_LIMIT = 1.0
STEP_VALUE = 10.0

@jax.custom_vjp
def low(v):
    return lax.optimization_barrier(v.astype(jnp.bfloat16)).astype(jnp.float32)

@jax.custom_vjp
def low_back(v):
    return v

def low_keep(v):
    return (low(v), None)

def low_pass(kept, grad):
    return (grad,)

def back_keep(v):
    return (v, None)

def back_low(kept, grad):
    return (low(grad),)
low.defvjp(low_keep, low_pass)
low_back.defvjp(back_keep, back_low)

def both_ways(values):
    return low(low_back(values))

def exact_dot(left, right):
    return jnp.dot(left, right, precision=lax.Precision.HIGHEST)

def gelu_tanh(values):
    return 0.5 * values * (1.0 + jnp.tanh(0.7978845608028654 * (values + 0.044715 * values * values * values)))

def rms_scale(values, gain_vector):
    return values * lax.rsqrt(lax.optimization_barrier(jnp.mean(values * values, axis=-1, keepdims=True)) + NORM_EPS) * gain_vector

def segment_ids(counts):
    item_sizes = jnp.where(counts > 0, TEXT + PATCH * counts, 0).astype(jnp.int32)
    item_ends = jnp.cumsum(item_sizes).astype(jnp.int32)
    places = jnp.arange(ROW, dtype=jnp.int32)
    return lax.optimization_barrier(jnp.sum((places[:, None] >= item_ends[None, :]).astype(jnp.int32), axis=1))

def block_layer(params, rows_in, same_item):
    attention_low, widen_low, narrow_low, gains_low = [low(master) for master in params]
    matrices = attention_low.reshape(4, D, D)
    normed = low(rms_scale(rows_in, gains_low[:D]))
    query_rows = both_ways(exact_dot(normed, matrices[0]))
    key_rows = both_ways(exact_dot(normed, matrices[1]))
    value_rows = both_ways(exact_dot(normed, matrices[2]))

    def split_heads(values):
        return values.reshape(ROW, H, HD).transpose(1, 0, 2)

    def one_head(pieces):
        query_head, key_head, value_head = pieces
        scores = low_back(exact_dot(query_head, key_head.T))
        scores = jnp.where(same_item, scores, MASKED)
        row_top = lax.optimization_barrier(jnp.max(scores, axis=-1, keepdims=True))
        shifted = jnp.exp(scores - row_top)
        attend = shifted / lax.optimization_barrier(jnp.sum(shifted, axis=-1, keepdims=True))
        return exact_dot(low(attend), value_head)
    mixed_heads = lax.map(jax.checkpoint(one_head), (split_heads(query_rows), split_heads(key_rows), split_heads(value_rows)))
    mixed_heads = both_ways(mixed_heads.transpose(1, 0, 2).reshape(ROW, D))
    hidden_one = rows_in + low_back(exact_dot(mixed_heads, matrices[3]))
    second = low(rms_scale(hidden_one, gains_low[D:]))
    gate_pre = low_back(exact_dot(second, widen_low[:, :FF]))
    upward = low_back(exact_dot(second, widen_low[:, FF:]))
    hidden = low(gelu_tanh(gate_pre) * upward)
    return hidden_one + low_back(exact_dot(hidden, narrow_low))

def adam_update(master, first, second, gradient, factors, rate, decay):
    clip_factor, first_fix, second_fix = factors
    clipped = clip_factor * gradient
    first_new = BETA_FIRST * first + (1.0 - BETA_FIRST) * clipped
    second_new = BETA_SECOND * second + (1.0 - BETA_SECOND) * clipped * clipped
    master_new = master - rate * (first_new / first_fix / (jnp.sqrt(second_new / second_fix) + ADAM_EPS) + decay * master)
    return (master_new, first_new, second_new)

def reference(tokens, cotangent, images, attention_weight, attention_first, attention_second, widen_weight, widen_first, widen_second, narrow_weight, narrow_first, narrow_second, norm_gains, gains_first, gains_second):
    row_inputs = tokens.reshape(MICRO * N_DP, ROW, D)
    row_grads = cotangent.reshape(MICRO * N_DP, ROW, D)
    row_counts = images.reshape(MICRO * N_DP, SLOTS)
    params = (attention_weight, widen_weight, narrow_weight, norm_gains)

    def one_row(running, pieces):
        rows_in, grad_rows, counts = pieces
        seg_row = segment_ids(counts)
        same_item = seg_row[:, None] == seg_row[None, :]
        result, pullback = jax.vjp(lambda weights, inputs: block_layer(weights, inputs, same_item), params, rows_in.astype(jnp.float32))
        weight_grads, input_rows = pullback(grad_rows.astype(jnp.float32))
        running = tuple((total + part_grad for total, part_grad in zip(running, weight_grads)))
        return (running, (result, input_rows))
    start_grads = tuple((jnp.zeros_like(master) for master in params))
    totals, (results, input_rows) = lax.scan(one_row, start_grads, (row_inputs, row_grads, row_counts))
    block_output = results.reshape(MICRO, N_DP * ROW, D)
    input_grad = input_rows.reshape(MICRO, N_DP * ROW, D)
    squares = jnp.sum(totals[0] * totals[0]) + jnp.sum(totals[1] * totals[1]) + jnp.sum(totals[2] * totals[2]) + jnp.sum(totals[3] * totals[3])
    grad_norm = jnp.sqrt(squares)
    clip_factor = jnp.minimum(1.0, CLIP_LIMIT / (grad_norm + 1e-06))
    step_value = jnp.float32(STEP_VALUE)
    factors = (clip_factor, 1.0 - jnp.power(jnp.float32(BETA_FIRST), step_value), 1.0 - jnp.power(jnp.float32(BETA_SECOND), step_value))
    attention_master, attention_mean, attention_square = adam_update(attention_weight, attention_first, attention_second, totals[0], factors, MATRIX_RATE, DECAY)
    widen_master, widen_mean, widen_square = adam_update(widen_weight, widen_first, widen_second, totals[1], factors, MATRIX_RATE, DECAY)
    narrow_master, narrow_mean, narrow_square = adam_update(narrow_weight, narrow_first, narrow_second, totals[2], factors, MATRIX_RATE, DECAY)
    gains_master, gains_mean, gains_square = adam_update(norm_gains, gains_first, gains_second, totals[3], factors, GAIN_RATE, 0.0)
    return (block_output, input_grad, attention_master, attention_mean, attention_square, widen_master, widen_mean, widen_square, narrow_master, narrow_mean, narrow_square, gains_master, gains_mean, gains_square, grad_norm)
```

```python
import functools

import jax
import jax.numpy as jnp
from jax import lax
from jax.experimental import pallas as pl
from jax.experimental.pallas import tpu as pltpu
from jax.sharding import PartitionSpec as P

HD = 64
TEXT = 128
PATCH = 256
ROW = 1152
WIDTH = 1024
HALF = ROW // 2
TILE = 384
WINDOWS = ((0, 640), (0, 1024), (384, 1152))
FF_BLOCK = 256

NORM_EPS = 1e-06
MASKED = -1000000000.0
BETA_FIRST = 0.9
BETA_SECOND = 0.999
ADAM_EPS = 1e-08
MATRIX_RATE = 0.05
GAIN_RATE = 0.3
DECAY = 0.1
CLIP_LIMIT = 1.0
STEP_VALUE = 10.0
GELU_SCALE = 0.7978845608028654
GELU_CUBE = 0.044715

BF16 = jnp.bfloat16
F32 = jnp.float32
MESH = pl.DeviceIdType.MESH
ANY = pl.BlockSpec(memory_space=pl.ANY)
VMEM_WHOLE = pl.BlockSpec(memory_space=pltpu.VMEM)
DMA = pltpu.SemaphoreType.DMA
VMEM_LIMIT = 60 * 2**20

NT = (((1,), (1,)), ((), ()))
TN = (((0,), (0,)), ((), ()))


def dot(left, right, dims=(((1,), (0,)), ((), ()))):
    return lax.dot_general(left, right, dims, preferred_element_type=F32)


class Place:
    def __init__(self):
        self.dp = lax.axis_index("dp")
        self.core = lax.axis_index("fsdp")
        self.z = self.dp // 4
        self.y = lax.rem(self.dp // 2, 2)
        self.x = lax.rem(self.dp, 2)
        flip_y = 1 - self.y
        flip_x = 1 - self.x
        is_zero = self.core == 0
        self.own = (self.y, self.x)
        self.first = (jnp.where(is_zero, self.y, flip_y), jnp.where(is_zero, flip_x, self.x))
        self.second = (jnp.where(is_zero, flip_y, self.y), jnp.where(is_zero, self.x, flip_x))
        self.across = (flip_y, flip_x)

    def at(self, z, spot):
        return (z * 4 + spot[0] * 2 + spot[1], self.core)

    def above(self, step):
        return self.at(lax.rem(self.z + step, 4), self.own)

    def to_first(self):
        return self.at(self.z, self.first)

    def to_second(self):
        return self.at(self.z, self.second)

    def sibling(self):
        return (self.dp, 1 - self.core)

    def greet(self):
        barrier = pltpu.get_barrier_semaphore()
        peers = [self.above(1), self.above(2), self.above(3)]
        peers += [self.to_first(), self.to_second(), self.sibling()]
        for peer in peers:
            pl.semaphore_signal(barrier, inc=1, device_id=peer, device_id_type=MESH)
        pl.semaphore_wait(barrier, len(peers))


def remote(source, target, send_sem, recv_sem, device):
    return pltpu.make_async_remote_copy(
        src_ref=source,
        dst_ref=target,
        send_sem=send_sem,
        recv_sem=recv_sem,
        device_id=device,
        device_id_type=MESH,
    )


def gather_kernel(chunks, arrays, *refs):
    ins = refs[:arrays]
    tokens, cotangent = refs[arrays : arrays + 2]
    outs = refs[arrays + 2 : 2 * arrays + 2]
    tokens_row, cotangent_row = refs[2 * arrays + 2 : 2 * arrays + 4]
    (own_sem, z_send, z_recv, p_send, p_recv, c_send, c_recv, t_own, t_send, t_recv) = refs[
        2 * arrays + 4 :
    ]
    here = Place()
    here.greet()
    count = len(chunks)
    core = here.core

    halves = []
    for index, (source, target) in enumerate(
        ((tokens, tokens_row), (cotangent, cotangent_row))
    ):
        halves.append(
            (
                pltpu.make_async_copy(source.at[core], target.at[core], t_own.at[index]),
                remote(
                    source.at[1 - core],
                    target.at[core],
                    t_send.at[index],
                    t_recv.at[index],
                    here.sibling(),
                ),
            )
        )

    def spot(k, where):
        array, start, rows = chunks[k]
        return outs[array].at[:, where[0], where[1], core, pl.ds(start, rows), :]

    def mine(k):
        array, start, rows = chunks[k]
        return (
            ins[array].at[pl.ds(start, rows), :],
            outs[array].at[here.z, here.y, here.x, core, pl.ds(start, rows), :],
        )

    def keep(k):
        source, target = mine(k)
        return pltpu.make_async_copy(source, target, own_sem.at[k])

    def along_z(k, step):
        source, target = mine(k)
        return remote(
            source, target, z_send.at[k, step - 1], z_recv.at[k, step - 1], here.above(step)
        )

    def plane(k, index, where, device):
        return remote(
            spot(k, where), spot(k, where), p_send.at[k, index], p_recv.at[k, index], device
        )

    def to_first(k):
        return plane(k, 0, here.own, here.to_first())

    def to_second(k):
        return plane(k, 1, here.own, here.to_second())

    def pass_on(k):
        return plane(k, 2, here.first, here.to_second())

    columns = (here.own, here.first, here.second, here.across)

    def to_sibling(k, index):
        where = columns[index]
        return remote(
            spot(k, where), spot(k, where), c_send.at[k, index], c_recv.at[k, index], here.sibling()
        )

    for tick in range(count + 3):
        if tick < count:
            keep(tick).start()
            for step in (2, 1, 3):
                along_z(tick, step).start()
        if tick == 0:
            for local, across in halves:
                across.start()
                local.start()
        k = tick - 1
        if 0 <= k < count:
            keep(k).wait()
            for step in (1, 2, 3):
                along_z(k, step).wait_recv()
            to_second(k).start()
            to_first(k).start()
            to_sibling(k, 0).start()
        k = tick - 2
        if 0 <= k < count:
            to_first(k).wait_recv()
            pass_on(k).start()
            to_sibling(k, 1).start()
            to_second(k).wait_recv()
            to_sibling(k, 2).start()
        k = tick - 3
        if 0 <= k < count:
            pass_on(k).wait_recv()
            to_sibling(k, 3).start()
    for k in range(count):
        for step in (1, 2, 3):
            along_z(k, step).wait_send()
        to_first(k).wait_send()
        to_second(k).wait_send()
        pass_on(k).wait_send()
        for index in range(4):
            to_sibling(k, index).wait()
    for local, across in halves:
        local.wait()
        across.wait()


def cut(index, rows, most):
    pieces = -(-rows // most)
    step = -(-rows // (pieces * 16)) * 16
    return [(index, at, min(step, rows - at)) for at in range(0, rows, step)]


def gather_all(shards, tokens, cotangent, most=48):
    chunks = []
    for index, shard in enumerate(shards):
        chunks += cut(index, shard.shape[0], most)
    count = len(chunks)
    gathered = [jax.ShapeDtypeStruct((4, 2, 2, 2) + s.shape, s.dtype) for s in shards]
    rows = jax.ShapeDtypeStruct((2, HALF, WIDTH), BF16)
    results = pl.pallas_call(
        functools.partial(gather_kernel, chunks, len(shards)),
        out_shape=gathered + [rows, rows],
        in_specs=[ANY] * (len(shards) + 2),
        out_specs=[ANY] * (len(shards) + 2),
        scratch_shapes=[
            DMA((count,)),
            DMA((count, 3)),
            DMA((count, 3)),
            DMA((count, 3)),
            DMA((count, 3)),
            DMA((count, 4)),
            DMA((count, 4)),
            DMA((2,)),
            DMA((2,)),
            DMA((2,)),
        ],
        compiler_params=pltpu.CompilerParams(collective_id=0, has_side_effects=True),
        name="gather_weights",
    )(*shards, tokens, cotangent)
    return results[:-2], results[-2], results[-1]


def reduce_kernel(chunks, arrays, *refs):
    ins = refs[:arrays]
    gains, result, forward = refs[arrays : arrays + 3]
    outs = refs[arrays + 3 : 2 * arrays + 3]
    gains_out, square_out, result_out, forward_out = refs[2 * arrays + 3 : 2 * arrays + 7]
    own = refs[2 * arrays + 7 : 3 * arrays + 7]
    from_core = refs[3 * arrays + 7 : 4 * arrays + 7]
    from_second = refs[4 * arrays + 7 : 5 * arrays + 7]
    from_first = refs[5 * arrays + 7 : 6 * arrays + 7]
    from_z = refs[6 * arrays + 7 : 7 * arrays + 7]
    (
        small,
        tiny,
        own_sem,
        c_send,
        c_recv,
        p_send,
        p_recv,
        z_send,
        z_recv,
        g_send,
        g_recv,
        n_send,
        n_recv,
        t_own,
        t_send,
        t_recv,
    ) = refs[7 * arrays + 7 :]
    here = Place()
    here.greet()
    count = len(chunks)
    core = here.core

    halves = []
    for index, (source, target) in enumerate(((result, result_out), (forward, forward_out))):
        halves.append(
            (
                pltpu.make_async_copy(source.at[core], target.at[core], t_own.at[index]),
                remote(
                    source.at[1 - core],
                    target.at[core],
                    t_send.at[index],
                    t_recv.at[index],
                    here.sibling(),
                ),
            )
        )

    def part(k):
        array, start, rows = chunks[k]
        return array, pl.ds(start, rows)

    def load(k):
        array, rows = part(k)
        return pltpu.make_async_copy(
            ins[array].at[:, :, :, core, rows, :], own[array].at[:, :, :, rows, :], own_sem.at[k]
        )

    def swap_core(k):
        array, rows = part(k)
        return remote(
            ins[array].at[:, :, :, 1 - core, rows, :],
            from_core[array].at[:, :, :, rows, :],
            c_send.at[k],
            c_recv.at[k],
            here.sibling(),
        )

    def send_second(k, index):
        array, rows = part(k)
        where = here.second if index == 0 else here.across
        return remote(
            own[array].at[:, where[0], where[1], rows, :],
            from_second[array].at[index, :, rows, :],
            p_send.at[k, index],
            p_recv.at[k, index],
            here.to_second(),
        )

    def send_first(k):
        array, rows = part(k)
        return remote(
            own[array].at[:, here.first[0], here.first[1], rows, :],
            from_first[array].at[:, rows, :],
            p_send.at[k, 2],
            p_recv.at[k, 2],
            here.to_first(),
        )

    def send_z(k, step):
        array, rows = part(k)
        other = lax.rem(here.z + step, 4)
        return remote(
            own[array].at[other, here.y, here.x, rows, :],
            from_z[array].at[step - 1, rows, :],
            z_send.at[k, step - 1],
            z_recv.at[k, step - 1],
            here.above(step),
        )

    def add(mine, other):
        return (mine.astype(F32) + other.astype(F32)).astype(BF16)

    def after_core(k):
        array, rows = part(k)

        def body(i, carry):
            z, y, x = i // 4, lax.rem(i // 2, 2), lax.rem(i, 2)
            own[array][z, y, x, rows, :] = add(
                own[array][z, y, x, rows, :], from_core[array][z, y, x, rows, :]
            )
            return carry

        lax.fori_loop(0, 16, body, 0)

    def after_second(k, index):
        array, rows = part(k)
        where = here.own if index == 0 else here.first

        def body(z, carry):
            own[array][z, where[0], where[1], rows, :] = add(
                own[array][z, where[0], where[1], rows, :], from_second[array][index, z, rows, :]
            )
            return carry

        lax.fori_loop(0, 4, body, 0)

    def after_first(k):
        array, rows = part(k)

        def body(z, carry):
            own[array][z, here.y, here.x, rows, :] = add(
                own[array][z, here.y, here.x, rows, :], from_first[array][z, rows, :]
            )
            return carry

        lax.fori_loop(0, 4, body, 0)

    def after_z(k):
        array, rows = part(k)
        total = own[array][here.z, here.y, here.x, rows, :].astype(F32)
        for step in range(3):
            total = total + from_z[array][step, rows, :].astype(F32)
        outs[array][rows, :] = total
        return jnp.sum((total * total).reshape(-1, 8, 128), axis=0)

    def everywhere(buffer, value, send, recv):
        stages = (here.sibling(), here.to_first(), here.to_second())
        for index, device in enumerate(stages):
            buffer[2 * index] = value
            copy = remote(
                buffer.at[2 * index],
                buffer.at[2 * index + 1],
                send.at[index],
                recv.at[index],
                device,
            )
            copy.start()
            yield
            copy.wait()
            value = buffer[2 * index] + buffer[2 * index + 1]
        buffer[6 + here.z] = value
        copies = [
            remote(
                buffer.at[6 + here.z],
                buffer.at[6 + here.z],
                send.at[2 + step],
                recv.at[2 + step],
                here.above(step),
            )
            for step in (1, 2, 3)
        ]
        for copy in copies:
            copy.start()
        yield
        for copy in copies:
            copy.wait()
        yield (buffer[6] + buffer[7]) + (buffer[8] + buffer[9])

    squares = jnp.zeros((8, 128), F32)
    gains_steps = everywhere(small, gains[...], g_send, g_recv)
    for tick in range(count + 4):
        if tick < count:
            swap_core(tick).start()
            load(tick).start()
        if tick == 1:
            for local, across in halves:
                across.start()
                local.start()
        k = tick - 1
        if 0 <= k < count:
            load(k).wait()
            swap_core(k).wait_recv()
            after_core(k)
            for index in (1, 0):
                send_second(k, index).start()
        k = tick - 2
        if 0 <= k < count:
            send_second(k, 1).wait_recv()
            after_second(k, 1)
            send_first(k).start()
            send_second(k, 0).wait_recv()
            after_second(k, 0)
        k = tick - 3
        if 0 <= k < count:
            send_first(k).wait_recv()
            after_first(k)
            for step in (2, 1, 3):
                send_z(k, step).start()
        k = tick - 4
        if 0 <= k < count:
            for step in (1, 2, 3):
                send_z(k, step).wait_recv()
            squares = squares + after_z(k)
        if tick < 5:
            gains_total = next(gains_steps)
    gains_out[...] = gains_total
    norm_steps = everywhere(tiny, squares, n_send, n_recv)
    for _ in range(5):
        total = next(norm_steps)
    square_out[...] = jnp.broadcast_to(
        jnp.sum(total) + jnp.sum(gains_total * gains_total), (8, 128)
    )
    for k in range(count):
        swap_core(k).wait_send()
        for index in (1, 0):
            send_second(k, index).wait_send()
        send_first(k).wait_send()
        for step in (1, 2, 3):
            send_z(k, step).wait_send()
    for local, across in halves:
        local.wait()
        across.wait()


def reduce_all(gradients, gains, result, forward, most=48):
    chunks = []
    for index, gradient in enumerate(gradients):
        chunks += cut(index, gradient.shape[4], most)
    count, arrays = len(chunks), len(gradients)
    shapes = [g.shape[4:] for g in gradients]
    padded = [(-(-s[0] // 16) * 16, s[1]) for s in shapes]
    exchanged = jax.ShapeDtypeStruct((2, HALF, WIDTH), F32)
    scratch = [pltpu.VMEM((4, 2, 2) + s, BF16) for s in padded]
    scratch += [pltpu.VMEM((4, 2, 2) + s, BF16) for s in padded]
    scratch += [pltpu.VMEM((2, 4) + s, BF16) for s in padded]
    scratch += [pltpu.VMEM((4,) + s, BF16) for s in padded]
    scratch += [pltpu.VMEM((3,) + s, BF16) for s in padded]
    scratch += [
        pltpu.VMEM((10, 16, 128), F32),
        pltpu.VMEM((10, 8, 128), F32),
        DMA((count,)),
        DMA((count,)),
        DMA((count,)),
        DMA((count, 3)),
        DMA((count, 3)),
        DMA((count, 3)),
        DMA((count, 3)),
        DMA((6,)),
        DMA((6,)),
        DMA((6,)),
        DMA((6,)),
        DMA((2,)),
        DMA((2,)),
        DMA((2,)),
    ]
    return pl.pallas_call(
        functools.partial(reduce_kernel, chunks, arrays),
        out_shape=[jax.ShapeDtypeStruct(s, F32) for s in shapes]
        + [
            jax.ShapeDtypeStruct((16, 128), F32),
            jax.ShapeDtypeStruct((8, 128), F32),
            exchanged,
            exchanged,
        ],
        in_specs=[ANY] * arrays + [VMEM_WHOLE, ANY, ANY],
        out_specs=[VMEM_WHOLE] * arrays + [VMEM_WHOLE, VMEM_WHOLE, ANY, ANY],
        scratch_shapes=scratch,
        compiler_params=pltpu.CompilerParams(
            collective_id=1, has_side_effects=True, vmem_limit_bytes=VMEM_LIMIT
        ),
        name="reduce_gradients",
    )(*gradients, gains, result, forward)


def item_ends(counts):
    sizes = [jnp.where(counts[i] > 0, TEXT + PATCH * counts[i], 0) for i in range(3)]
    return sizes[0], sizes[0] + sizes[1], sizes[0] + sizes[1] + sizes[2]


def segments(ends, start, size, axis):
    shape = (size, 1) if axis == 0 else (1, size)
    place = start + lax.broadcasted_iota(jnp.int32, shape, axis)
    one = jnp.ones(shape, jnp.int32)
    none = jnp.zeros(shape, jnp.int32)
    return sum(jnp.where(place >= end, one, none) for end in ends)


def attend_kernel(counts, q_ref, k_ref, v_ref, o_ref, log_ref):
    pair = pl.program_id(0)
    ends = item_ends(counts)
    lane = lax.broadcasted_iota(jnp.int32, (1, 2 * HD), 1)
    in_head = (lane < HD, lane >= HD)

    @pl.when(pair == 0)
    def _():
        log_ref[...] = jnp.zeros_like(log_ref)

    def run(masked):
        for index in range(ROW // TILE):
            low, high = WINDOWS[index] if masked else (0, ROW)
            rows = pl.ds(index * TILE, TILE)
            query = q_ref[0, rows, :]
            key = k_ref[0, low:high, :]
            value = v_ref[0, low:high, :]
            if masked:
                same = segments(ends, index * TILE, TILE, 0) == segments(ends, low, high - low, 1)
            mixed = []
            logs = log_ref[rows, :]
            for head in range(2):
                scores = dot(jnp.where(in_head[head], query, jnp.zeros_like(query)), key, NT)
                if masked:
                    scores = jnp.where(same, scores, MASKED)
                top = jnp.max(scores, axis=-1, keepdims=True)
                weight = jnp.exp(scores - top).astype(BF16)
                both = dot(weight, jnp.where(in_head[head], value, jnp.ones_like(value)))
                other = pltpu.roll(both, HD, 1)
                mixed.append(both / other)
                total = jnp.where(in_head[head], other, both)
                logs = jnp.where(lane == 2 * pair + head, top + jnp.log(total), logs)
            log_ref[rows, :] = logs
            o_ref[rows, :] = jnp.where(in_head[0], mixed[0], mixed[1]).astype(BF16)

    whole = ends[0] == ROW

    @pl.when(whole)
    def _():
        run(False)

    @pl.when(jnp.logical_not(whole))
    def _():
        run(True)


def attend(counts, projected):
    pairs = WIDTH // (2 * HD)

    def pick(which):
        return pl.BlockSpec((1, ROW, 2 * HD), lambda p, c, which=which: (which, 0, p))

    return pl.pallas_call(
        attend_kernel,
        out_shape=[
            jax.ShapeDtypeStruct((ROW, WIDTH), BF16),
            jax.ShapeDtypeStruct((ROW, 128), F32),
        ],
        grid_spec=pltpu.PrefetchScalarGridSpec(
            num_scalar_prefetch=1,
            grid=(pairs,),
            in_specs=[pick(0), pick(1), pick(2)],
            out_specs=[
                pl.BlockSpec((ROW, 2 * HD), lambda p, c: (0, p)),
                pl.BlockSpec((ROW, 128), lambda p, c: (0, 0)),
            ],
        ),
        compiler_params=pltpu.CompilerParams(vmem_limit_bytes=VMEM_LIMIT),
        name="attend",
    )(counts, projected, projected, projected)


def attend_back_kernel(counts, q_ref, k_ref, v_ref, o_ref, do_ref, log_ref, out_ref, dk, dv):
    pair = pl.program_id(0)
    ends = item_ends(counts)
    lane = lax.broadcasted_iota(jnp.int32, (1, 2 * HD), 1)
    in_head = (lane < HD, lane >= HD)
    pick = jnp.where(
        (lax.broadcasted_iota(jnp.int32, (8, 2 * HD), 1) < HD)
        == (lax.broadcasted_iota(jnp.int32, (8, 2 * HD), 0) == 0),
        jnp.ones((8, 2 * HD), F32),
        jnp.zeros((8, 2 * HD), F32),
    )

    def only(values, head):
        return jnp.where(in_head[head], values, jnp.zeros_like(values))

    def run(masked):
        dk[...] = jnp.zeros_like(dk)
        dv[...] = jnp.zeros_like(dv)
        for index in range(ROW // TILE):
            low, high = WINDOWS[index] if masked else (0, ROW)
            rows = pl.ds(index * TILE, TILE)
            query = q_ref[0, rows, :]
            grad = do_ref[rows, :]
            key = k_ref[0, low:high, :]
            value = v_ref[0, low:high, :]
            inner = lax.dot_general(
                pick,
                grad.astype(F32) * o_ref[rows, :].astype(F32),
                NT,
                precision=lax.Precision.HIGHEST,
                preferred_element_type=F32,
            )
            if masked:
                same = segments(ends, low, high - low, 0) == segments(ends, index * TILE, TILE, 1)
            dq = None
            for head in range(2):
                log_total = log_ref[pl.ds(2 * pair + head, 1), index * TILE : (index + 1) * TILE]
                scores = dot(only(key, head), query, NT)
                if masked:
                    scores = jnp.where(same, scores, MASKED)
                weight = jnp.exp(scores - log_total)
                down = dot(only(value, head), grad, NT)
                slope = (weight * (down - inner[head : head + 1, :])).astype(BF16)
                dv[low:high, :] += dot(weight.astype(BF16), only(grad, head))
                dk[low:high, :] += dot(slope, only(query, head))
                step = dot(slope, only(key, head), TN)
                dq = step if dq is None else dq + step
            out_ref[0, rows, :] = dq.astype(BF16)
        out_ref[1] = dk[...].astype(BF16)
        out_ref[2] = dv[...].astype(BF16)

    whole = ends[0] == ROW

    @pl.when(whole)
    def _():
        run(False)

    @pl.when(jnp.logical_not(whole))
    def _():
        run(True)


def attend_back(counts, projected, mixed, grad_mixed, log_rows):
    pairs = WIDTH // (2 * HD)

    def pick(which):
        return pl.BlockSpec((1, ROW, 2 * HD), lambda p, c, which=which: (which, 0, p))

    column = pl.BlockSpec((ROW, 2 * HD), lambda p, c: (0, p))
    return pl.pallas_call(
        attend_back_kernel,
        out_shape=jax.ShapeDtypeStruct((3, ROW, WIDTH), BF16),
        grid_spec=pltpu.PrefetchScalarGridSpec(
            num_scalar_prefetch=1,
            grid=(pairs,),
            in_specs=[
                pick(0),
                pick(1),
                pick(2),
                column,
                column,
                pl.BlockSpec((2 * pairs, ROW), lambda p, c: (0, 0)),
            ],
            out_specs=pl.BlockSpec((3, ROW, 2 * HD), lambda p, c: (0, 0, p)),
            scratch_shapes=[pltpu.VMEM((ROW, 2 * HD), F32), pltpu.VMEM((ROW, 2 * HD), F32)],
        ),
        compiler_params=pltpu.CompilerParams(vmem_limit_bytes=VMEM_LIMIT),
        name="attend_back",
    )(counts, projected, projected, projected, mixed, grad_mixed, log_rows)


def feed_kernel(
    n2_ref, cot_ref, h1_ref, gain_ref, widen_ref, narrow_ref,
    result_ref, dh1_ref, e_ref, gain_grad_ref, widen_grad_ref, narrow_grad_ref,
    back,
):
    step = pl.program_id(0)
    n2 = n2_ref[...]
    cot = cot_ref[...]
    wide_gate, wide_up, narrow = widen_ref[0], widen_ref[1], narrow_ref[...]
    gate = dot(n2, wide_gate, NT)
    up = dot(n2, wide_up, NT)
    down = dot(cot, narrow, NT)
    square = gate * gate
    bend = jnp.tanh(GELU_SCALE * gate * (1.0 + GELU_CUBE * square))
    half = 0.5 * (1.0 + bend)
    curve = gate * half
    slope = half + 0.5 * gate * (1.0 - bend * bend) * (
        GELU_SCALE * (1.0 + 3.0 * GELU_CUBE * square)
    )
    hidden = (curve * up).astype(BF16)
    grad_gate = (down * up * slope).astype(BF16)
    grad_up = (down * curve).astype(BF16)
    narrow_grad_ref[...] = dot(hidden, cot, TN).astype(BF16)
    widen_grad_ref[0] = dot(grad_gate, n2, TN).astype(BF16)
    widen_grad_ref[1] = dot(grad_up, n2, TN).astype(BF16)

    @pl.when(step == 0)
    def _():
        result_ref[...] = h1_ref[...]
        back[...] = jnp.zeros_like(back)

    result_ref[...] += dot(hidden, narrow)
    back[...] += dot(grad_gate, wide_gate) + dot(grad_up, wide_up)

    @pl.when(step == pl.num_programs(0) - 1)
    def _():
        gain = gain_ref[...]

        def tile(i, total):
            rows = pl.ds(pl.multiple_of(i * 64, 64), 64)
            h1 = h1_ref[rows, :]
            grad = back[rows, :]
            scale = lax.rsqrt(jnp.mean(h1 * h1, axis=-1, keepdims=True) + NORM_EPS)
            lifted = gain * grad
            inner = jnp.mean(h1 * lifted, axis=-1, keepdims=True)
            dh1 = (
                cot_ref[rows, :].astype(F32)
                + scale * lifted
                - h1 * (scale * scale * scale * inner)
            )
            dh1_ref[rows, :] = dh1
            e_ref[rows, :] = dh1.astype(BF16)
            return total + jnp.sum((grad * h1 * scale).reshape(8, 8, WIDTH), axis=0)

        total = lax.fori_loop(0, ROW // 64, tile, jnp.zeros((8, WIDTH), F32))
        gain_grad_ref[...] = jnp.sum(total, axis=0, keepdims=True)


def feed(n2, cot, h1, gain, widen, narrow):
    hidden = narrow.shape[0]
    steps = hidden // FF_BLOCK
    whole = lambda *shape: pl.BlockSpec(shape, lambda j: (0,) * len(shape))
    once = lambda *shape: pl.BlockSpec(
        shape, lambda j: (0,) * len(shape), pipeline_mode=pl.Buffered(1)
    )
    wide = pl.BlockSpec((2, FF_BLOCK, WIDTH), lambda j: (0, j, 0))
    tall = pl.BlockSpec((FF_BLOCK, WIDTH), lambda j: (j, 0))
    return pl.pallas_call(
        feed_kernel,
        grid=(steps,),
        out_shape=[
            jax.ShapeDtypeStruct((ROW, WIDTH), F32),
            jax.ShapeDtypeStruct((ROW, WIDTH), F32),
            jax.ShapeDtypeStruct((ROW, WIDTH), BF16),
            jax.ShapeDtypeStruct((1, WIDTH), F32),
            jax.ShapeDtypeStruct((2, hidden, WIDTH), BF16),
            jax.ShapeDtypeStruct((hidden, WIDTH), BF16),
        ],
        in_specs=[
            once(ROW, WIDTH),
            once(ROW, WIDTH),
            once(ROW, WIDTH),
            whole(1, WIDTH),
            wide,
            tall,
        ],
        out_specs=[
            once(ROW, WIDTH),
            once(ROW, WIDTH),
            once(ROW, WIDTH),
            whole(1, WIDTH),
            wide,
            tall,
        ],
        scratch_shapes=[pltpu.VMEM((ROW, WIDTH), F32)],
        compiler_params=pltpu.CompilerParams(vmem_limit_bytes=VMEM_LIMIT),
        name="feed",
    )(n2, cot, h1, gain, widen, narrow)


def rms_scale(values, gain_vector):
    return (
        values
        * lax.rsqrt(jnp.mean(values * values, axis=-1, keepdims=True) + NORM_EPS)
        * gain_vector
    )


def layer(counts, inputs_low, cot, attention, widen, narrow, gains):
    first_gain = gains[:WIDTH].astype(F32)
    second_gain = gains[WIDTH:].astype(F32)
    inputs = inputs_low.astype(F32)
    normed = rms_scale(inputs, first_gain).astype(BF16)
    projected = jnp.einsum(
        "sd,jde->jse", normed, attention[:3], preferred_element_type=F32
    ).astype(BF16)
    mixed, log_columns = attend(counts, projected)
    log_rows = log_columns[:, : WIDTH // HD].T
    h1 = inputs + dot(mixed, attention[3])
    n2 = rms_scale(h1, second_gain).astype(BF16)
    result, dh1, e, grad_gain_two, grad_widen, grad_narrow = feed(
        n2, cot, h1, second_gain[None], widen, narrow
    )
    grad_out = dot(mixed, e, TN).astype(BF16)
    grad_mixed = dot(e, attention[3], NT).astype(BF16)
    grad_projected = attend_back(counts, projected, mixed, grad_mixed, log_rows)
    grad_qkv = jnp.einsum(
        "sd,jse->jde", normed, grad_projected, preferred_element_type=F32
    ).astype(BF16)
    grad_normed = jnp.einsum(
        "jse,jde->sd", grad_projected, attention[:3], preferred_element_type=F32
    )
    scale = lax.rsqrt(jnp.mean(inputs * inputs, axis=-1, keepdims=True) + NORM_EPS)
    lifted = first_gain * grad_normed
    inner = jnp.mean(inputs * lifted, axis=-1, keepdims=True)
    input_rows = dh1 + scale * lifted - inputs * (scale * scale * scale * inner)
    grad_gain_one = jnp.sum(grad_normed * inputs * scale, axis=0)
    grad_attention = jnp.concatenate([grad_qkv, grad_out[None]], axis=0)
    grad_gains = jnp.concatenate([grad_gain_one, grad_gain_two[0]])
    return result, input_rows, grad_attention, grad_widen, grad_narrow, grad_gains


def adam_update(master, first, second, gradient, factors, rate, decay):
    clip_factor, first_fix, second_fix = factors
    clipped = clip_factor * gradient
    first_new = BETA_FIRST * first + (1.0 - BETA_FIRST) * clipped
    second_new = BETA_SECOND * second + (1.0 - BETA_SECOND) * clipped * clipped
    master_new = master - rate * (
        first_new / first_fix / (jnp.sqrt(second_new / second_fix) + ADAM_EPS) + decay * master
    )
    return (master_new, first_new, second_new)


def swap_halves(parts):
    core = lax.axis_index("fsdp")
    got = lax.ppermute(parts[1 - core], "fsdp", [(0, 1), (1, 0)])
    return jnp.where(core == 0, jnp.stack([parts[0], got]), jnp.stack([got, parts[1]]))


def local(
    own_kernels,
    tokens,
    cotangent,
    images,
    attention_weight,
    attention_first,
    attention_second,
    widen_weight,
    widen_first,
    widen_second,
    narrow_weight,
    narrow_first,
    narrow_second,
    norm_gains,
    gains_first,
    gains_second,
):
    axes = ("dp", "fsdp")
    devices = lax.axis_size(axes)
    core = lax.axis_index("fsdp")
    position = lax.axis_index(axes)
    hidden_width = narrow_weight.shape[0] * devices
    gain_count = norm_gains.shape[0]
    attention_low = attention_weight.astype(BF16)
    widen_low = widen_weight.astype(BF16).T
    narrow_low = narrow_weight.astype(BF16)
    gains_low = norm_gains.astype(BF16)
    if own_kernels:
        gains_tile = jnp.zeros((16, 128), BF16).at[0, :gain_count].set(gains_low)
        (attention_full, widen_full, narrow_full, gains_full), tokens_row, cotangent_row = (
            gather_all((attention_low, widen_low, narrow_low, gains_tile), tokens, cotangent)
        )
        gains_full = gains_full.reshape(devices, 16, 128)[:, 0, :gain_count].reshape(-1)
    else:
        attention_full, widen_full, narrow_full, gains_full = (
            lax.all_gather(part, axes, axis=0, tiled=True)
            for part in (attention_low, widen_low, narrow_low, gains_low)
        )
        tokens_row, cotangent_row = swap_halves(tokens), swap_halves(cotangent)
    counts = lax.dynamic_index_in_dim(images[:, 0, :], core, 0, keepdims=False)
    result, input_rows, grad_attention, grad_widen, grad_narrow, grad_gains = layer(
        counts,
        tokens_row.reshape(ROW, WIDTH),
        cotangent_row.reshape(ROW, WIDTH),
        attention_full.reshape(4, WIDTH, WIDTH),
        widen_full.reshape(2, hidden_width, WIDTH),
        narrow_full.reshape(hidden_width, WIDTH),
        gains_full,
    )
    result = result.reshape(2, HALF, WIDTH)
    input_rows = input_rows.reshape(2, HALF, WIDTH)
    if own_kernels:
        grid = (4, 2, 2, 2)
        (
            narrow_sum,
            widen_sum,
            attention_sum,
            gains_total,
            square_total,
            block_output,
            input_grad,
        ) = reduce_all(
            (
                grad_narrow.reshape(grid + (-1, WIDTH)),
                grad_widen.reshape(grid + (-1, WIDTH)),
                grad_attention.reshape(grid + (-1, WIDTH)),
            ),
            grad_gains.reshape(16, 128),
            result,
            input_rows,
        )
        gains_sum = lax.dynamic_slice_in_dim(
            gains_total.reshape(-1), position * gain_count, gain_count
        )
        squares = square_total[0, 0]
    else:
        attention_sum, widen_sum, narrow_sum = (
            lax.psum_scatter(
                grad.astype(F32).reshape(-1, 128), axes, scatter_dimension=0, tiled=True
            ).reshape(-1, WIDTH)
            for grad in (grad_attention, grad_widen, grad_narrow)
        )
        gains_sum = lax.psum_scatter(grad_gains, axes, scatter_dimension=0, tiled=True)
        squares = lax.psum(
            sum(jnp.sum(g * g) for g in (attention_sum, widen_sum, narrow_sum, gains_sum)), axes
        )
        block_output, input_grad = swap_halves(result), swap_halves(input_rows)
    grad_norm = jnp.sqrt(squares)
    clip_factor = jnp.minimum(1.0, CLIP_LIMIT / (grad_norm + 1e-06))
    step_value = jnp.float32(STEP_VALUE)
    factors = (
        clip_factor,
        1.0 - jnp.power(jnp.float32(BETA_FIRST), step_value),
        1.0 - jnp.power(jnp.float32(BETA_SECOND), step_value),
    )
    return (
        block_output,
        input_grad,
        *adam_update(
            attention_weight,
            attention_first,
            attention_second,
            attention_sum,
            factors,
            MATRIX_RATE,
            DECAY,
        ),
        *adam_update(
            widen_weight, widen_first, widen_second, widen_sum.T, factors, MATRIX_RATE, DECAY
        ),
        *adam_update(
            narrow_weight, narrow_first, narrow_second, narrow_sum, factors, MATRIX_RATE, DECAY
        ),
        *adam_update(norm_gains, gains_first, gains_second, gains_sum, factors, GAIN_RATE, 0.0),
        grad_norm,
    )


def solution(mesh):
    both = ("dp", "fsdp")
    rows = P(None, both, None)
    tall = P(both, None)
    wide = P(None, both)
    flat = P(both)
    weights = (tall, tall, tall, wide, wide, wide, tall, tall, tall, flat, flat, flat)
    own_kernels = dict(mesh.shape) == {"dp": 16, "fsdp": 2}
    return jax.shard_map(
        functools.partial(local, own_kernels),
        mesh=mesh,
        in_specs=(rows, rows, P(None, "dp", None)) + weights,
        out_specs=(rows, rows) + weights + (P(),),
        check_vma=False,
    )
```

```python
import functools

import jax
import jax.numpy as jnp
from jax import lax
from jax.experimental import pallas as pl
from jax.experimental.pallas import tpu as pltpu
from jax.sharding import PartitionSpec as P

HD = 64
TEXT = 128
PATCH = 256
ROW = 1152
WIDTH = 1024
HALF = ROW // 2
QUERY_TILE = 576
BACK_TILE = 384
FF_BLOCK = 256

NORM_EPS = 1e-06
MASKED = -(2.0**30)
BETA_FIRST = 0.9
BETA_SECOND = 0.999
ADAM_EPS = 1e-08
MATRIX_RATE = 0.05
GAIN_RATE = 0.3
DECAY = 0.1
CLIP_LIMIT = 1.0
STEP_VALUE = 10.0
GELU_SCALE = 0.7978845608028654
GELU_CUBE = 0.044715

BF16 = jnp.bfloat16
F32 = jnp.float32
MESH = pl.DeviceIdType.MESH
ANY = pl.BlockSpec(memory_space=pl.ANY)
VMEM_WHOLE = pl.BlockSpec(memory_space=pltpu.VMEM)
DMA = pltpu.SemaphoreType.DMA
VMEM_LIMIT = 60 * 2**20

NT = (((1,), (1,)), ((), ()))
TN = (((0,), (0,)), ((), ()))


def dot(left, right, dims=(((1,), (0,)), ((), ()))):
    return lax.dot_general(left, right, dims, preferred_element_type=F32)


class Place:
    def __init__(self):
        self.dp = lax.axis_index("dp")
        self.core = lax.axis_index("fsdp")
        self.z = self.dp // 4
        self.y = lax.rem(self.dp // 2, 2)
        self.x = lax.rem(self.dp, 2)
        flip_y = 1 - self.y
        flip_x = 1 - self.x
        is_zero = self.core == 0
        self.own = (self.y, self.x)
        self.first = (jnp.where(is_zero, self.y, flip_y), jnp.where(is_zero, flip_x, self.x))
        self.second = (jnp.where(is_zero, flip_y, self.y), jnp.where(is_zero, self.x, flip_x))
        self.across = (flip_y, flip_x)

    def at(self, z, spot):
        return (z * 4 + spot[0] * 2 + spot[1], self.core)

    def above(self, step):
        return self.at(lax.rem(self.z + step, 4), self.own)

    def to_first(self):
        return self.at(self.z, self.first)

    def to_second(self):
        return self.at(self.z, self.second)

    def sibling(self):
        return (self.dp, 1 - self.core)

    def greet(self):
        barrier = pltpu.get_barrier_semaphore()
        peers = [self.above(1), self.above(2), self.above(3)]
        peers += [self.to_first(), self.to_second(), self.sibling()]
        for peer in peers:
            pl.semaphore_signal(barrier, inc=1, device_id=peer, device_id_type=MESH)
        pl.semaphore_wait(barrier, len(peers))


def remote(source, target, send_sem, recv_sem, device):
    return pltpu.make_async_remote_copy(
        src_ref=source,
        dst_ref=target,
        send_sem=send_sem,
        recv_sem=recv_sem,
        device_id=device,
        device_id_type=MESH,
    )


def cut(index, rows, most):
    pieces = -(-rows // most)
    step = -(-rows // (pieces * 16)) * 16
    return [(index, at, min(step, rows - at)) for at in range(0, rows, step)]


class Gather:
    def __init__(self, shards, swaps=(), most=48):
        self.arrays = [*shards, *swaps]
        self.shards, self.swaps = len(shards), len(swaps)
        self.chunks = []
        for index, shard in enumerate(shards):
            self.chunks += cut(index, shard.shape[0], most)
        count = len(self.chunks)
        self.ticks = count + 3
        self.in_specs = [VMEM_WHOLE] * len(self.arrays)
        self.out_shapes = [jax.ShapeDtypeStruct((4, 2, 2, 2) + a.shape, a.dtype) for a in shards]
        self.out_shapes += [jax.ShapeDtypeStruct(a.shape, a.dtype) for a in swaps]
        self.out_specs = [ANY] * len(self.arrays)
        self.scratch = [
            DMA((count,)),
            DMA((count, 3)),
            DMA((count, 3)),
            DMA((count, 3)),
            DMA((count, 3)),
            DMA((count, 4)),
            DMA((count, 4)),
            DMA((max(self.swaps, 1),)),
            DMA((max(self.swaps, 1),)),
            DMA((max(self.swaps, 1),)),
        ]

    def bind(self, ins, outs, scratch):
        self.ins, self.outs = ins, outs
        (
            self.own_sem,
            self.z_send,
            self.z_recv,
            self.p_send,
            self.p_recv,
            self.c_send,
            self.c_recv,
            self.s_own,
            self.s_send,
            self.s_recv,
        ) = scratch
        self.here = Place()
        self.columns = (self.here.own, self.here.first, self.here.second, self.here.across)

    def spot(self, k, where):
        array, start, rows = self.chunks[k]
        return self.outs[array].at[:, where[0], where[1], self.here.core, pl.ds(start, rows), :]

    def mine(self, k):
        array, start, rows = self.chunks[k]
        here = self.here
        return (
            self.ins[array].at[pl.ds(start, rows), :],
            self.outs[array].at[here.z, here.y, here.x, here.core, pl.ds(start, rows), :],
        )

    def keep(self, k):
        source, target = self.mine(k)
        return pltpu.make_async_copy(source, target, self.own_sem.at[k])

    def along_z(self, k, step):
        source, target = self.mine(k)
        return remote(
            source,
            target,
            self.z_send.at[k, step - 1],
            self.z_recv.at[k, step - 1],
            self.here.above(step),
        )

    def plane(self, k, index):
        where = self.here.first if index == 2 else self.here.own
        device = self.here.to_first() if index == 0 else self.here.to_second()
        return remote(
            self.spot(k, where),
            self.spot(k, where),
            self.p_send.at[k, index],
            self.p_recv.at[k, index],
            device,
        )

    def to_sibling(self, k, index):
        where = self.columns[index]
        return remote(
            self.spot(k, where),
            self.spot(k, where),
            self.c_send.at[k, index],
            self.c_recv.at[k, index],
            self.here.sibling(),
        )

    def swap(self, index):
        source = self.ins[self.shards + index]
        target = self.outs[self.shards + index]
        core = self.here.core
        return (
            pltpu.make_async_copy(source.at[core], target.at[core], self.s_own.at[index]),
            remote(
                source.at[1 - core],
                target.at[core],
                self.s_send.at[index],
                self.s_recv.at[index],
                self.here.sibling(),
            ),
        )

    def tick(self, tick):
        count = len(self.chunks)
        if tick < count:
            self.keep(tick).start()
            for step in (2, 1, 3):
                self.along_z(tick, step).start()
        if tick == 0:
            for index in range(self.swaps):
                for copy in self.swap(index):
                    copy.start()
        k = tick - 1
        if 0 <= k < count:
            self.keep(k).wait()
            for step in (1, 2, 3):
                self.along_z(k, step).wait_recv()
            self.plane(k, 1).start()
            self.plane(k, 0).start()
            self.to_sibling(k, 0).start()
        k = tick - 2
        if 0 <= k < count:
            self.plane(k, 0).wait_recv()
            self.plane(k, 2).start()
            self.to_sibling(k, 1).start()
            self.plane(k, 1).wait_recv()
            self.to_sibling(k, 2).start()
        k = tick - 3
        if 0 <= k < count:
            self.plane(k, 2).wait_recv()
            self.to_sibling(k, 3).start()

    def finish(self):
        for k in range(len(self.chunks)):
            for step in (1, 2, 3):
                self.along_z(k, step).wait_send()
            for index in range(3):
                self.plane(k, index).wait_send()
            for index in range(4):
                self.to_sibling(k, index).wait()
        for index in range(self.swaps):
            for copy in self.swap(index):
                copy.wait()


class Reduce:
    def __init__(self, gradients, swaps=(), most=48):
        self.arrays = [*gradients, *swaps]
        self.gradients, self.swaps = len(gradients), len(swaps)
        self.chunks = []
        for index, gradient in enumerate(gradients):
            self.chunks += cut(index, gradient.shape[4], most)
        count = len(self.chunks)
        self.ticks = count + 4
        shapes = [g.shape[4:] for g in gradients]
        padded = [(-(-s[0] // 16) * 16, s[1]) for s in shapes]
        self.in_specs = [ANY] * len(self.arrays)
        self.out_shapes = [jax.ShapeDtypeStruct(s, F32) for s in shapes]
        self.out_shapes += [jax.ShapeDtypeStruct(a.shape[1:], a.dtype) for a in swaps]
        self.out_specs = [VMEM_WHOLE] * len(gradients) + [ANY] * len(swaps)
        self.scratch = []
        for lead in ((4, 2, 2), (4, 2, 2), (2, 4), (4,), (3,)):
            self.scratch += [pltpu.VMEM(lead + s, BF16) for s in padded]
        self.scratch += [
            DMA((count,)),
            DMA((count,)),
            DMA((count,)),
            DMA((count, 3)),
            DMA((count, 3)),
            DMA((count, 3)),
            DMA((count, 3)),
            DMA((max(self.swaps, 1),)),
            DMA((max(self.swaps, 1),)),
        ]

    def bind(self, ins, outs, scratch):
        n = self.gradients
        self.ins, self.outs = ins, outs
        self.own, self.from_core, self.from_second, self.from_first, self.from_z = (
            scratch[i * n : (i + 1) * n] for i in range(5)
        )
        (
            self.own_sem,
            self.c_send,
            self.c_recv,
            self.p_send,
            self.p_recv,
            self.z_send,
            self.z_recv,
            self.s_send,
            self.s_recv,
        ) = scratch[5 * n :]
        self.here = Place()

    def part(self, k):
        array, start, rows = self.chunks[k]
        return array, pl.ds(start, rows)

    def load(self, k):
        array, rows = self.part(k)
        return pltpu.make_async_copy(
            self.ins[array].at[:, :, :, self.here.core, rows, :],
            self.own[array].at[:, :, :, rows, :],
            self.own_sem.at[k],
        )

    def swap_core(self, k):
        array, rows = self.part(k)
        return remote(
            self.ins[array].at[:, :, :, 1 - self.here.core, rows, :],
            self.from_core[array].at[:, :, :, rows, :],
            self.c_send.at[k],
            self.c_recv.at[k],
            self.here.sibling(),
        )

    def send_second(self, k, index):
        array, rows = self.part(k)
        where = self.here.second if index == 0 else self.here.across
        return remote(
            self.own[array].at[:, where[0], where[1], rows, :],
            self.from_second[array].at[index, :, rows, :],
            self.p_send.at[k, index],
            self.p_recv.at[k, index],
            self.here.to_second(),
        )

    def send_first(self, k):
        array, rows = self.part(k)
        where = self.here.first
        return remote(
            self.own[array].at[:, where[0], where[1], rows, :],
            self.from_first[array].at[:, rows, :],
            self.p_send.at[k, 2],
            self.p_recv.at[k, 2],
            self.here.to_first(),
        )

    def send_z(self, k, step):
        array, rows = self.part(k)
        here = self.here
        return remote(
            self.own[array].at[lax.rem(here.z + step, 4), here.y, here.x, rows, :],
            self.from_z[array].at[step - 1, rows, :],
            self.z_send.at[k, step - 1],
            self.z_recv.at[k, step - 1],
            here.above(step),
        )

    def swap(self, index):
        source = self.ins[self.gradients + index]
        return remote(
            source.at[1 - self.here.core],
            self.outs[self.gradients + index],
            self.s_send.at[index],
            self.s_recv.at[index],
            self.here.sibling(),
        )

    def add_all(self, k):
        array, rows = self.part(k)
        own, other = self.own[array], self.from_core[array]

        def body(i, carry):
            z, y, x = i // 4, lax.rem(i // 2, 2), lax.rem(i, 2)
            own[z, y, x, rows, :] = both_sum(own[z, y, x, rows, :], other[z, y, x, rows, :])
            return carry

        lax.fori_loop(0, 16, body, 0)

    def add_column(self, k, where, other):
        array, rows = self.part(k)
        own = self.own[array]

        def body(z, carry):
            own[z, where[0], where[1], rows, :] = both_sum(
                own[z, where[0], where[1], rows, :], other[z, rows, :]
            )
            return carry

        lax.fori_loop(0, 4, body, 0)

    def total(self, k):
        array, rows = self.part(k)
        here = self.here
        total = self.own[array][here.z, here.y, here.x, rows, :].astype(F32)
        for step in range(3):
            total = total + self.from_z[array][step, rows, :].astype(F32)
        self.outs[array][rows, :] = total

    def tick(self, tick):
        count = len(self.chunks)
        if tick < count:
            self.swap_core(tick).start()
            self.load(tick).start()
        if tick == 1:
            for index in range(self.swaps):
                self.swap(index).start()
        k = tick - 1
        if 0 <= k < count:
            self.load(k).wait()
            self.swap_core(k).wait_recv()
            self.add_all(k)
            for index in (1, 0):
                self.send_second(k, index).start()
        k = tick - 2
        if 0 <= k < count:
            array = self.chunks[k][0]
            self.send_second(k, 1).wait_recv()
            self.add_column(k, self.here.first, self.from_second[array].at[1])
            self.send_first(k).start()
            self.send_second(k, 0).wait_recv()
            self.add_column(k, self.here.own, self.from_second[array].at[0])
        k = tick - 3
        if 0 <= k < count:
            array = self.chunks[k][0]
            self.send_first(k).wait_recv()
            self.add_column(k, self.here.own, self.from_first[array])
            for step in (2, 1, 3):
                self.send_z(k, step).start()
        k = tick - 4
        if 0 <= k < count:
            for step in (1, 2, 3):
                self.send_z(k, step).wait_recv()
            self.total(k)

    def finish(self):
        for k in range(len(self.chunks)):
            self.swap_core(k).wait_send()
            for index in (1, 0):
                self.send_second(k, index).wait_send()
            self.send_first(k).wait_send()
            for step in (1, 2, 3):
                self.send_z(k, step).wait_send()
        for index in range(self.swaps):
            self.swap(index).wait()


def both_sum(mine, other):
    return (mine.astype(F32) + other.astype(F32)).astype(BF16)


def everywhere(here, buffer, value, send, recv):
    for index, device in enumerate((here.sibling(), here.to_first(), here.to_second())):
        buffer[2 * index] = value
        copy = remote(
            buffer.at[2 * index], buffer.at[2 * index + 1], send.at[index], recv.at[index], device
        )
        copy.start()
        yield
        copy.wait()
        value = buffer[2 * index] + buffer[2 * index + 1]
    buffer[6 + here.z] = value
    copies = [
        remote(
            buffer.at[6 + here.z],
            buffer.at[6 + here.z],
            send.at[2 + step],
            recv.at[2 + step],
            here.above(step),
        )
        for step in (1, 2, 3)
    ]
    for copy in copies:
        copy.start()
    yield
    for copy in copies:
        copy.wait()
    yield (buffer[6] + buffer[7]) + (buffer[8] + buffer[9])


def call(name, body, grid, inner, ins, in_specs, out_shapes, out_specs, scratch=(), comm=None, key=0):
    params = {"vmem_limit_bytes": VMEM_LIMIT}
    if comm is None:

        def kernel(*refs):
            body(lambda point: None, *refs)

        extra = ([], [], [], [], [])
    else:
        params.update(collective_id=key, has_side_effects=True)
        extra = (comm.arrays, comm.in_specs, comm.out_shapes, comm.out_specs, comm.scratch)
        sizes = (len(ins), len(extra[0]), len(out_shapes), len(extra[2]), len(scratch), len(extra[4]))

        def kernel(*refs):
            parts, at = [], 0
            for size in sizes:
                parts.append(refs[at : at + size])
                at += size
            comm.bind(parts[1], parts[3], parts[5])
            step = pl.program_id(0)

            def pump(point):
                for tick in range(comm.ticks):
                    slot = tick * grid * inner // comm.ticks
                    if slot % inner == point:

                        @pl.when(step == slot // inner)
                        def _(tick=tick):
                            if tick == 0:
                                comm.here.greet()
                            comm.tick(tick)

            body(pump, *parts[0], *parts[2], *parts[4])

            @pl.when(step == grid - 1)
            def _():
                comm.finish()

    results = pl.pallas_call(
        kernel,
        grid=(grid,),
        out_shape=[*out_shapes, *extra[2]],
        in_specs=[*in_specs, *extra[1]],
        out_specs=[*out_specs, *extra[3]],
        scratch_shapes=[*scratch, *extra[4]],
        compiler_params=pltpu.CompilerParams(**params),
        name=name,
    )(*ins, *extra[0])
    return results[: len(out_shapes)], results[len(out_shapes) :]


def gather_now(comm, key):
    def kernel(*refs):
        sizes = (len(comm.arrays), len(comm.out_shapes))
        comm.bind(refs[: sizes[0]], refs[sizes[0] : sum(sizes)], refs[sum(sizes) :])
        comm.here.greet()
        for tick in range(comm.ticks):
            comm.tick(tick)
        comm.finish()

    return pl.pallas_call(
        kernel,
        out_shape=comm.out_shapes,
        in_specs=comm.in_specs,
        out_specs=comm.out_specs,
        scratch_shapes=comm.scratch,
        compiler_params=pltpu.CompilerParams(
            collective_id=key, has_side_effects=True, vmem_limit_bytes=VMEM_LIMIT
        ),
        name="gather_first",
    )(*comm.arrays)


def reduce_last(comm, gains, sums, key):
    def kernel(*refs):
        outs = len(comm.out_shapes)
        ins = refs[: len(comm.arrays)]
        gains_ref = refs[len(ins)]
        sums_refs = refs[len(ins) + 1 : len(ins) + 1 + len(sums)]
        at = len(ins) + 1 + len(sums)
        comm_outs, gains_out, square_out = refs[at : at + outs], refs[at + outs], refs[at + outs + 1]
        small, tiny, g_send, g_recv, n_send, n_recv = refs[at + outs + 2 : at + outs + 8]
        comm.bind(ins, comm_outs, refs[at + outs + 8 :])
        here = comm.here
        here.greet()
        gains_steps = everywhere(here, small, gains_ref[...], g_send, g_recv)
        for tick in range(comm.ticks):
            comm.tick(tick)
            if tick < 5:
                gains_total = next(gains_steps)
        gains_out[...] = gains_total
        squares = jnp.zeros((8, 128), F32)
        for ref in (*sums_refs, *comm_outs[: comm.gradients]):
            values = ref[...]
            squares = squares + jnp.sum((values * values).reshape(-1, 8, 128), axis=0)
        for total in everywhere(here, tiny, squares, n_send, n_recv):
            pass
        square_out[...] = jnp.broadcast_to(
            jnp.sum(total) + jnp.sum(gains_total * gains_total), (8, 128)
        )
        comm.finish()

    return pl.pallas_call(
        kernel,
        out_shape=[
            *comm.out_shapes,
            jax.ShapeDtypeStruct((16, 128), F32),
            jax.ShapeDtypeStruct((8, 128), F32),
        ],
        in_specs=[*comm.in_specs, VMEM_WHOLE, *([VMEM_WHOLE] * len(sums))],
        out_specs=[*comm.out_specs, VMEM_WHOLE, VMEM_WHOLE],
        scratch_shapes=[
            pltpu.VMEM((10, 16, 128), F32),
            pltpu.VMEM((10, 8, 128), F32),
            DMA((6,)),
            DMA((6,)),
            DMA((6,)),
            DMA((6,)),
            *comm.scratch,
        ],
        compiler_params=pltpu.CompilerParams(
            collective_id=key, has_side_effects=True, vmem_limit_bytes=VMEM_LIMIT
        ),
        name="reduce_last",
    )(*comm.arrays, gains, *sums)


def segment_lanes(counts):
    sizes = [jnp.where(counts[i] > 0, TEXT + PATCH * counts[i], 0) for i in range(3)]
    ends = (sizes[0], sizes[0] + sizes[1], sizes[0] + sizes[1] + sizes[2])
    places = jnp.arange(ROW, dtype=jnp.int32)[:, None]
    segment = sum((places >= end).astype(jnp.int32) for end in ends)
    lane = jnp.arange(2 * HD, dtype=jnp.int32)[None, :] % HD
    same = lane == segment
    queries = jnp.where((lane < 4) & ~same, MASKED, 0.0).astype(BF16)
    return queries, jnp.where(same, 1.0, 0.0).astype(BF16)


def lanes_of_heads():
    lane = lax.broadcasted_iota(jnp.int32, (1, 2 * HD), 1)
    return lane, (lane < HD, lane >= HD)


def attend_body(pump, q_ref, k_ref, v_ref, mq_ref, mk_ref, o_ref, log_ref):
    pair = pl.program_id(0)
    lane, in_head = lanes_of_heads()

    @pl.when(pair == 0)
    def _():
        log_ref[...] = jnp.zeros_like(log_ref)

    key = jnp.concatenate([k_ref[0], mk_ref[...]], axis=1)
    value = v_ref[0]
    values = [jnp.where(mine, value, jnp.ones_like(value)) for mine in in_head]
    for index in range(ROW // QUERY_TILE):
        pump(index)
        rows = pl.ds(index * QUERY_TILE, QUERY_TILE)
        query, extra = q_ref[0, rows, :], mq_ref[rows, :]
        mixed = []
        logs = log_ref[rows, :]
        for head in range(2):
            masked = jnp.where(in_head[head], query, jnp.zeros_like(query))
            scores = dot(jnp.concatenate([masked, extra], axis=1), key, NT)
            top = jnp.max(scores, axis=-1, keepdims=True)
            weight = jnp.exp(scores - top).astype(BF16)
            both = dot(weight, values[head])
            other = pltpu.roll(both, HD, 1)
            mixed.append(both / other)
            total = jnp.where(in_head[head], other, both)
            logs = jnp.where(lane == 2 * pair + head, top + jnp.log(total), logs)
        log_ref[rows, :] = logs
        o_ref[rows, :] = jnp.where(in_head[0], mixed[0], mixed[1]).astype(BF16)


PAIRS = WIDTH // (2 * HD)


def third(which):
    return pl.BlockSpec((1, ROW, 2 * HD), lambda p: (which, 0, p))


def attend(projected, extras, comm=None, key=0):
    whole = pl.BlockSpec((ROW, 128), lambda p: (0, 0))
    return call(
        "attend",
        attend_body,
        PAIRS,
        ROW // QUERY_TILE,
        [projected, projected, projected, *extras],
        [third(0), third(1), third(2), whole, whole],
        [jax.ShapeDtypeStruct((ROW, WIDTH), BF16), jax.ShapeDtypeStruct((ROW, 128), F32)],
        [pl.BlockSpec((ROW, 2 * HD), lambda p: (0, p)), whole],
        comm=comm,
        key=key,
    )


def attend_back_body(
    pump, q_ref, k_ref, v_ref, mq_ref, mk_ref, o_ref, do_ref, log_ref, out_ref, dk, dv
):
    pair = pl.program_id(0)
    _, in_head = lanes_of_heads()
    pick = jnp.where(
        (lax.broadcasted_iota(jnp.int32, (8, 2 * HD), 1) < HD)
        == (lax.broadcasted_iota(jnp.int32, (8, 2 * HD), 0) == 0),
        jnp.ones((8, 2 * HD), F32),
        jnp.zeros((8, 2 * HD), F32),
    )

    def only(values, head):
        return jnp.where(in_head[head], values, jnp.zeros_like(values))

    dk[...] = jnp.zeros_like(dk)
    dv[...] = jnp.zeros_like(dv)
    for index in range(ROW // BACK_TILE):
        pump(index)
        rows = pl.ds(index * BACK_TILE, BACK_TILE)
        query, grad, extra = q_ref[0, rows, :], do_ref[rows, :], mq_ref[rows, :]
        key, value = k_ref[0], v_ref[0]
        inner = lax.dot_general(
            pick,
            grad.astype(F32) * o_ref[rows, :].astype(F32),
            NT,
            precision=lax.Precision.HIGHEST,
            preferred_element_type=F32,
        )
        dq = None
        for head in range(2):
            log_total = log_ref[
                pl.ds(2 * pair + head, 1), index * BACK_TILE : (index + 1) * BACK_TILE
            ]
            scores = dot(
                jnp.where(in_head[head], key, mk_ref[...]),
                jnp.where(in_head[head], query, extra),
                NT,
            )
            weight = jnp.exp(scores - log_total)
            down = dot(only(value, head), grad, NT)
            slope = (weight * (down - inner[head : head + 1, :])).astype(BF16)
            dv[...] += dot(weight.astype(BF16), only(grad, head))
            dk[...] += dot(slope, only(query, head))
            step = dot(slope, only(key, head), TN)
            dq = step if dq is None else dq + step
        out_ref[0, rows, :] = dq.astype(BF16)
    out_ref[1] = dk[...].astype(BF16)
    out_ref[2] = dv[...].astype(BF16)


def attend_back(projected, extras, mixed, grad_mixed, log_rows, comm=None, key=0):
    whole = pl.BlockSpec((ROW, 128), lambda p: (0, 0))
    column = pl.BlockSpec((ROW, 2 * HD), lambda p: (0, p))
    return call(
        "attend_back",
        attend_back_body,
        PAIRS,
        ROW // BACK_TILE,
        [projected, projected, projected, *extras, mixed, grad_mixed, log_rows],
        [third(0), third(1), third(2), whole, whole, column, column]
        + [pl.BlockSpec((2 * PAIRS, ROW), lambda p: (0, 0))],
        [jax.ShapeDtypeStruct((3, ROW, WIDTH), BF16)],
        [pl.BlockSpec((3, ROW, 2 * HD), lambda p: (0, 0, p))],
        [pltpu.VMEM((ROW, 2 * HD), F32), pltpu.VMEM((ROW, 2 * HD), F32)],
        comm=comm,
        key=key,
    )


def feed_units(pump, n2_ref, cot_ref, widen_ref, narrow_ref, widen_grad_ref, narrow_grad_ref):
    pump(0)
    n2, cot = n2_ref[...], cot_ref[...]
    wide_gate, wide_up, narrow = widen_ref[0], widen_ref[1], narrow_ref[...]
    gate = dot(n2, wide_gate, NT)
    up = dot(n2, wide_up, NT)
    down = dot(cot, narrow, NT)
    square = gate * gate
    bend = jnp.tanh(GELU_SCALE * gate * (1.0 + GELU_CUBE * square))
    half = 0.5 * (1.0 + bend)
    curve = gate * half
    slope = half + 0.5 * gate * (1.0 - bend * bend) * (
        GELU_SCALE * (1.0 + 3.0 * GELU_CUBE * square)
    )
    hidden = (curve * up).astype(BF16)
    grad_gate = (down * up * slope).astype(BF16)
    grad_up = (down * curve).astype(BF16)
    pump(1)
    narrow_grad_ref[...] = dot(hidden, cot, TN).astype(BF16)
    widen_grad_ref[0] = dot(grad_gate, n2, TN).astype(BF16)
    widen_grad_ref[1] = dot(grad_up, n2, TN).astype(BF16)
    return lambda: dot(hidden, narrow), lambda: dot(grad_gate, wide_gate) + dot(grad_up, wide_up)


def feed_start_body(
    pump, n2_ref, cot_ref, widen_ref, narrow_ref, result_ref, back_ref, widen_grad_ref, narrow_grad_ref
):
    result, back = feed_units(
        pump, n2_ref, cot_ref, widen_ref, narrow_ref, widen_grad_ref, narrow_grad_ref
    )

    @pl.when(pl.program_id(0) == 0)
    def _():
        result_ref[...] = jnp.zeros_like(result_ref)
        back_ref[...] = jnp.zeros_like(back_ref)

    result_ref[...] += result()
    back_ref[...] += back()


def feed_end_body(
    pump, n2_ref, cot_ref, h1_ref, gain_ref, result_part, back_part, widen_ref, narrow_ref,
    result_ref, dh1_ref, e_ref, gain_grad_ref, widen_grad_ref, narrow_grad_ref,
    back_ref, part_sem,
):
    step = pl.program_id(0)
    parts = (
        pltpu.make_async_copy(result_part, result_ref, part_sem.at[0]),
        pltpu.make_async_copy(back_part, back_ref, part_sem.at[1]),
    )

    @pl.when(step == 0)
    def _():
        for part in parts:
            part.start()

    result, back = feed_units(
        pump, n2_ref, cot_ref, widen_ref, narrow_ref, widen_grad_ref, narrow_grad_ref
    )

    @pl.when(step == 0)
    def _():
        for part in parts:
            part.wait()

    result_ref[...] += result()
    back_ref[...] += back()

    @pl.when(step == pl.num_programs(0) - 1)
    def _():
        gain = gain_ref[...]

        def tile(i, total):
            rows = pl.ds(pl.multiple_of(i * 64, 64), 64)
            h1 = h1_ref[rows, :]
            grad = back_ref[rows, :]
            result_ref[rows, :] += h1
            scale = lax.rsqrt(jnp.mean(h1 * h1, axis=-1, keepdims=True) + NORM_EPS)
            lifted = gain * grad
            inner = jnp.mean(h1 * lifted, axis=-1, keepdims=True)
            dh1 = (
                cot_ref[rows, :].astype(F32)
                + scale * lifted
                - h1 * (scale * scale * scale * inner)
            )
            dh1_ref[rows, :] = dh1
            e_ref[rows, :] = dh1.astype(BF16)
            return total + jnp.sum((grad * h1 * scale).reshape(8, 8, WIDTH), axis=0)

        total = lax.fori_loop(0, ROW // 64, tile, jnp.zeros((8, WIDTH), F32))
        gain_grad_ref[...] = jnp.sum(total, axis=0, keepdims=True)


def whole_block(*shape):
    return pl.BlockSpec(shape, lambda j: (0,) * len(shape), pipeline_mode=pl.Buffered(1))


WIDE_BLOCK = pl.BlockSpec((2, FF_BLOCK, WIDTH), lambda j: (0, j, 0))
TALL_BLOCK = pl.BlockSpec((FF_BLOCK, WIDTH), lambda j: (j, 0))
ROW_F32 = jax.ShapeDtypeStruct((ROW, WIDTH), F32)
ROW_BF16 = jax.ShapeDtypeStruct((ROW, WIDTH), BF16)


def feed_start(n2, cot, widen, narrow, comm=None, key=0):
    rows = whole_block(ROW, WIDTH)
    return call(
        "feed_start",
        feed_start_body,
        narrow.shape[0] // FF_BLOCK,
        2,
        [n2, cot, widen, narrow],
        [rows, rows, WIDE_BLOCK, TALL_BLOCK],
        [
            ROW_F32,
            ROW_F32,
            jax.ShapeDtypeStruct(widen.shape, BF16),
            jax.ShapeDtypeStruct(narrow.shape, BF16),
        ],
        [rows, rows, WIDE_BLOCK, TALL_BLOCK],
        comm=comm,
        key=key,
    )


def feed_end(n2, cot, h1, gain, result_part, back_part, widen, narrow, comm=None, key=0):
    rows = whole_block(ROW, WIDTH)
    line = whole_block(1, WIDTH)
    return call(
        "feed_end",
        feed_end_body,
        narrow.shape[0] // FF_BLOCK,
        2,
        [n2, cot, h1, gain, result_part, back_part, widen, narrow],
        [rows, rows, rows, line, ANY, ANY, WIDE_BLOCK, TALL_BLOCK],
        [
            ROW_F32,
            ROW_F32,
            ROW_BF16,
            jax.ShapeDtypeStruct((1, WIDTH), F32),
            jax.ShapeDtypeStruct(widen.shape, BF16),
            jax.ShapeDtypeStruct(narrow.shape, BF16),
        ],
        [rows, rows, rows, line, WIDE_BLOCK, TALL_BLOCK],
        [pltpu.VMEM((ROW, WIDTH), F32), DMA((2,))],
        comm=comm,
        key=key,
    )


def rms_scale(values, gain_vector):
    return (
        values
        * lax.rsqrt(jnp.mean(values * values, axis=-1, keepdims=True) + NORM_EPS)
        * gain_vector
    )


def adam_update(master, first, second, gradient, factors, rate, decay):
    clip_factor, first_fix, second_fix = factors
    clipped = clip_factor * gradient
    first_new = BETA_FIRST * first + (1.0 - BETA_FIRST) * clipped
    second_new = BETA_SECOND * second + (1.0 - BETA_SECOND) * clipped * clipped
    master_new = master - rate * (
        first_new / first_fix / (jnp.sqrt(second_new / second_fix) + ADAM_EPS) + decay * master
    )
    return (master_new, first_new, second_new)


def swap_halves(parts):
    core = lax.axis_index("fsdp")
    got = lax.ppermute(parts[1 - core], "fsdp", [(0, 1), (1, 0)])
    return jnp.where(core == 0, jnp.stack([parts[0], got]), jnp.stack([got, parts[1]]))


def with_half(rows, got):
    own = rows.reshape(2, HALF, WIDTH)
    first = lax.axis_index("fsdp") == 0
    return jnp.where(first, jnp.stack([own[0], got]), jnp.stack([got, own[1]]))


def local(
    own_kernels,
    tokens,
    cotangent,
    images,
    attention_weight,
    attention_first,
    attention_second,
    widen_weight,
    widen_first,
    widen_second,
    narrow_weight,
    narrow_first,
    narrow_second,
    norm_gains,
    gains_first,
    gains_second,
):
    axes = ("dp", "fsdp")
    devices = lax.axis_size(axes)
    core = lax.axis_index("fsdp")
    position = lax.axis_index(axes)
    gain_count = norm_gains.shape[0]
    units = narrow_weight.shape[0]
    split = units * 6 // 11
    attention_low = attention_weight.astype(BF16)
    widen_low = widen_weight.astype(BF16).T.reshape(2, units, WIDTH)
    narrow_low = narrow_weight.astype(BF16)
    gains_low = norm_gains.astype(BF16)
    feed_low = [
        (widen_low[:, :split].reshape(-1, WIDTH), narrow_low[:split]),
        (widen_low[:, split:].reshape(-1, WIDTH), narrow_low[split:]),
    ]
    grid = (4, 2, 2, 2)

    def fetch(shards):
        return [lax.all_gather(shard, axes, axis=0, tiled=True) for shard in shards]

    def summed(gradients):
        return [
            lax.psum_scatter(
                g.astype(F32).reshape(-1, 128), axes, scatter_dimension=0, tiled=True
            ).reshape(-1, WIDTH)
            for g in gradients
        ]

    def other_half(parts):
        return lax.ppermute(
            lax.dynamic_index_in_dim(parts, 1 - core, 0, keepdims=False), "fsdp", [(0, 1), (1, 0)]
        )

    def as_feed(shards):
        return shards[0].reshape(2, -1, WIDTH), shards[1].reshape(-1, WIDTH)

    def as_shards(*gradients):
        return [g.reshape(grid + (-1, WIDTH)) for g in gradients]

    gather_a = gather_b = None
    if own_kernels:
        gains_tile = jnp.zeros((16, 128), BF16).at[0, :gain_count].set(gains_low)
        attention_full, gains_full, tokens_row, cotangent_row = gather_now(
            Gather((attention_low, gains_tile), (tokens, cotangent)), 0
        )
        gains_full = gains_full.reshape(devices, 16, 128)[:, 0, :gain_count].reshape(-1)
        gather_a, gather_b = Gather(feed_low[0]), Gather(feed_low[1])
    else:
        attention_full, gains_full = fetch((attention_low, gains_low))
        first = core == 0
        tokens_row, cotangent_row = (
            jnp.where(first, jnp.stack([a[0], got]), jnp.stack([got, a[1]]))
            for a, got in ((a, other_half(a)) for a in (tokens, cotangent))
        )
    counts = lax.dynamic_index_in_dim(images[:, 0, :], core, 0, keepdims=False)
    attention = attention_full.reshape(4, WIDTH, WIDTH)
    cot = cotangent_row.reshape(ROW, WIDTH)
    inputs = tokens_row.reshape(ROW, WIDTH).astype(F32)
    first_gain = gains_full[:WIDTH].astype(F32)
    second_gain = gains_full[WIDTH:].astype(F32)

    normed = rms_scale(inputs, first_gain).astype(BF16)
    projected = jnp.einsum(
        "sd,jde->jse", normed, attention[:3], preferred_element_type=F32
    ).astype(BF16)
    extras = segment_lanes(counts)
    (mixed, log_columns), feed_a = attend(projected, extras, gather_a, 1)
    log_rows = log_columns[:, : WIDTH // HD].T
    h1 = inputs + dot(mixed, attention[3])
    n2 = rms_scale(h1, second_gain).astype(BF16)
    widen_a, narrow_a = as_feed(feed_a if own_kernels else fetch(feed_low[0]))
    (result_part, back_part, *grads_a), feed_b = feed_start(
        n2, cot, widen_a, narrow_a, gather_b, 2
    )
    widen_b, narrow_b = as_feed(feed_b if own_kernels else fetch(feed_low[1]))
    (result, dh1, e, grad_gain_two, *grads_b), sums_a = feed_end(
        n2,
        cot,
        h1,
        second_gain[None],
        result_part,
        back_part,
        widen_b,
        narrow_b,
        Reduce(as_shards(*grads_a)) if own_kernels else None,
        3,
    )
    grad_out = dot(mixed, e, TN).astype(BF16)
    grad_mixed = dot(e, attention[3], NT).astype(BF16)
    (grad_projected,), sums_b = attend_back(
        projected,
        extras,
        mixed,
        grad_mixed,
        log_rows,
        Reduce(as_shards(*grads_b), (result.reshape(2, HALF, WIDTH),)) if own_kernels else None,
        4,
    )
    grad_qkv = jnp.einsum(
        "sd,jse->jde", normed, grad_projected, preferred_element_type=F32
    ).astype(BF16)
    grad_normed = jnp.einsum(
        "jse,jde->sd", grad_projected, attention[:3], preferred_element_type=F32
    )
    scale = lax.rsqrt(jnp.mean(inputs * inputs, axis=-1, keepdims=True) + NORM_EPS)
    lifted = first_gain * grad_normed
    inner = jnp.mean(inputs * lifted, axis=-1, keepdims=True)
    input_rows = dh1 + scale * lifted - inputs * (scale * scale * scale * inner)
    grad_gain_one = jnp.sum(grad_normed * inputs * scale, axis=0)
    grad_attention = jnp.concatenate([grad_qkv, grad_out[None]], axis=0)
    grad_gains = jnp.concatenate([grad_gain_one, grad_gain_two[0]])

    if own_kernels:
        *sums_b, got_result = sums_b
        attention_sum, got_input, gains_total, square_total = reduce_last(
            Reduce(as_shards(grad_attention), (input_rows.reshape(2, HALF, WIDTH),)),
            grad_gains.reshape(16, 128),
            [*sums_a, *sums_b],
            5,
        )
        gains_sum = lax.dynamic_slice_in_dim(
            gains_total.reshape(-1), position * gain_count, gain_count
        )
        squares = square_total[0, 0]
    else:
        sums_a, sums_b, (attention_sum,) = summed(grads_a), summed(grads_b), summed([grad_attention])
        gains_sum = lax.psum_scatter(grad_gains, axes, scatter_dimension=0, tiled=True)
        squares = lax.psum(
            sum(jnp.sum(g * g) for g in (*sums_a, *sums_b, attention_sum, gains_sum)), axes
        )
        got_result = other_half(result.reshape(2, HALF, WIDTH))
        got_input = other_half(input_rows.reshape(2, HALF, WIDTH))
    widen_sum = jnp.concatenate(
        [sums_a[0].reshape(2, -1, WIDTH), sums_b[0].reshape(2, -1, WIDTH)], axis=1
    ).reshape(-1, WIDTH)
    narrow_sum = jnp.concatenate([sums_a[1], sums_b[1]], axis=0)
    grad_norm = jnp.sqrt(squares)
    clip_factor = jnp.minimum(1.0, CLIP_LIMIT / (grad_norm + 1e-06))
    step_value = jnp.float32(STEP_VALUE)
    factors = (
        clip_factor,
        1.0 - jnp.power(jnp.float32(BETA_FIRST), step_value),
        1.0 - jnp.power(jnp.float32(BETA_SECOND), step_value),
    )
    return (
        with_half(result, got_result),
        with_half(input_rows, got_input),
        *adam_update(
            attention_weight,
            attention_first,
            attention_second,
            attention_sum,
            factors,
            MATRIX_RATE,
            DECAY,
        ),
        *adam_update(
            widen_weight, widen_first, widen_second, widen_sum.T, factors, MATRIX_RATE, DECAY
        ),
        *adam_update(
            narrow_weight, narrow_first, narrow_second, narrow_sum, factors, MATRIX_RATE, DECAY
        ),
        *adam_update(norm_gains, gains_first, gains_second, gains_sum, factors, GAIN_RATE, 0.0),
        grad_norm,
    )


def solution(mesh):
    both = ("dp", "fsdp")
    rows = P(None, both, None)
    tall = P(both, None)
    wide = P(None, both)
    flat = P(both)
    weights = (tall, tall, tall, wide, wide, wide, tall, tall, tall, flat, flat, flat)
    own_kernels = dict(mesh.shape) == {"dp": 16, "fsdp": 2}
    return jax.shard_map(
        functools.partial(local, own_kernels),
        mesh=mesh,
        in_specs=(rows, rows, P(None, "dp", None)) + weights,
        out_specs=(rows, rows) + weights + (P(),),
        check_vma=False,
    )
```

```python
import functools

import jax
import jax.numpy as jnp
from jax import lax
from jax.experimental import pallas as pl
from jax.experimental.pallas import tpu as pltpu
from jax.sharding import PartitionSpec as P

HD = 64
TEXT = 128
PATCH = 256
ROW = 1152
WIDTH = 1024
HALF = ROW // 2
QUERY_TILE = 576
BACK_TILE = 384
FF_BLOCK = 256
GATHER_ROWS = 16
REDUCE_ROWS = 16
LAG = 2

NORM_EPS = 1e-06
MASKED = -(2.0**30)
BETA_FIRST = 0.9
BETA_SECOND = 0.999
ADAM_EPS = 1e-08
MATRIX_RATE = 0.05
GAIN_RATE = 0.3
DECAY = 0.1
CLIP_LIMIT = 1.0
STEP_VALUE = 10.0
GELU_SCALE = 0.7978845608028654
GELU_CUBE = 0.044715

BF16 = jnp.bfloat16
F32 = jnp.float32
MESH = pl.DeviceIdType.MESH
ANY = pl.BlockSpec(memory_space=pl.ANY)
VMEM_WHOLE = pl.BlockSpec(memory_space=pltpu.VMEM)
DMA = pltpu.SemaphoreType.DMA
VMEM_LIMIT = 60 * 2**20

NT = (((1,), (1,)), ((), ()))
TN = (((0,), (0,)), ((), ()))


def dot(left, right, dims=(((1,), (0,)), ((), ()))):
    return lax.dot_general(left, right, dims, preferred_element_type=F32)


class Place:
    def __init__(self):
        self.dp = lax.axis_index("dp")
        self.core = lax.axis_index("fsdp")
        self.z = self.dp // 4
        self.y = lax.rem(self.dp // 2, 2)
        self.x = lax.rem(self.dp, 2)
        flip_y = 1 - self.y
        flip_x = 1 - self.x
        is_zero = self.core == 0
        self.own = (self.y, self.x)
        self.first = (jnp.where(is_zero, self.y, flip_y), jnp.where(is_zero, flip_x, self.x))
        self.second = (jnp.where(is_zero, flip_y, self.y), jnp.where(is_zero, self.x, flip_x))
        self.across = (flip_y, flip_x)

    def at(self, z, spot):
        return (z * 4 + spot[0] * 2 + spot[1], self.core)

    def above(self, step):
        return self.at(lax.rem(self.z + step, 4), self.own)

    def to_first(self):
        return self.at(self.z, self.first)

    def to_second(self):
        return self.at(self.z, self.second)

    def sibling(self):
        return (self.dp, 1 - self.core)

    def greet(self):
        barrier = pltpu.get_barrier_semaphore()
        peers = [self.above(1), self.above(2), self.above(3)]
        peers += [self.to_first(), self.to_second(), self.sibling()]
        for peer in peers:
            pl.semaphore_signal(barrier, inc=1, device_id=peer, device_id_type=MESH)
        pl.semaphore_wait(barrier, len(peers))


def remote(source, target, send_sem, recv_sem, device):
    return pltpu.make_async_remote_copy(
        src_ref=source,
        dst_ref=target,
        send_sem=send_sem,
        recv_sem=recv_sem,
        device_id=device,
        device_id_type=MESH,
    )


def cut(index, rows, most):
    pieces = -(-rows // most)
    step = -(-rows // (pieces * 16)) * 16
    return [(index, at, min(step, rows - at)) for at in range(0, rows, step)]


class Gather:
    def __init__(self, shards, swaps=(), most=GATHER_ROWS, lag=LAG):
        self.arrays = [*shards, *swaps]
        self.shards, self.swaps = len(shards), len(swaps)
        self.chunks = []
        for index, shard in enumerate(shards):
            self.chunks += cut(index, shard.shape[0], most * WIDTH // shard.shape[1])
        count = len(self.chunks)
        self.lag = lag
        self.ticks = count + 3 * lag
        self.in_specs = [VMEM_WHOLE] * len(self.arrays)
        self.out_shapes = [jax.ShapeDtypeStruct((4, 2, 2, 2) + a.shape, a.dtype) for a in shards]
        self.out_shapes += [jax.ShapeDtypeStruct(a.shape, a.dtype) for a in swaps]
        self.out_specs = [ANY] * len(self.arrays)
        self.scratch = [
            DMA((count,)),
            DMA((count, 3)),
            DMA((count, 3)),
            DMA((count, 3)),
            DMA((count, 3)),
            DMA((count, 4)),
            DMA((count, 4)),
            DMA((max(self.swaps, 1),)),
            DMA((max(self.swaps, 1),)),
            DMA((max(self.swaps, 1),)),
        ]

    def bind(self, ins, outs, scratch):
        self.ins, self.outs = ins, outs
        (
            self.own_sem,
            self.z_send,
            self.z_recv,
            self.p_send,
            self.p_recv,
            self.c_send,
            self.c_recv,
            self.s_own,
            self.s_send,
            self.s_recv,
        ) = scratch
        self.claimed = set()
        self.here = Place()
        self.columns = (self.here.own, self.here.first, self.here.second, self.here.across)

    def spot(self, k, where):
        array, start, rows = self.chunks[k]
        return self.outs[array].at[:, where[0], where[1], self.here.core, pl.ds(start, rows), :]

    def mine(self, k):
        array, start, rows = self.chunks[k]
        here = self.here
        return (
            self.ins[array].at[pl.ds(start, rows), :],
            self.outs[array].at[here.z, here.y, here.x, here.core, pl.ds(start, rows), :],
        )

    def keep(self, k):
        source, target = self.mine(k)
        return pltpu.make_async_copy(source, target, self.own_sem.at[k])

    def along_z(self, k, step):
        source, target = self.mine(k)
        return remote(
            source,
            target,
            self.z_send.at[k, step - 1],
            self.z_recv.at[k, step - 1],
            self.here.above(step),
        )

    def plane(self, k, index):
        where = self.here.first if index == 2 else self.here.own
        device = self.here.to_first() if index == 0 else self.here.to_second()
        return remote(
            self.spot(k, where),
            self.spot(k, where),
            self.p_send.at[k, index],
            self.p_recv.at[k, index],
            device,
        )

    def to_sibling(self, k, index):
        where = self.columns[index]
        return remote(
            self.spot(k, where),
            self.spot(k, where),
            self.c_send.at[k, index],
            self.c_recv.at[k, index],
            self.here.sibling(),
        )

    def swap(self, index):
        source = self.ins[self.shards + index]
        target = self.outs[self.shards + index]
        core = self.here.core
        return (
            pltpu.make_async_copy(source.at[core], target.at[core], self.s_own.at[index]),
            remote(
                source.at[1 - core],
                target.at[core],
                self.s_send.at[index],
                self.s_recv.at[index],
                self.here.sibling(),
            ),
        )

    def tick(self, tick):
        count = len(self.chunks)
        if tick < count:
            self.keep(tick).start()
            for step in (2, 1, 3):
                self.along_z(tick, step).start()
        if tick == 0:
            for index in range(self.swaps):
                for copy in self.swap(index):
                    copy.start()
        k = tick - self.lag
        if 0 <= k < count:
            self.keep(k).wait()
            for step in (1, 2, 3):
                self.along_z(k, step).wait_recv()
            self.plane(k, 1).start()
            self.plane(k, 0).start()
            self.to_sibling(k, 0).start()
        k = tick - 2 * self.lag
        if 0 <= k < count:
            self.plane(k, 0).wait_recv()
            self.plane(k, 2).start()
            self.to_sibling(k, 1).start()
            self.plane(k, 1).wait_recv()
            self.to_sibling(k, 2).start()
        k = tick - 3 * self.lag
        if 0 <= k < count:
            self.plane(k, 2).wait_recv()
            self.to_sibling(k, 3).start()

    def arrived(self, k):
        self.claimed.add(k)
        for index in range(4):
            self.to_sibling(k, index).wait_recv()

    def finish(self):
        for k in range(len(self.chunks)):
            for step in (1, 2, 3):
                self.along_z(k, step).wait_send()
            for index in range(3):
                self.plane(k, index).wait_send()
            for index in range(4):
                self.to_sibling(k, index).wait_send()
                if k not in self.claimed:
                    self.to_sibling(k, index).wait_recv()
        for index in range(self.swaps):
            for copy in self.swap(index):
                copy.wait()


class Reduce:
    def __init__(self, gradients, inside=(), swaps=(), most=REDUCE_ROWS, lag=LAG):
        self.arrays = [*gradients, *swaps]
        self.outside, self.inside, self.swaps = len(gradients), list(inside), len(swaps)
        self.chunks = []
        for index, gradient in enumerate(gradients):
            self.chunks += cut(index, gradient.shape[4], most)
        shapes = [g.shape[4:] for g in gradients] + self.inside
        for index, shape in enumerate(self.inside):
            made = cut(self.outside + index, shape[0], most * WIDTH // shape[1])
            self.weave(made)
        count = len(self.chunks)
        self.lag = lag
        self.ticks = count + 4 * lag
        padded = [(-(-s[0] // 16) * 16, s[1]) for s in shapes]
        self.total_count = len(shapes)
        self.in_specs = [ANY] * len(self.arrays)
        self.out_shapes = [jax.ShapeDtypeStruct(s, F32) for s in shapes]
        self.out_shapes += [jax.ShapeDtypeStruct(a.shape[1:], a.dtype) for a in swaps]
        self.out_specs = [VMEM_WHOLE] * len(shapes) + [ANY] * len(swaps)
        self.scratch = [pltpu.VMEM((4, 2, 2) + s, BF16) for s in padded[: self.outside]]
        self.scratch += [pltpu.VMEM((4, 2, 2, 2) + s, BF16) for s in self.inside]
        for lead in ((4, 2, 2), (2, 4), (4,), (3,)):
            self.scratch += [pltpu.VMEM(lead + s, BF16) for s in padded]
        self.scratch += [
            DMA((count,)),
            DMA((count,)),
            DMA((count,)),
            DMA((count, 3)),
            DMA((count, 3)),
            DMA((count, 3)),
            DMA((count, 3)),
            DMA((max(self.swaps, 1),)),
            DMA((max(self.swaps, 1),)),
        ]

    def weave(self, made):
        others, self.chunks, self.starts = self.chunks, [], []
        for index, chunk in enumerate(made):
            for _ in range(2 if index == 0 else 1):
                if others:
                    self.chunks.append(others.pop(0))
            self.starts.append(len(self.chunks))
            self.chunks.append(chunk)
        self.chunks += others

    def bind(self, ins, outs, scratch):
        n = self.total_count
        self.ins, self.outs = ins, outs
        self.own = scratch[:n]
        self.from_core, self.from_second, self.from_first, self.from_z = (
            scratch[i * n : (i + 1) * n] for i in range(1, 5)
        )
        (
            self.own_sem,
            self.c_send,
            self.c_recv,
            self.p_send,
            self.p_recv,
            self.z_send,
            self.z_recv,
            self.s_send,
            self.s_recv,
        ) = scratch[5 * n :]
        self.here = Place()

    def part(self, k):
        array, start, rows = self.chunks[k]
        return array, pl.ds(start, rows)

    def own_at(self, k, z, y, x):
        array, rows = self.part(k)
        if array < self.outside:
            return self.own[array].at[z, y, x, rows, :]
        return self.own[array].at[z, y, x, self.here.core, rows, :]

    def load(self, k):
        array, rows = self.part(k)
        return pltpu.make_async_copy(
            self.ins[array].at[:, :, :, self.here.core, rows, :],
            self.own[array].at[:, :, :, rows, :],
            self.own_sem.at[k],
        )

    def swap_core(self, k):
        array, rows = self.part(k)
        source = self.ins[array] if array < self.outside else self.own[array]
        return remote(
            source.at[:, :, :, 1 - self.here.core, rows, :],
            self.from_core[array].at[:, :, :, rows, :],
            self.c_send.at[k],
            self.c_recv.at[k],
            self.here.sibling(),
        )

    def send_second(self, k, index):
        array, rows = self.part(k)
        where = self.here.second if index == 0 else self.here.across
        return remote(
            self.own_at(k, slice(None), *where),
            self.from_second[array].at[index, :, rows, :],
            self.p_send.at[k, index],
            self.p_recv.at[k, index],
            self.here.to_second(),
        )

    def send_first(self, k):
        array, rows = self.part(k)
        return remote(
            self.own_at(k, slice(None), *self.here.first),
            self.from_first[array].at[:, rows, :],
            self.p_send.at[k, 2],
            self.p_recv.at[k, 2],
            self.here.to_first(),
        )

    def send_z(self, k, step):
        array, rows = self.part(k)
        here = self.here
        return remote(
            self.own_at(k, lax.rem(here.z + step, 4), *here.own),
            self.from_z[array].at[step - 1, rows, :],
            self.z_send.at[k, step - 1],
            self.z_recv.at[k, step - 1],
            here.above(step),
        )

    def swap(self, index):
        source = self.ins[self.outside + index]
        return remote(
            source.at[1 - self.here.core],
            self.outs[self.total_count + index],
            self.s_send.at[index],
            self.s_recv.at[index],
            self.here.sibling(),
        )

    def add_all(self, k):
        array, rows = self.part(k)
        other = self.from_core[array]

        def body(i, carry):
            z, y, x = i // 4, lax.rem(i // 2, 2), lax.rem(i, 2)
            own = self.own_at(k, z, y, x)
            own[...] = both_sum(own[...], other[z, y, x, rows, :])
            return carry

        lax.fori_loop(0, 16, body, 0)

    def add_column(self, k, where, other):
        rows = self.part(k)[1]

        def body(z, carry):
            own = self.own_at(k, z, *where)
            own[...] = both_sum(own[...], other[z, rows, :])
            return carry

        lax.fori_loop(0, 4, body, 0)

    def total(self, k):
        array, rows = self.part(k)
        total = self.own_at(k, self.here.z, *self.here.own)[...].astype(F32)
        for step in range(3):
            total = total + self.from_z[array][step, rows, :].astype(F32)
        self.outs[array][rows, :] = total

    def tick(self, tick):
        count = len(self.chunks)
        if tick < count:
            self.swap_core(tick).start()
            if self.chunks[tick][0] < self.outside:
                self.load(tick).start()
        if tick == 1:
            for index in range(self.swaps):
                self.swap(index).start()
        k = tick - self.lag
        if 0 <= k < count:
            if self.chunks[k][0] < self.outside:
                self.load(k).wait()
            else:
                self.swap_core(k).wait_send()
            self.swap_core(k).wait_recv()
            self.add_all(k)
            for index in (1, 0):
                self.send_second(k, index).start()
        k = tick - 2 * self.lag
        if 0 <= k < count:
            array = self.chunks[k][0]
            self.send_second(k, 1).wait_recv()
            self.add_column(k, self.here.first, self.from_second[array].at[1])
            self.send_first(k).start()
            self.send_second(k, 0).wait_recv()
            self.add_column(k, self.here.own, self.from_second[array].at[0])
        k = tick - 3 * self.lag
        if 0 <= k < count:
            array = self.chunks[k][0]
            self.send_first(k).wait_recv()
            self.add_column(k, self.here.own, self.from_first[array])
            for step in (2, 1, 3):
                self.send_z(k, step).start()
        k = tick - 4 * self.lag
        if 0 <= k < count:
            for step in (1, 2, 3):
                self.send_z(k, step).wait_recv()
            self.total(k)

    def finish(self):
        for k in range(len(self.chunks)):
            if self.chunks[k][0] < self.outside:
                self.swap_core(k).wait_send()
            for index in (1, 0):
                self.send_second(k, index).wait_send()
            self.send_first(k).wait_send()
            for step in (1, 2, 3):
                self.send_z(k, step).wait_send()
        for index in range(self.swaps):
            self.swap(index).wait()


def both_sum(mine, other):
    return (mine.astype(F32) + other.astype(F32)).astype(BF16)


def everywhere(here, buffer, value, send, recv):
    for index, device in enumerate((here.sibling(), here.to_first(), here.to_second())):
        buffer[2 * index] = value
        copy = remote(
            buffer.at[2 * index], buffer.at[2 * index + 1], send.at[index], recv.at[index], device
        )
        copy.start()
        yield
        copy.wait()
        value = buffer[2 * index] + buffer[2 * index + 1]
    buffer[6 + here.z] = value
    copies = [
        remote(
            buffer.at[6 + here.z],
            buffer.at[6 + here.z],
            send.at[2 + step],
            recv.at[2 + step],
            here.above(step),
        )
        for step in (1, 2, 3)
    ]
    for copy in copies:
        copy.start()
    yield
    for copy in copies:
        copy.wait()
    yield (buffer[6] + buffer[7]) + (buffer[8] + buffer[9])


def call(name, body, grid, inner, ins, in_specs, out_shapes, out_specs, scratch=(), comm=None, key=0, plan=None):
    params = {"vmem_limit_bytes": VMEM_LIMIT}
    if comm is None:

        def kernel(*refs):
            body(lambda point: None, *refs)

        extra = ([], [], [], [], [])
    else:
        params.update(collective_id=key, has_side_effects=True)
        extra = (comm.arrays, comm.in_specs, comm.out_shapes, comm.out_specs, comm.scratch)
        sizes = (len(ins), len(extra[0]), len(out_shapes), len(extra[2]), len(scratch), len(extra[4]))

        def kernel(*refs):
            parts, at = [], 0
            for size in sizes:
                parts.append(refs[at : at + size])
                at += size
            comm.bind(parts[1], parts[3], parts[5])
            step = pl.program_id(0)

            def pump(point):
                for tick in range(comm.ticks):
                    slot = plan[tick] if plan else tick * grid * inner // comm.ticks
                    if slot % inner == point:

                        @pl.when(step == slot // inner)
                        def _(tick=tick):
                            if tick == 0:
                                comm.here.greet()
                            comm.tick(tick)

            body(pump, *parts[0], *parts[2], *parts[4])

            @pl.when(step == grid - 1)
            def _():
                comm.finish()

    results = pl.pallas_call(
        kernel,
        grid=(grid,),
        out_shape=[*out_shapes, *extra[2]],
        in_specs=[*in_specs, *extra[1]],
        out_specs=[*out_specs, *extra[3]],
        scratch_shapes=[*scratch, *extra[4]],
        compiler_params=pltpu.CompilerParams(**params),
        name=name,
    )(*ins, *extra[0])
    return results[: len(out_shapes)], results[len(out_shapes) :]


def settle(rows, gains, sums, key):
    def kernel(rows_ref, gains_ref, *refs):
        sums_refs = refs[: len(sums)]
        got_ref, gains_out, square_out, buffer, send, recv, s_send, s_recv = refs[len(sums) :]
        here = Place()
        here.greet()
        swap = remote(rows_ref.at[1 - here.core], got_ref, s_send, s_recv, here.sibling())
        swap.start()
        squares = jnp.zeros((8, 128), F32)
        for ref in sums_refs:
            values = ref[...]
            squares = squares + jnp.sum((values * values).reshape(-1, 8, 128), axis=0)
        for total in everywhere(
            here, buffer, jnp.concatenate([gains_ref[...], squares], axis=0), send, recv
        ):
            pass
        gains_total = total[:16]
        gains_out[...] = gains_total
        square_out[...] = jnp.broadcast_to(
            jnp.sum(total[16:]) + jnp.sum(gains_total * gains_total), (8, 128)
        )
        swap.wait()

    return pl.pallas_call(
        kernel,
        out_shape=[
            jax.ShapeDtypeStruct(rows.shape[1:], F32),
            jax.ShapeDtypeStruct((16, 128), F32),
            jax.ShapeDtypeStruct((8, 128), F32),
        ],
        in_specs=[ANY, VMEM_WHOLE] + [VMEM_WHOLE] * len(sums),
        out_specs=[ANY, VMEM_WHOLE, VMEM_WHOLE],
        scratch_shapes=[pltpu.VMEM((10, 24, 128), F32), DMA((6,)), DMA((6,)), DMA, DMA],
        compiler_params=pltpu.CompilerParams(
            collective_id=key, has_side_effects=True, vmem_limit_bytes=VMEM_LIMIT
        ),
        name="settle",
    )(rows, gains, *sums)


def segment_lanes(counts):
    sizes = [jnp.where(counts[i] > 0, TEXT + PATCH * counts[i], 0) for i in range(3)]
    ends = (sizes[0], sizes[0] + sizes[1], sizes[0] + sizes[1] + sizes[2])
    places = jnp.arange(ROW, dtype=jnp.int32)[:, None]
    segment = sum((places >= end).astype(jnp.int32) for end in ends)
    lane = jnp.arange(2 * HD, dtype=jnp.int32)[None, :] % HD
    same = lane == segment
    queries = jnp.where((lane < 4) & ~same, MASKED, 0.0).astype(BF16)
    return queries, jnp.where(same, 1.0, 0.0).astype(BF16)


def lanes_of_heads():
    lane = lax.broadcasted_iota(jnp.int32, (1, 2 * HD), 1)
    return lane, (lane < HD, lane >= HD)


def attend_tiles(pump, pair, q_ref, k_ref, v_ref, mq_ref, mk_ref, o_ref, log_ref):
    lane, in_head = lanes_of_heads()
    key = jnp.concatenate([k_ref[...], mk_ref[...]], axis=1)
    value = v_ref[...]
    values = [jnp.where(mine, value, jnp.ones_like(value)) for mine in in_head]
    for index in range(ROW // QUERY_TILE):
        pump(index)
        rows = pl.ds(index * QUERY_TILE, QUERY_TILE)
        query, extra = q_ref[rows, :], mq_ref[rows, :]
        mixed = []
        logs = log_ref[rows, :]
        for head in range(2):
            masked = jnp.where(in_head[head], query, jnp.zeros_like(query))
            scores = dot(jnp.concatenate([masked, extra], axis=1), key, NT)
            top = jnp.max(scores, axis=-1, keepdims=True)
            weight = jnp.exp(scores - top).astype(BF16)
            both = dot(weight, values[head])
            other = pltpu.roll(both, HD, 1)
            mixed.append(both / other)
            total = jnp.where(in_head[head], other, both)
            logs = jnp.where(lane == 2 * pair + head, top + jnp.log(total), logs)
        log_ref[rows, :] = logs
        o_ref[rows, :] = jnp.where(in_head[0], mixed[0], mixed[1]).astype(BF16)


def attend_body(pump, q_ref, k_ref, v_ref, mq_ref, mk_ref, o_ref, log_ref):
    pair = pl.program_id(0)

    @pl.when(pair == 0)
    def _():
        log_ref[...] = jnp.zeros_like(log_ref)

    attend_tiles(
        pump, pair, q_ref.at[0], k_ref.at[0], v_ref.at[0], mq_ref, mk_ref, o_ref, log_ref
    )


PAIRS = WIDTH // (2 * HD)


def third(which):
    return pl.BlockSpec((1, ROW, 2 * HD), lambda p: (which, 0, p))


def attend(projected, extras):
    whole = pl.BlockSpec((ROW, 128), lambda p: (0, 0))
    return call(
        "attend",
        attend_body,
        PAIRS,
        ROW // QUERY_TILE,
        [projected, projected, projected, *extras],
        [third(0), third(1), third(2), whole, whole],
        [jax.ShapeDtypeStruct((ROW, WIDTH), BF16), jax.ShapeDtypeStruct((ROW, 128), F32)],
        [pl.BlockSpec((ROW, 2 * HD), lambda p: (0, p)), whole],
    )


def attend_back_tiles(
    pump, pair, q_ref, k_ref, v_ref, mq_ref, mk_ref, o_ref, do_ref, log_ref, dq_ref, dk, dv
):
    _, in_head = lanes_of_heads()
    pick = jnp.where(
        (lax.broadcasted_iota(jnp.int32, (8, 2 * HD), 1) < HD)
        == (lax.broadcasted_iota(jnp.int32, (8, 2 * HD), 0) == 0),
        jnp.ones((8, 2 * HD), F32),
        jnp.zeros((8, 2 * HD), F32),
    )

    def only(values, head):
        return jnp.where(in_head[head], values, jnp.zeros_like(values))

    dk[...] = jnp.zeros_like(dk)
    dv[...] = jnp.zeros_like(dv)
    for index in range(ROW // BACK_TILE):
        pump(index)
        rows = pl.ds(index * BACK_TILE, BACK_TILE)
        query, grad, extra = q_ref[rows, :], do_ref[rows, :], mq_ref[rows, :]
        key, value = k_ref[...], v_ref[...]
        inner = lax.dot_general(
            pick,
            grad.astype(F32) * o_ref[rows, :].astype(F32),
            NT,
            precision=lax.Precision.HIGHEST,
            preferred_element_type=F32,
        )
        dq = None
        for head in range(2):
            log_total = log_ref[
                pl.ds(2 * pair + head, 1), index * BACK_TILE : (index + 1) * BACK_TILE
            ]
            scores = dot(
                jnp.where(in_head[head], key, mk_ref[...]),
                jnp.where(in_head[head], query, extra),
                NT,
            )
            weight = jnp.exp(scores - log_total)
            down = dot(only(value, head), grad, NT)
            slope = (weight * (down - inner[head : head + 1, :])).astype(BF16)
            dv[...] += dot(weight.astype(BF16), only(grad, head))
            dk[...] += dot(slope, only(query, head))
            step = dot(slope, only(key, head), TN)
            dq = step if dq is None else dq + step
        dq_ref[rows, :] = dq.astype(BF16)


def attend_back_body(
    pump, q_ref, k_ref, v_ref, mq_ref, mk_ref, o_ref, do_ref, log_ref, out_ref, dk, dv
):
    attend_back_tiles(
        pump, pl.program_id(0), q_ref.at[0], k_ref.at[0], v_ref.at[0], mq_ref, mk_ref, o_ref,
        do_ref, log_ref, out_ref.at[0], dk, dv,
    )
    out_ref[1] = dk[...].astype(BF16)
    out_ref[2] = dv[...].astype(BF16)


def attend_back(projected, extras, mixed, grad_mixed, log_rows):
    whole = pl.BlockSpec((ROW, 128), lambda p: (0, 0))
    column = pl.BlockSpec((ROW, 2 * HD), lambda p: (0, p))
    return call(
        "attend_back",
        attend_back_body,
        PAIRS,
        ROW // BACK_TILE,
        [projected, projected, projected, *extras, mixed, grad_mixed, log_rows],
        [third(0), third(1), third(2), whole, whole, column, column]
        + [pl.BlockSpec((2 * PAIRS, ROW), lambda p: (0, 0))],
        [jax.ShapeDtypeStruct((3, ROW, WIDTH), BF16)],
        [pl.BlockSpec((3, ROW, 2 * HD), lambda p: (0, 0, p))],
        [pltpu.VMEM((ROW, 2 * HD), F32), pltpu.VMEM((ROW, 2 * HD), F32)],
    )


def feed_units(pump, n2_ref, cot_ref, widen_ref, narrow_ref, widen_grad_ref, narrow_grad_ref):
    pump(0)
    n2, cot = n2_ref[...], cot_ref[...]
    wide_gate, wide_up, narrow = widen_ref[0], widen_ref[1], narrow_ref[...]
    gate = dot(n2, wide_gate, NT)
    up = dot(n2, wide_up, NT)
    down = dot(cot, narrow, NT)
    square = gate * gate
    bend = jnp.tanh(GELU_SCALE * gate * (1.0 + GELU_CUBE * square))
    half = 0.5 * (1.0 + bend)
    curve = gate * half
    slope = half + 0.5 * gate * (1.0 - bend * bend) * (
        GELU_SCALE * (1.0 + 3.0 * GELU_CUBE * square)
    )
    hidden = (curve * up).astype(BF16)
    grad_gate = (down * up * slope).astype(BF16)
    grad_up = (down * curve).astype(BF16)
    pump(1)
    narrow_grad_ref[...] = dot(hidden, cot, TN).astype(BF16)
    widen_grad_ref[0] = dot(grad_gate, n2, TN).astype(BF16)
    widen_grad_ref[1] = dot(grad_up, n2, TN).astype(BF16)
    return lambda: dot(hidden, narrow), lambda: dot(grad_gate, wide_gate) + dot(grad_up, wide_up)


def feed_start_body(
    pump, n2_ref, cot_ref, widen_ref, narrow_ref, result_ref, back_ref, widen_grad_ref, narrow_grad_ref
):
    result, back = feed_units(
        pump, n2_ref, cot_ref, widen_ref, narrow_ref, widen_grad_ref, narrow_grad_ref
    )

    @pl.when(pl.program_id(0) == 0)
    def _():
        result_ref[...] = jnp.zeros_like(result_ref)
        back_ref[...] = jnp.zeros_like(back_ref)

    result_ref[...] += result()
    back_ref[...] += back()


def feed_end_body(
    pump, n2_ref, cot_ref, h1_ref, gain_ref, result_part, back_part, widen_ref, narrow_ref,
    result_ref, dh1_ref, e_ref, gain_grad_ref, widen_grad_ref, narrow_grad_ref,
    back_ref, part_sem,
):
    step = pl.program_id(0)
    parts = (
        pltpu.make_async_copy(result_part, result_ref, part_sem.at[0]),
        pltpu.make_async_copy(back_part, back_ref, part_sem.at[1]),
    )

    @pl.when(step == 0)
    def _():
        for part in parts:
            part.start()

    result, back = feed_units(
        pump, n2_ref, cot_ref, widen_ref, narrow_ref, widen_grad_ref, narrow_grad_ref
    )

    @pl.when(step == 0)
    def _():
        for part in parts:
            part.wait()

    result_ref[...] += result()
    back_ref[...] += back()

    @pl.when(step == pl.num_programs(0) - 1)
    def _():
        gain = gain_ref[...]

        def tile(i, total):
            rows = pl.ds(pl.multiple_of(i * 64, 64), 64)
            h1 = h1_ref[rows, :]
            grad = back_ref[rows, :]
            result_ref[rows, :] += h1
            scale = lax.rsqrt(jnp.mean(h1 * h1, axis=-1, keepdims=True) + NORM_EPS)
            lifted = gain * grad
            inner = jnp.mean(h1 * lifted, axis=-1, keepdims=True)
            dh1 = (
                cot_ref[rows, :].astype(F32)
                + scale * lifted
                - h1 * (scale * scale * scale * inner)
            )
            dh1_ref[rows, :] = dh1
            e_ref[rows, :] = dh1.astype(BF16)
            return total + jnp.sum((grad * h1 * scale).reshape(8, 8, WIDTH), axis=0)

        total = lax.fori_loop(0, ROW // 64, tile, jnp.zeros((8, WIDTH), F32))
        gain_grad_ref[...] = jnp.sum(total, axis=0, keepdims=True)


def whole_block(*shape):
    return pl.BlockSpec(shape, lambda j: (0,) * len(shape), pipeline_mode=pl.Buffered(1))


WIDE_BLOCK = pl.BlockSpec((2, FF_BLOCK, WIDTH), lambda j: (0, j, 0))
TALL_BLOCK = pl.BlockSpec((FF_BLOCK, WIDTH), lambda j: (j, 0))
ROW_F32 = jax.ShapeDtypeStruct((ROW, WIDTH), F32)
ROW_BF16 = jax.ShapeDtypeStruct((ROW, WIDTH), BF16)


def feed_start(n2, cot, widen, narrow, comm=None, key=0):
    rows = whole_block(ROW, WIDTH)
    return call(
        "feed_start",
        feed_start_body,
        narrow.shape[0] // FF_BLOCK,
        2,
        [n2, cot, widen, narrow],
        [rows, rows, WIDE_BLOCK, TALL_BLOCK],
        [
            ROW_F32,
            ROW_F32,
            jax.ShapeDtypeStruct(widen.shape, BF16),
            jax.ShapeDtypeStruct(narrow.shape, BF16),
        ],
        [rows, rows, WIDE_BLOCK, TALL_BLOCK],
        comm=comm,
        key=key,
    )


def feed_end(n2, cot, h1, gain, result_part, back_part, widen, narrow, comm=None, key=0):
    rows = whole_block(ROW, WIDTH)
    line = whole_block(1, WIDTH)
    return call(
        "feed_end",
        feed_end_body,
        narrow.shape[0] // FF_BLOCK,
        2,
        [n2, cot, h1, gain, result_part, back_part, widen, narrow],
        [rows, rows, rows, line, ANY, ANY, WIDE_BLOCK, TALL_BLOCK],
        [
            ROW_F32,
            ROW_F32,
            ROW_BF16,
            jax.ShapeDtypeStruct((1, WIDTH), F32),
            jax.ShapeDtypeStruct(widen.shape, BF16),
            jax.ShapeDtypeStruct(narrow.shape, BF16),
        ],
        [rows, rows, rows, line, WIDE_BLOCK, TALL_BLOCK],
        [pltpu.VMEM((ROW, WIDTH), F32), DMA((2,))],
        comm=comm,
        key=key,
    )


def front(attention_shard, gains_tile, feed_shards, tokens, cotangent, extras, key):
    comm = Gather((gains_tile, attention_shard, *feed_shards), (cotangent,), most=16, lag=2)
    points = [0] * 7 + [1] * 2
    rest = comm.ticks - len(points)
    points += [2 + tick * (5 * PAIRS - 2) // rest for tick in range(rest)]

    def body(
        pump, tokens_ref, mq_ref, mk_ref,
        turned_ref, row_ref, qkv_ref, o_ref, o_turned_ref, log_ref, h1_ref, n2_ref,
        normed, landed, parts, out_weights, o_all, gains, t_send, t_recv, part_sem, gains_sem,
    ):
        pair = pl.program_id(0)
        here = comm.here
        core = here.core
        across = remote(tokens_ref.at[1 - core], landed, t_send, t_recv, here.sibling())

        def fetch(p, slot):
            return pltpu.make_async_copy(
                comm.outs[1].at[:, :, :, :, pl.ds(128 * p, 128), :], parts.at[slot], part_sem.at[slot]
            )

        pump(0)

        @pl.when(pair == 0)
        def _():
            across.start()
            log_ref[...] = jnp.zeros_like(log_ref)
            row_ref[core] = tokens_ref[core]
            across.wait_recv()
            row_ref[1 - core] = landed[...]
            comm.arrived(0)
            copy = pltpu.make_async_copy(comm.outs[0], gains, gains_sem)
            copy.start()
            copy.wait()

        def gain_of(which):
            tiles = [
                gains[which * 2 + z, y, x, 0, 0:1, :] + gains[which * 2 + z, y, x, 1, 0:1, :]
                for z in range(2)
                for y in range(2)
                for x in range(2)
            ]
            return jnp.concatenate(tiles, axis=1).astype(F32)

        @pl.when(pair == 0)
        def _():
            gain = gain_of(0)
            for half in range(2):

                def tile(i, carry, half=half):
                    rows = pl.ds(pl.multiple_of(i * 64, 64), 64)
                    x = row_ref[half, rows, :].astype(F32)
                    scale = lax.rsqrt(jnp.mean(x * x, axis=-1, keepdims=True) + NORM_EPS)
                    normed[pl.ds(pl.multiple_of(half * HALF + i * 64, 64), 64), :] = (
                        x * scale * gain
                    ).astype(BF16)
                    return carry

                lax.fori_loop(0, HALF // 64, tile, 0)
            turned_ref[...] = normed[...].T

        pump(1)

        @pl.when(pair == 0)
        def _():
            comm.arrived(1)
            fetch(0, 0).start()

        slot = lax.rem(pair, 2)
        fetch(pair, slot).wait()
        weights = parts[slot].reshape(4, WIDTH, 128)
        three = dot(normed[...], jnp.concatenate([weights[0], weights[1], weights[2]], axis=1))
        for index in range(3):
            qkv_ref[index] = three[:, 128 * index : 128 * (index + 1)].astype(BF16)
        out_weights[pair] = weights[3]
        pump(2)
        for p in range(1, PAIRS):

            @pl.when(pair == p - 1)
            def _(p=p):
                comm.arrived(1 + p)
                fetch(p, p % 2).start()

        attend_tiles(
            lambda index: pump(3 + index),
            pair,
            qkv_ref.at[0],
            qkv_ref.at[1],
            qkv_ref.at[2],
            mq_ref,
            mk_ref,
            o_ref,
            log_ref,
        )
        mixed = o_ref[...]
        o_all[:, pl.ds(pl.multiple_of(pair * 128, 128), 128)] = mixed
        o_turned_ref[...] = mixed.T

        @pl.when(pair == PAIRS - 1)
        def _():
            across.wait_send()
            full = jnp.concatenate([out_weights[p] for p in range(PAIRS)], axis=1)
            gain = gain_of(1)
            for part in range(4):
                rows = pl.ds(part * (ROW // 4), ROW // 4)
                x = row_ref[part // 2, pl.ds((part % 2) * (ROW // 4), ROW // 4), :].astype(F32)
                h1_ref[rows, :] = x + dot(o_all[rows, :], full)

            def tile(i, carry):
                rows = pl.ds(pl.multiple_of(i * 64, 64), 64)
                h1 = h1_ref[rows, :]
                scale = lax.rsqrt(jnp.mean(h1 * h1, axis=-1, keepdims=True) + NORM_EPS)
                n2_ref[rows, :] = (h1 * scale * gain).astype(BF16)
                return carry

            lax.fori_loop(0, ROW // 64, tile, 0)

    whole = pl.BlockSpec((ROW, 128), lambda p: (0, 0))
    turned = jax.ShapeDtypeStruct((WIDTH, ROW), BF16)
    return call(
        "front",
        body,
        PAIRS,
        5,
        [tokens, *extras],
        [VMEM_WHOLE, whole, whole],
        [
            turned,
            jax.ShapeDtypeStruct((2, HALF, WIDTH), BF16),
            jax.ShapeDtypeStruct((3, ROW, WIDTH), BF16),
            ROW_BF16,
            turned,
            jax.ShapeDtypeStruct((ROW, 128), F32),
            ROW_F32,
            ROW_BF16,
        ],
        [
            whole_block(WIDTH, ROW),
            whole_block(2, HALF, WIDTH),
            pl.BlockSpec((3, ROW, 128), lambda p: (0, 0, p)),
            pl.BlockSpec((ROW, 128), lambda p: (0, p)),
            pl.BlockSpec((128, ROW), lambda p: (p, 0)),
            whole,
            whole_block(ROW, WIDTH),
            whole_block(ROW, WIDTH),
        ],
        [
            pltpu.VMEM((ROW, WIDTH), BF16),
            pltpu.VMEM((HALF, WIDTH), BF16),
            pltpu.VMEM((2, 4, 2, 2, 2, 128, 128), BF16),
            pltpu.VMEM((PAIRS, WIDTH, 128), BF16),
            pltpu.VMEM((ROW, WIDTH), BF16),
            pltpu.VMEM((4, 2, 2, 2, 16, 128), BF16),
            DMA,
            DMA,
            DMA((2,)),
            DMA,
        ],
        comm,
        key,
        points,
    )


PART = 144


def back(
    gradients, result, e, dh1, tokens_row, gain, projected, extras, mixed, log_rows,
    attention_parts, normed_turned, mixed_turned, key,
):
    comm = Reduce(gradients, [(PAIRS * 128, 128)], (result,), most=16, lag=1)
    inner, made, rest = 6, 4, 5
    plan = []
    for tick in range(comm.ticks):
        if tick in comm.starts:
            plan.append(comm.starts.index(tick) * inner + made)
        elif tick < 2:
            plan.append(tick)
        elif tick < comm.starts[-1]:
            plan.append((plan[-1] // inner + 1) * inner + 2)
        else:
            plan.append((PAIRS - 1) * inner + rest)

    def body(
        pump, q_ref, k_ref, v_ref, mq_ref, mk_ref, o_ref, log_ref, parts_ref, rows_ref,
        e_ref, n_turned_ref, o_turned_ref, gain_ref, tokens_ref, dh1_ref,
        da_ref, gain_grad_ref,
        do, three, dk, dv, x_part, dh1_part, x_sem, dh1_sem,
    ):
        pair = pl.program_id(0)
        pump(0)
        out_rows = rows_ref[0, 0, 0, 0]
        out_rows = jnp.concatenate(
            [out_rows[128 * p : 128 * (p + 1)] for p in range(PAIRS)], axis=1
        )
        do[...] = dot(e_ref[...], out_rows, NT).astype(BF16)
        attend_back_tiles(
            lambda index: pump(1 + index), pair, q_ref.at[0], k_ref.at[0], v_ref.at[0],
            mq_ref, mk_ref, o_ref, do, log_ref, three.at[:, 0:128], dk, dv,
        )
        three[:, 128:256] = dk[...].astype(BF16)
        three[:, 256:384] = dv[...].astype(BF16)
        made_ref = comm.own[comm.outside]
        mine = pl.ds(pl.multiple_of(pair * 128, 128), 128)
        grads = dot(n_turned_ref[...], three[...]).astype(BF16)
        for index in range(3):
            made_ref[index, :, :, :, mine, :] = grads[
                :, 128 * index : 128 * (index + 1)
            ].reshape(2, 2, 2, 128, 128)
        made_ref[3, :, :, :, mine, :] = (
            dot(o_turned_ref[...], e_ref[:, mine]).astype(BF16).reshape(2, 2, 2, 128, 128)
        )
        pump(made)
        weights = parts_ref[...].reshape(4, WIDTH, 128)
        columns = jnp.concatenate([weights[0], weights[1], weights[2]], axis=1)

        @pl.when(pair == 0)
        def _():
            da_ref[...] = dot(three[...], columns, NT)

        @pl.when(pair > 0)
        def _():
            da_ref[...] += dot(three[...], columns, NT)

        @pl.when(pair == PAIRS - 1)
        def _():
            def fetch(i):
                rows = pl.ds(i * PART, PART)
                slot = i % 2
                return (
                    pltpu.make_async_copy(tokens_ref.at[rows, :], x_part.at[slot], x_sem.at[slot]),
                    pltpu.make_async_copy(dh1_ref.at[rows, :], dh1_part.at[slot], dh1_sem.at[slot]),
                )

            gain_row = gain_ref[...]
            total = jnp.zeros((8, WIDTH), F32)
            for copy in fetch(0):
                copy.start()
            for i in range(ROW // PART):
                if i + 1 < ROW // PART:
                    for copy in fetch(i + 1):
                        copy.start()
                for copy in fetch(i):
                    copy.wait()

                def tile(j, total, i=i):
                    near = pl.ds(pl.multiple_of(j * 48, 16), 48)
                    rows = pl.ds(pl.multiple_of(i * PART + j * 48, 16), 48)
                    x = x_part[i % 2, near, :].astype(F32)
                    grad = da_ref[rows, :]
                    scale = lax.rsqrt(jnp.mean(x * x, axis=-1, keepdims=True) + NORM_EPS)
                    lifted = gain_row * grad
                    middle = jnp.mean(x * lifted, axis=-1, keepdims=True)
                    da_ref[rows, :] = (
                        dh1_part[i % 2, near, :]
                        + scale * lifted
                        - x * (scale * scale * scale * middle)
                    )
                    return total + jnp.sum((grad * x * scale).reshape(6, 8, WIDTH), axis=0)

                total = lax.fori_loop(0, PART // 48, tile, total)
            gain_grad_ref[...] = jnp.sum(total, axis=0, keepdims=True)

        pump(rest)

    extra = pl.BlockSpec((ROW, 128), lambda p: (0, 0), pipeline_mode=pl.Buffered(1))
    line = whole_block(1, WIDTH)
    return call(
        "back",
        body,
        PAIRS,
        inner,
        [projected, projected, projected, *extras, mixed, log_rows, attention_parts, attention_parts]
        + [e, normed_turned, mixed_turned, gain, tokens_row, dh1],
        [third(0), third(1), third(2), extra, extra]
        + [
            pl.BlockSpec((ROW, 128), lambda p: (0, p)),
            whole_block(2 * PAIRS, ROW),
            pl.BlockSpec((4, 2, 2, 2, 128, 128), lambda p: (0, 0, 0, 0, p, 0)),
            pl.BlockSpec(
                (1, 1, 1, 1, WIDTH, 128), lambda p: (3, p // 4, lax.rem(p // 2, 2), lax.rem(p, 2), 0, 0)
            ),
            whole_block(ROW, WIDTH),
            whole_block(WIDTH, ROW),
            whole_block(WIDTH, ROW),
            line,
            ANY,
            ANY,
        ],
        [ROW_F32, jax.ShapeDtypeStruct((1, WIDTH), F32)],
        [whole_block(ROW, WIDTH), line],
        [
            pltpu.VMEM((ROW, 128), BF16),
            pltpu.VMEM((ROW, 384), BF16),
            pltpu.VMEM((ROW, 128), F32),
            pltpu.VMEM((ROW, 128), F32),
            pltpu.VMEM((2, PART, WIDTH), BF16),
            pltpu.VMEM((2, PART, WIDTH), F32),
            DMA((2,)),
            DMA((2,)),
        ],
        comm,
        key,
        plan,
    )


def rms_scale(values, gain_vector):
    return (
        values
        * lax.rsqrt(jnp.mean(values * values, axis=-1, keepdims=True) + NORM_EPS)
        * gain_vector
    )


def adam_update(master, first, second, gradient, factors, rate, decay):
    clip_factor, first_fix, second_fix = factors
    clipped = clip_factor * gradient
    first_new = BETA_FIRST * first + (1.0 - BETA_FIRST) * clipped
    second_new = BETA_SECOND * second + (1.0 - BETA_SECOND) * clipped * clipped
    master_new = master - rate * (
        first_new / first_fix / (jnp.sqrt(second_new / second_fix) + ADAM_EPS) + decay * master
    )
    return (master_new, first_new, second_new)


def swap_halves(parts):
    core = lax.axis_index("fsdp")
    got = lax.ppermute(parts[1 - core], "fsdp", [(0, 1), (1, 0)])
    return jnp.where(core == 0, jnp.stack([parts[0], got]), jnp.stack([got, parts[1]]))


def with_half(rows, got):
    own = rows.reshape(2, HALF, WIDTH)
    first = lax.axis_index("fsdp") == 0
    return jnp.where(first, jnp.stack([own[0], got]), jnp.stack([got, own[1]]))


def local(
    own_kernels,
    tokens,
    cotangent,
    images,
    attention_weight,
    attention_first,
    attention_second,
    widen_weight,
    widen_first,
    widen_second,
    narrow_weight,
    narrow_first,
    narrow_second,
    norm_gains,
    gains_first,
    gains_second,
):
    axes = ("dp", "fsdp")
    devices = lax.axis_size(axes)
    core = lax.axis_index("fsdp")
    position = lax.axis_index(axes)
    gain_count = norm_gains.shape[0]
    units = narrow_weight.shape[0]
    split = units * 6 // 11
    attention_low = attention_weight.astype(BF16)
    widen_low = widen_weight.astype(BF16).T.reshape(2, units, WIDTH)
    narrow_low = narrow_weight.astype(BF16)
    gains_low = norm_gains.astype(BF16)
    feed_low = [
        (widen_low[:, :split].reshape(-1, WIDTH), narrow_low[:split]),
        (widen_low[:, split:].reshape(-1, WIDTH), narrow_low[split:]),
    ]
    grid = (4, 2, 2, 2)

    def fetch(shards):
        return [lax.all_gather(shard, axes, axis=0, tiled=True) for shard in shards]

    def summed(gradients):
        return [
            lax.psum_scatter(
                g.astype(F32).reshape(-1, 128), axes, scatter_dimension=0, tiled=True
            ).reshape(-1, WIDTH)
            for g in gradients
        ]

    def other_half(parts):
        return lax.ppermute(
            lax.dynamic_index_in_dim(parts, 1 - core, 0, keepdims=False), "fsdp", [(0, 1), (1, 0)]
        )

    def as_feed(shards):
        return shards[0].reshape(2, -1, WIDTH), shards[1].reshape(-1, WIDTH)

    def as_shards(*gradients):
        return [g.reshape(grid + (-1, WIDTH)) for g in gradients]

    counts = lax.dynamic_index_in_dim(images[:, 0, :], core, 0, keepdims=False)
    extras = segment_lanes(counts)
    gather_b = None
    if own_kernels:
        spread = jnp.zeros((2, gain_count), BF16).at[core].set(gains_low).reshape(1, -1)
        gains_tile = jnp.concatenate([spread, jnp.zeros((15, 2 * gain_count), BF16)], axis=0)
        columns = attention_low.reshape(-1, PAIRS, 2 * HD).transpose(1, 0, 2).reshape(-1, 2 * HD)
        (
            (normed_turned, tokens_row, projected, mixed, mixed_turned, log_columns, h1, n2),
            (gains_full, attention_parts, *feed_a, cotangent_row),
        ) = front(columns, gains_tile, feed_low[0], tokens, cotangent, extras, 0)
        gains_full = gains_full[:, :, :, :, 0, :].sum(axis=3).reshape(-1)
        gather_b = Gather(feed_low[1])
        cot = cotangent_row.reshape(ROW, WIDTH)
        inputs = tokens_row.reshape(ROW, WIDTH).astype(F32)
        first_gain = gains_full[:WIDTH].astype(F32)
        second_gain = gains_full[WIDTH:].astype(F32)
    else:
        attention_full, gains_full = fetch((attention_low, gains_low))
        first = core == 0
        tokens_row, cotangent_row = (
            jnp.where(first, jnp.stack([a[0], got]), jnp.stack([got, a[1]]))
            for a, got in ((a, other_half(a)) for a in (tokens, cotangent))
        )
        attention = attention_full.reshape(4, WIDTH, WIDTH)
        cot = cotangent_row.reshape(ROW, WIDTH)
        inputs = tokens_row.reshape(ROW, WIDTH).astype(F32)
        first_gain = gains_full[:WIDTH].astype(F32)
        second_gain = gains_full[WIDTH:].astype(F32)
        normed = rms_scale(inputs, first_gain).astype(BF16)
        projected = jnp.einsum(
            "sd,jde->jse", normed, attention[:3], preferred_element_type=F32
        ).astype(BF16)
        (mixed, log_columns), _ = attend(projected, extras)
        h1 = inputs + dot(mixed, attention[3])
        n2 = rms_scale(h1, second_gain).astype(BF16)
    log_rows = log_columns[:, : WIDTH // HD].T
    widen_a, narrow_a = as_feed(feed_a if own_kernels else fetch(feed_low[0]))
    (result_part, back_part, *grads_a), feed_b = feed_start(
        n2, cot, widen_a, narrow_a, gather_b, 2
    )
    widen_b, narrow_b = as_feed(feed_b if own_kernels else fetch(feed_low[1]))
    (result, dh1, e, grad_gain_two, *grads_b), sums_a = feed_end(
        n2,
        cot,
        h1,
        second_gain[None],
        result_part,
        back_part,
        widen_b,
        narrow_b,
        Reduce(as_shards(*grads_a)) if own_kernels else None,
        3,
    )
    if own_kernels:
        (input_rows, grad_gain_one), (*sums_b, attention_sum, got_result) = back(
            as_shards(*grads_b),
            result.reshape(2, HALF, WIDTH),
            e,
            dh1,
            tokens_row.reshape(ROW, WIDTH),
            first_gain[None],
            projected,
            extras,
            mixed,
            log_rows,
            attention_parts,
            normed_turned,
            mixed_turned,
            4,
        )
        got_input, gains_total, square_total = settle(
            input_rows.reshape(2, HALF, WIDTH),
            jnp.concatenate([grad_gain_one, grad_gain_two]).reshape(16, 128),
            [*sums_a, *sums_b, attention_sum],
            5,
        )
        attention_sum = (
            attention_sum.reshape(PAIRS, -1, 128).transpose(1, 0, 2).reshape(-1, WIDTH)
        )
        gains_sum = lax.dynamic_slice_in_dim(
            gains_total.reshape(-1), position * gain_count, gain_count
        )
        squares = square_total[0, 0]
    else:
        grad_out = dot(mixed, e, TN).astype(BF16)
        grad_mixed = dot(e, attention[3], NT).astype(BF16)
        (grad_projected,), _ = attend_back(projected, extras, mixed, grad_mixed, log_rows)
        grad_qkv = jnp.einsum(
            "sd,jse->jde", normed, grad_projected, preferred_element_type=F32
        ).astype(BF16)
        grad_normed = jnp.einsum(
            "jse,jde->sd", grad_projected, attention[:3], preferred_element_type=F32
        )
        scale = lax.rsqrt(jnp.mean(inputs * inputs, axis=-1, keepdims=True) + NORM_EPS)
        lifted = first_gain * grad_normed
        inner = jnp.mean(inputs * lifted, axis=-1, keepdims=True)
        input_rows = dh1 + scale * lifted - inputs * (scale * scale * scale * inner)
        grad_gain_one = jnp.sum(grad_normed * inputs * scale, axis=0)
        grad_attention = jnp.concatenate([grad_qkv, grad_out[None]], axis=0)
        grad_gains = jnp.concatenate([grad_gain_one, grad_gain_two[0]])
        sums_a, sums_b, (attention_sum,) = summed(grads_a), summed(grads_b), summed([grad_attention])
        gains_sum = lax.psum_scatter(grad_gains, axes, scatter_dimension=0, tiled=True)
        squares = lax.psum(
            sum(jnp.sum(g * g) for g in (*sums_a, *sums_b, attention_sum, gains_sum)), axes
        )
        got_result = other_half(result.reshape(2, HALF, WIDTH))
        got_input = other_half(input_rows.reshape(2, HALF, WIDTH))
    widen_sum = jnp.concatenate(
        [sums_a[0].reshape(2, -1, WIDTH), sums_b[0].reshape(2, -1, WIDTH)], axis=1
    ).reshape(-1, WIDTH)
    narrow_sum = jnp.concatenate([sums_a[1], sums_b[1]], axis=0)
    grad_norm = jnp.sqrt(squares)
    clip_factor = jnp.minimum(1.0, CLIP_LIMIT / (grad_norm + 1e-06))
    step_value = jnp.float32(STEP_VALUE)
    factors = (
        clip_factor,
        1.0 - jnp.power(jnp.float32(BETA_FIRST), step_value),
        1.0 - jnp.power(jnp.float32(BETA_SECOND), step_value),
    )
    return (
        with_half(result, got_result),
        with_half(input_rows, got_input),
        *adam_update(
            attention_weight,
            attention_first,
            attention_second,
            attention_sum,
            factors,
            MATRIX_RATE,
            DECAY,
        ),
        *adam_update(
            widen_weight, widen_first, widen_second, widen_sum.T, factors, MATRIX_RATE, DECAY
        ),
        *adam_update(
            narrow_weight, narrow_first, narrow_second, narrow_sum, factors, MATRIX_RATE, DECAY
        ),
        *adam_update(norm_gains, gains_first, gains_second, gains_sum, factors, GAIN_RATE, 0.0),
        grad_norm,
    )


def solution(mesh):
    both = ("dp", "fsdp")
    rows = P(None, both, None)
    tall = P(both, None)
    wide = P(None, both)
    flat = P(both)
    weights = (tall, tall, tall, wide, wide, wide, tall, tall, tall, flat, flat, flat)
    own_kernels = dict(mesh.shape) == {"dp": 16, "fsdp": 2}
    return jax.shard_map(
        functools.partial(local, own_kernels),
        mesh=mesh,
        in_specs=(rows, rows, P(None, "dp", None)) + weights,
        out_specs=(rows, rows) + weights + (P(),),
        check_vma=False,
    )
```

```python
import functools

import jax
import jax.numpy as jnp
from jax import lax
from jax.experimental import pallas as pl
from jax.experimental.pallas import tpu as pltpu
from jax.sharding import PartitionSpec as P

HD = 64
TEXT = 128
PATCH = 256
ROW = 1152
WIDTH = 1024
HALF = ROW // 2
QUERY_TILE = 576
BACK_TILE = 384
FF_BLOCK = 256
GATHER_ROWS = 16
REDUCE_ROWS = 16

NORM_EPS = 1e-06
MASKED = -(2.0**30)
BETA_FIRST = 0.9
BETA_SECOND = 0.999
ADAM_EPS = 1e-08
MATRIX_RATE = 0.05
GAIN_RATE = 0.3
DECAY = 0.1
CLIP_LIMIT = 1.0
STEP_VALUE = 10.0
GELU_SCALE = 0.7978845608028654
GELU_CUBE = 0.044715

BF16 = jnp.bfloat16
F32 = jnp.float32
MESH = pl.DeviceIdType.MESH
ANY = pl.BlockSpec(memory_space=pl.ANY)
VMEM_WHOLE = pl.BlockSpec(memory_space=pltpu.VMEM)
DMA = pltpu.SemaphoreType.DMA
VMEM_LIMIT = 62 * 2**20

NT = (((1,), (1,)), ((), ()))
TN = (((0,), (0,)), ((), ()))


def dot(left, right, dims=(((1,), (0,)), ((), ()))):
    return lax.dot_general(left, right, dims, preferred_element_type=F32)


class Place:
    def __init__(self):
        self.dp = lax.axis_index("dp")
        self.core = lax.axis_index("fsdp")
        self.z = self.dp // 4
        self.y = lax.rem(self.dp // 2, 2)
        self.x = lax.rem(self.dp, 2)
        flip_y = 1 - self.y
        flip_x = 1 - self.x
        is_zero = self.core == 0
        self.own = (self.y, self.x)
        self.first = (jnp.where(is_zero, self.y, flip_y), jnp.where(is_zero, flip_x, self.x))
        self.second = (jnp.where(is_zero, flip_y, self.y), jnp.where(is_zero, self.x, flip_x))
        self.across = (flip_y, flip_x)

    def at(self, z, spot):
        return (z * 4 + spot[0] * 2 + spot[1], self.core)

    def above(self, step):
        return self.at(lax.rem(self.z + step, 4), self.own)

    def to_first(self):
        return self.at(self.z, self.first)

    def to_second(self):
        return self.at(self.z, self.second)

    def sibling(self):
        return (self.dp, 1 - self.core)

    def in_plane(self, step):
        y, x, core = ((1 - a) if step & bit else a for a, bit in ((self.y, 4), (self.x, 2), (self.core, 1)))
        return (self.z * 4 + y * 2 + x, core)

    def greet(self, plane=False):
        barrier = pltpu.get_barrier_semaphore()
        peers = [self.above(1), self.above(2), self.above(3)]
        if plane:
            peers += [self.in_plane(step) for step in range(1, 8)]
        else:
            peers += [self.to_first(), self.to_second(), self.sibling()]
        for peer in peers:
            pl.semaphore_signal(barrier, inc=1, device_id=peer, device_id_type=MESH)
        pl.semaphore_wait(barrier, len(peers))


def remote(source, target, send_sem, recv_sem, device):
    return pltpu.make_async_remote_copy(
        src_ref=source,
        dst_ref=target,
        send_sem=send_sem,
        recv_sem=recv_sem,
        device_id=device,
        device_id_type=MESH,
    )


def cut(index, rows, most):
    pieces = -(-rows // most)
    step = -(-rows // (pieces * 16)) * 16
    return [(index, at, min(step, rows - at)) for at in range(0, rows, step)]


class Gather:
    def __init__(self, shards, swaps=(), most=GATHER_ROWS, lag=3):
        self.arrays = [*shards, *swaps]
        self.shards, self.swaps = len(shards), len(swaps)
        self.chunks = []
        for index, shard in enumerate(shards):
            self.chunks += cut(index, shard.shape[0], most * WIDTH // shard.shape[1])
        count = len(self.chunks)
        self.lags = [lag] * count
        self.ticks = max(k + 3 * g for k, g in enumerate(self.lags)) + 1
        self.in_specs = [VMEM_WHOLE] * len(self.arrays)
        self.out_shapes = [jax.ShapeDtypeStruct((4, 2, 2, 2) + a.shape, a.dtype) for a in shards]
        self.out_shapes += [jax.ShapeDtypeStruct(a.shape, a.dtype) for a in swaps]
        self.out_specs = [ANY] * len(self.arrays)
        self.scratch = [
            DMA((count,)),
            DMA((count, 3)),
            DMA((count, 3)),
            DMA((count, 3)),
            DMA((count, 3)),
            DMA((count, 4)),
            DMA((count, 4)),
            DMA((max(self.swaps, 1),)),
            DMA((max(self.swaps, 1),)),
            DMA((max(self.swaps, 1),)),
        ]

    def bind(self, ins, outs, scratch):
        self.ins, self.outs = ins, outs
        (
            self.own_sem,
            self.z_send,
            self.z_recv,
            self.p_send,
            self.p_recv,
            self.c_send,
            self.c_recv,
            self.s_own,
            self.s_send,
            self.s_recv,
        ) = scratch
        self.claimed = set()
        self.here = Place()
        self.columns = (self.here.own, self.here.first, self.here.second, self.here.across)

    def spot(self, k, where):
        array, start, rows = self.chunks[k]
        return self.outs[array].at[:, where[0], where[1], self.here.core, pl.ds(start, rows), :]

    def mine(self, k):
        array, start, rows = self.chunks[k]
        here = self.here
        return (
            self.ins[array].at[pl.ds(start, rows), :],
            self.outs[array].at[here.z, here.y, here.x, here.core, pl.ds(start, rows), :],
        )

    def keep(self, k):
        source, target = self.mine(k)
        return pltpu.make_async_copy(source, target, self.own_sem.at[k])

    def along_z(self, k, step):
        source, target = self.mine(k)
        return remote(
            source,
            target,
            self.z_send.at[k, step - 1],
            self.z_recv.at[k, step - 1],
            self.here.above(step),
        )

    def plane(self, k, index):
        where = self.here.first if index == 2 else self.here.own
        device = self.here.to_first() if index == 0 else self.here.to_second()
        return remote(
            self.spot(k, where),
            self.spot(k, where),
            self.p_send.at[k, index],
            self.p_recv.at[k, index],
            device,
        )

    def to_sibling(self, k, index):
        where = self.columns[index]
        return remote(
            self.spot(k, where),
            self.spot(k, where),
            self.c_send.at[k, index],
            self.c_recv.at[k, index],
            self.here.sibling(),
        )

    def swap(self, index):
        source = self.ins[self.shards + index]
        target = self.outs[self.shards + index]
        core = self.here.core
        return (
            pltpu.make_async_copy(source.at[core], target.at[core], self.s_own.at[index]),
            remote(
                source.at[1 - core],
                target.at[core],
                self.s_send.at[index],
                self.s_recv.at[index],
                self.here.sibling(),
            ),
        )

    def tick(self, tick):
        for leg in (0, 3, 2, 1):
            for k in range(len(self.chunks)):
                if k + leg * self.lags[k] == tick:
                    self.leg(k, leg)
        if tick == self.ticks // 2:
            for index in range(self.swaps):
                for copy in self.swap(index):
                    copy.start()

    def leg(self, k, leg):
        if leg == 0:
            self.keep(k).start()
            for step in (2, 1, 3):
                self.along_z(k, step).start()
        elif leg == 1:
            self.keep(k).wait()
            for step in (1, 2, 3):
                self.along_z(k, step).wait_recv()
            self.plane(k, 1).start()
            self.plane(k, 0).start()
            self.to_sibling(k, 0).start()
        elif leg == 2:
            self.plane(k, 0).wait_recv()
            self.plane(k, 2).start()
            self.to_sibling(k, 1).start()
            self.plane(k, 1).wait_recv()
            self.to_sibling(k, 2).start()
        else:
            self.plane(k, 2).wait_recv()
            self.to_sibling(k, 3).start()

    def arrived(self, k):
        self.claimed.add(k)
        for index in range(4):
            self.to_sibling(k, index).wait_recv()

    def finish(self):
        for k in range(len(self.chunks)):
            for step in (1, 2, 3):
                self.along_z(k, step).wait_send()
            for index in range(3):
                self.plane(k, index).wait_send()
            for index in range(4):
                self.to_sibling(k, index).wait_send()
                if k not in self.claimed:
                    self.to_sibling(k, index).wait_recv()
        for index in range(self.swaps):
            for copy in self.swap(index):
                copy.wait()


class Reduce:
    def __init__(self, gradients, inside=(), swaps=(), most=REDUCE_ROWS, lag=2, starts=None, lags=None):
        self.arrays = [*gradients, *swaps]
        self.outside, self.inside, self.swaps = len(gradients), list(inside), len(swaps)
        self.chunks = []
        for index, gradient in enumerate(gradients):
            self.chunks += cut(index, gradient.shape[4], most)
        shapes = [g.shape[4:] for g in gradients] + self.inside
        for index, shape in enumerate(self.inside):
            self.chunks += cut(self.outside + index, shape[0], most * WIDTH // shape[1])
        count = len(self.chunks)
        self.starts = starts or list(range(count))
        self.lags = lags or [lag] * count
        self.ticks = max(s + 4 * g for s, g in zip(self.starts, self.lags)) + 1
        padded = [(-(-s[0] // 16) * 16, s[1]) for s in shapes]
        self.total_count = len(shapes)
        self.in_specs = [ANY] * len(self.arrays)
        self.out_shapes = [jax.ShapeDtypeStruct(s, F32) for s in shapes]
        self.out_shapes += [jax.ShapeDtypeStruct(a.shape[1:], a.dtype) for a in swaps]
        self.out_specs = [VMEM_WHOLE] * len(shapes) + [ANY] * len(swaps)
        self.scratch = [pltpu.VMEM((4, 2, 2) + s, BF16) for s in padded[: self.outside]]
        self.scratch += [pltpu.VMEM((4, 2, 2, 2) + s, BF16) for s in self.inside]
        for lead in ((4, 2, 2), (2, 4), (4,), (3,)):
            self.scratch += [pltpu.VMEM(lead + s, BF16) for s in padded]
        self.scratch += [
            DMA((count,)),
            DMA((count,)),
            DMA((count,)),
            DMA((count, 3)),
            DMA((count, 3)),
            DMA((count, 3)),
            DMA((count, 3)),
            DMA((max(self.swaps, 1),)),
            DMA((max(self.swaps, 1),)),
        ]

    def bind(self, ins, outs, scratch):
        n = self.total_count
        self.ins, self.outs = ins, outs
        self.own = scratch[:n]
        self.from_core, self.from_second, self.from_first, self.from_z = (
            scratch[i * n : (i + 1) * n] for i in range(1, 5)
        )
        (
            self.own_sem,
            self.c_send,
            self.c_recv,
            self.p_send,
            self.p_recv,
            self.z_send,
            self.z_recv,
            self.s_send,
            self.s_recv,
        ) = scratch[5 * n :]
        self.here = Place()

    def part(self, k):
        array, start, rows = self.chunks[k]
        return array, pl.ds(start, rows)

    def own_at(self, k, z, y, x):
        array, rows = self.part(k)
        if array < self.outside:
            return self.own[array].at[z, y, x, rows, :]
        return self.own[array].at[z, y, x, self.here.core, rows, :]

    def load(self, k):
        array, rows = self.part(k)
        return pltpu.make_async_copy(
            self.ins[array].at[:, :, :, self.here.core, rows, :],
            self.own[array].at[:, :, :, rows, :],
            self.own_sem.at[k],
        )

    def swap_core(self, k):
        array, rows = self.part(k)
        source = self.ins[array] if array < self.outside else self.own[array]
        return remote(
            source.at[:, :, :, 1 - self.here.core, rows, :],
            self.from_core[array].at[:, :, :, rows, :],
            self.c_send.at[k],
            self.c_recv.at[k],
            self.here.sibling(),
        )

    def send_second(self, k, index):
        array, rows = self.part(k)
        where = self.here.second if index == 0 else self.here.across
        return remote(
            self.own_at(k, slice(None), *where),
            self.from_second[array].at[index, :, rows, :],
            self.p_send.at[k, index],
            self.p_recv.at[k, index],
            self.here.to_second(),
        )

    def send_first(self, k):
        array, rows = self.part(k)
        return remote(
            self.own_at(k, slice(None), *self.here.first),
            self.from_first[array].at[:, rows, :],
            self.p_send.at[k, 2],
            self.p_recv.at[k, 2],
            self.here.to_first(),
        )

    def send_z(self, k, step):
        array, rows = self.part(k)
        here = self.here
        return remote(
            self.own_at(k, lax.rem(here.z + step, 4), *here.own),
            self.from_z[array].at[step - 1, rows, :],
            self.z_send.at[k, step - 1],
            self.z_recv.at[k, step - 1],
            here.above(step),
        )

    def swap(self, index):
        source = self.ins[self.outside + index]
        return remote(
            source.at[1 - self.here.core],
            self.outs[self.total_count + index],
            self.s_send.at[index],
            self.s_recv.at[index],
            self.here.sibling(),
        )

    def add_all(self, k):
        array, rows = self.part(k)
        other = self.from_core[array]

        def body(i, carry):
            z, y, x = i // 4, lax.rem(i // 2, 2), lax.rem(i, 2)
            own = self.own_at(k, z, y, x)
            own[...] = both_sum(own[...], other[z, y, x, rows, :])
            return carry

        lax.fori_loop(0, 16, body, 0)

    def add_column(self, k, where, other):
        rows = self.part(k)[1]

        def body(z, carry):
            own = self.own_at(k, z, *where)
            own[...] = both_sum(own[...], other[z, rows, :])
            return carry

        lax.fori_loop(0, 4, body, 0)

    def total(self, k):
        array, rows = self.part(k)
        total = self.own_at(k, self.here.z, *self.here.own)[...].astype(F32)
        for step in range(3):
            total = total + self.from_z[array][step, rows, :].astype(F32)
        self.outs[array][rows, :] = total

    def tick(self, tick):
        if tick == 1:
            for index in range(self.swaps):
                self.swap(index).start()
        for leg in (0, 4, 3, 2, 1):
            for k in range(len(self.chunks)):
                if self.starts[k] + leg * self.lags[k] == tick:
                    self.leg(k, leg)

    def leg(self, k, leg):
        array = self.chunks[k][0]
        if leg == 0:
            self.swap_core(k).start()
            if array < self.outside:
                self.load(k).start()
        elif leg == 1:
            if array < self.outside:
                self.load(k).wait()
            self.swap_core(k).wait_recv()
            self.add_all(k)
            for index in (1, 0):
                self.send_second(k, index).start()
        elif leg == 2:
            self.send_second(k, 1).wait_recv()
            self.add_column(k, self.here.first, self.from_second[array].at[1])
            self.send_first(k).start()
            self.send_second(k, 0).wait_recv()
            self.add_column(k, self.here.own, self.from_second[array].at[0])
        elif leg == 3:
            self.send_first(k).wait_recv()
            self.add_column(k, self.here.own, self.from_first[array])
            for step in (2, 1, 3):
                self.send_z(k, step).start()
        else:
            for step in (1, 2, 3):
                self.send_z(k, step).wait_recv()
            self.total(k)

    def finish(self):
        for k in range(len(self.chunks)):
            self.swap_core(k).wait_send()
            for index in (1, 0):
                self.send_second(k, index).wait_send()
            self.send_first(k).wait_send()
            for step in (1, 2, 3):
                self.send_z(k, step).wait_send()
        for index in range(self.swaps):
            self.swap(index).wait()


def both_sum(mine, other):
    return mine + other


def everywhere(here, buffer, value, send, recv):
    me = here.y * 4 + here.x * 2 + here.core
    for base, slot, count, peer in (
        (0, me, 8, here.in_plane),
        (8, here.z, 4, here.above),
    ):
        buffer[base + slot] = value
        copies = [
            remote(
                buffer.at[base + slot],
                buffer.at[base + slot],
                send.at[base + step],
                recv.at[base + step],
                peer(step),
            )
            for step in range(1, count)
        ]
        for copy in copies:
            copy.start()
        for copy in copies:
            copy.wait()
        value = buffer[base]
        for index in range(1, count):
            value = value + buffer[base + index]
    return value


def call(name, body, grid, inner, ins, in_specs, out_shapes, out_specs, scratch=(), comm=None, key=0, plan=None):
    params = {"vmem_limit_bytes": VMEM_LIMIT}
    if comm is None:

        def kernel(*refs):
            body(lambda point: None, *refs)

        extra = ([], [], [], [], [])
    else:
        params.update(collective_id=key, has_side_effects=True)
        extra = (comm.arrays, comm.in_specs, comm.out_shapes, comm.out_specs, comm.scratch)
        sizes = (len(ins), len(extra[0]), len(out_shapes), len(extra[2]), len(scratch), len(extra[4]))

        def kernel(*refs):
            parts, at = [], 0
            for size in sizes:
                parts.append(refs[at : at + size])
                at += size
            comm.bind(parts[1], parts[3], parts[5])
            step = pl.program_id(0)

            def pump(point):
                for tick in range(comm.ticks):
                    slot = plan[tick] if plan else tick * grid * inner // comm.ticks
                    if slot % inner == point:

                        @pl.when(step == slot // inner)
                        def _(tick=tick):
                            if tick == 0:
                                comm.here.greet()
                            comm.tick(tick)

            body(pump, *parts[0], *parts[2], *parts[4])

            @pl.when(step == grid - 1)
            def _():
                comm.finish()

    results = pl.pallas_call(
        kernel,
        grid=(grid,),
        out_shape=[*out_shapes, *extra[2]],
        in_specs=[*in_specs, *extra[1]],
        out_specs=[*out_specs, *extra[3]],
        scratch_shapes=[*scratch, *extra[4]],
        compiler_params=pltpu.CompilerParams(**params),
        name=name,
    )(*ins, *extra[0])
    return results[: len(out_shapes)], results[len(out_shapes) :]


def settle(rows, gains, sums, key):
    def kernel(rows_ref, gains_ref, *refs):
        sums_refs = refs[: len(sums)]
        got_ref, gains_out, square_out, buffer, send, recv, s_send, s_recv = refs[len(sums) :]
        here = Place()
        here.greet(plane=True)
        swap = remote(rows_ref.at[1 - here.core], got_ref, s_send, s_recv, here.sibling())
        swap.start()
        squares = jnp.zeros((8, 128), F32)
        for ref in sums_refs:
            values = ref[...]
            squares = squares + jnp.sum((values * values).reshape(-1, 8, 128), axis=0)
        total = everywhere(
            here, buffer, jnp.concatenate([gains_ref[...], squares], axis=0), send, recv
        )
        gains_total = total[:16]
        gains_out[...] = gains_total
        square_out[...] = jnp.broadcast_to(
            jnp.sum(total[16:]) + jnp.sum(gains_total * gains_total), (8, 128)
        )
        swap.wait()

    return pl.pallas_call(
        kernel,
        out_shape=[
            jax.ShapeDtypeStruct(rows.shape[1:], F32),
            jax.ShapeDtypeStruct((16, 128), F32),
            jax.ShapeDtypeStruct((8, 128), F32),
        ],
        in_specs=[ANY, VMEM_WHOLE] + [VMEM_WHOLE] * len(sums),
        out_specs=[ANY, VMEM_WHOLE, VMEM_WHOLE],
        scratch_shapes=[pltpu.VMEM((12, 24, 128), F32), DMA((12,)), DMA((12,)), DMA, DMA],
        compiler_params=pltpu.CompilerParams(
            collective_id=key, has_side_effects=True, vmem_limit_bytes=VMEM_LIMIT
        ),
        name="settle",
    )(rows, gains, *sums)


def segment_lanes(counts):
    sizes = [jnp.where(counts[i] > 0, TEXT + PATCH * counts[i], 0) for i in range(3)]
    ends = (sizes[0], sizes[0] + sizes[1], sizes[0] + sizes[1] + sizes[2])
    places = jnp.arange(ROW, dtype=jnp.int32)[:, None]
    segment = sum((places >= end).astype(jnp.int32) for end in ends)
    lane = jnp.arange(2 * HD, dtype=jnp.int32)[None, :] % HD
    same = lane == segment
    queries = jnp.where((lane < 4) & ~same, MASKED, 0.0).astype(BF16)
    return queries, jnp.where(same, 1.0, 0.0).astype(BF16)


def lanes_of_heads():
    lane = lax.broadcasted_iota(jnp.int32, (1, 2 * HD), 1)
    return lane, (lane < HD, lane >= HD)


def attend_tiles(pump, pair, q_ref, k_ref, v_ref, mq_ref, mk_ref, o_ref, log_ref):
    lane, in_head = lanes_of_heads()
    key = jnp.concatenate([k_ref[...], mk_ref[...]], axis=1)
    value = v_ref[...]
    values = [jnp.where(mine, value, jnp.ones_like(value)) for mine in in_head]
    for index in range(ROW // QUERY_TILE):
        pump(index)
        rows = pl.ds(index * QUERY_TILE, QUERY_TILE)
        query, extra = q_ref[rows, :], mq_ref[rows, :]
        mixed = []
        logs = log_ref[rows, :]
        for head in range(2):
            masked = jnp.where(in_head[head], query, jnp.zeros_like(query))
            scores = dot(jnp.concatenate([masked, extra], axis=1), key, NT)
            top = jnp.max(scores, axis=-1, keepdims=True)
            weight = jnp.exp(scores - top).astype(BF16)
            both = dot(weight, values[head])
            other = pltpu.roll(both, HD, 1)
            mixed.append(both / other)
            total = jnp.where(in_head[head], other, both)
            logs = jnp.where(lane == 2 * pair + head, top + jnp.log(total), logs)
        log_ref[rows, :] = logs
        o_ref[rows, :] = jnp.where(in_head[0], mixed[0], mixed[1]).astype(BF16)


def attend_body(pump, q_ref, k_ref, v_ref, mq_ref, mk_ref, o_ref, log_ref):
    pair = pl.program_id(0)

    @pl.when(pair == 0)
    def _():
        log_ref[...] = jnp.zeros_like(log_ref)

    attend_tiles(
        pump, pair, q_ref.at[0], k_ref.at[0], v_ref.at[0], mq_ref, mk_ref, o_ref, log_ref
    )


PAIRS = WIDTH // (2 * HD)


def third(which):
    return pl.BlockSpec((1, ROW, 2 * HD), lambda p: (which, 0, p))


def attend(projected, extras):
    whole = pl.BlockSpec((ROW, 128), lambda p: (0, 0))
    return call(
        "attend",
        attend_body,
        PAIRS,
        ROW // QUERY_TILE,
        [projected, projected, projected, *extras],
        [third(0), third(1), third(2), whole, whole],
        [jax.ShapeDtypeStruct((ROW, WIDTH), BF16), jax.ShapeDtypeStruct((ROW, 128), F32)],
        [pl.BlockSpec((ROW, 2 * HD), lambda p: (0, p)), whole],
    )


def attend_back_tiles(
    pump, pair, q_ref, k_ref, v_ref, mq_ref, mk_ref, o_ref, do_ref, log_ref, dq_ref, dk, dv
):
    _, in_head = lanes_of_heads()
    pick = jnp.where(
        (lax.broadcasted_iota(jnp.int32, (8, 2 * HD), 1) < HD)
        == (lax.broadcasted_iota(jnp.int32, (8, 2 * HD), 0) == 0),
        jnp.ones((8, 2 * HD), F32),
        jnp.zeros((8, 2 * HD), F32),
    )

    def only(values, head):
        return jnp.where(in_head[head], values, jnp.zeros_like(values))

    dk[...] = jnp.zeros_like(dk)
    dv[...] = jnp.zeros_like(dv)
    for index in range(ROW // BACK_TILE):
        pump(index)
        rows = pl.ds(index * BACK_TILE, BACK_TILE)
        query, grad, extra = q_ref[rows, :], do_ref[rows, :], mq_ref[rows, :]
        key, value = k_ref[...], v_ref[...]
        inner = lax.dot_general(
            pick,
            grad.astype(F32) * o_ref[rows, :].astype(F32),
            NT,
            precision=lax.Precision.HIGHEST,
            preferred_element_type=F32,
        )
        dq = None
        for head in range(2):
            log_total = log_ref[
                pl.ds(2 * pair + head, 1), index * BACK_TILE : (index + 1) * BACK_TILE
            ]
            scores = dot(
                jnp.where(in_head[head], key, mk_ref[...]),
                jnp.where(in_head[head], query, extra),
                NT,
            )
            weight = jnp.exp(scores - log_total)
            down = dot(only(value, head), grad, NT)
            slope = (weight * (down - inner[head : head + 1, :])).astype(BF16)
            dv[...] += dot(weight.astype(BF16), only(grad, head))
            dk[...] += dot(slope, only(query, head))
            step = dot(slope, only(key, head), TN)
            dq = step if dq is None else dq + step
        dq_ref[rows, :] = dq.astype(BF16)


def attend_back_body(
    pump, q_ref, k_ref, v_ref, mq_ref, mk_ref, o_ref, do_ref, log_ref, out_ref, dk, dv
):
    attend_back_tiles(
        pump, pl.program_id(0), q_ref.at[0], k_ref.at[0], v_ref.at[0], mq_ref, mk_ref, o_ref,
        do_ref, log_ref, out_ref.at[0], dk, dv,
    )
    out_ref[1] = dk[...].astype(BF16)
    out_ref[2] = dv[...].astype(BF16)


def attend_back(projected, extras, mixed, grad_mixed, log_rows):
    whole = pl.BlockSpec((ROW, 128), lambda p: (0, 0))
    column = pl.BlockSpec((ROW, 2 * HD), lambda p: (0, p))
    return call(
        "attend_back",
        attend_back_body,
        PAIRS,
        ROW // BACK_TILE,
        [projected, projected, projected, *extras, mixed, grad_mixed, log_rows],
        [third(0), third(1), third(2), whole, whole, column, column]
        + [pl.BlockSpec((2 * PAIRS, ROW), lambda p: (0, 0))],
        [jax.ShapeDtypeStruct((3, ROW, WIDTH), BF16)],
        [pl.BlockSpec((3, ROW, 2 * HD), lambda p: (0, 0, p))],
        [pltpu.VMEM((ROW, 2 * HD), F32), pltpu.VMEM((ROW, 2 * HD), F32)],
    )


def feed_units(
    pump, n2_ref, cot_ref, widen_ref, narrow_ref, widen_grad_ref, narrow_grad_ref, units
):
    pump(0)
    n2, cot = n2_ref[...], cot_ref[...]
    gate = dot(n2, widen_ref[0], NT)
    up = dot(n2, widen_ref[1], NT)
    down = dot(cot, narrow_ref[...], NT)
    square = gate * gate
    bend = jnp.tanh(gate * (GELU_SCALE + (GELU_SCALE * GELU_CUBE) * square))
    half = 0.5 + 0.5 * bend
    curve = gate * half
    slope = half + 0.5 * gate * (1.0 - bend * bend) * (
        GELU_SCALE + (3.0 * GELU_SCALE * GELU_CUBE) * square
    )
    units[0] = (curve * up).astype(BF16)
    units[1] = (down * up * slope).astype(BF16)
    units[2] = (down * curve).astype(BF16)
    pump(1)
    narrow_grad_ref[...] = dot(units[0], cot, TN).astype(BF16)
    widen_grad_ref[0] = dot(units[1], n2, TN).astype(BF16)
    widen_grad_ref[1] = dot(units[2], n2, TN).astype(BF16)
    pump(2)
    return (
        lambda: dot(units[0], narrow_ref[...]),
        lambda: dot(units[1], widen_ref[0]) + dot(units[2], widen_ref[1]),
    )


def feed_start_body(
    pump, n2_ref, cot_ref, widen_ref, narrow_ref,
    result_ref, back_ref, widen_grad_ref, narrow_grad_ref, units,
):
    result, back = feed_units(
        pump, n2_ref, cot_ref, widen_ref, narrow_ref, widen_grad_ref, narrow_grad_ref, units
    )

    @pl.when(pl.program_id(0) == 0)
    def _():
        result_ref[...] = jnp.zeros_like(result_ref)
        back_ref[...] = jnp.zeros_like(back_ref)

    result_ref[...] += result()
    back_ref[...] += back()


def feed_end_body(
    pump, n2_ref, cot_ref, h1_ref, gain_ref, result_part, back_part, widen_ref, narrow_ref,
    result_ref, dh1_ref, e_ref, gain_grad_ref, widen_grad_ref, narrow_grad_ref,
    units, back_ref, part_sem,
):
    step = pl.program_id(0)
    parts = (
        pltpu.make_async_copy(result_part, result_ref, part_sem.at[0]),
        pltpu.make_async_copy(back_part, back_ref, part_sem.at[1]),
    )

    @pl.when(step == 0)
    def _():
        for part in parts:
            part.start()

    result, back = feed_units(
        pump, n2_ref, cot_ref, widen_ref, narrow_ref, widen_grad_ref, narrow_grad_ref, units
    )

    @pl.when(step == 0)
    def _():
        for part in parts:
            part.wait()

    result_ref[...] += result()
    back_ref[...] += back()

    @pl.when(step == pl.num_programs(0) - 1)
    def _():
        gain = gain_ref[...]

        def tile(i, total):
            rows = pl.ds(pl.multiple_of(i * 64, 64), 64)
            h1 = h1_ref[rows, :]
            grad = back_ref[rows, :]
            result_ref[rows, :] += h1
            scale = lax.rsqrt(jnp.mean(h1 * h1, axis=-1, keepdims=True) + NORM_EPS)
            lifted = gain * grad
            inner = jnp.mean(h1 * lifted, axis=-1, keepdims=True)
            dh1 = (
                cot_ref[rows, :].astype(F32)
                + scale * lifted
                - h1 * (scale * scale * scale * inner)
            )
            dh1_ref[rows, :] = dh1
            e_ref[rows, :] = dh1.astype(BF16)
            return total + jnp.sum((grad * h1 * scale).reshape(8, 8, WIDTH), axis=0)

        total = lax.fori_loop(0, ROW // 64, tile, jnp.zeros((8, WIDTH), F32))
        gain_grad_ref[...] = jnp.sum(total, axis=0, keepdims=True)


def whole_block(*shape):
    return pl.BlockSpec(shape, lambda j: (0,) * len(shape), pipeline_mode=pl.Buffered(1))


WIDE_BLOCK = pl.BlockSpec((2, FF_BLOCK, WIDTH), lambda j: (0, j, 0))
TALL_BLOCK = pl.BlockSpec((FF_BLOCK, WIDTH), lambda j: (j, 0))
ROW_F32 = jax.ShapeDtypeStruct((ROW, WIDTH), F32)
ROW_BF16 = jax.ShapeDtypeStruct((ROW, WIDTH), BF16)


def feed_start(n2, cot, widen, narrow, comm=None, key=0):
    rows = whole_block(ROW, WIDTH)
    return call(
        "feed_start",
        feed_start_body,
        narrow.shape[0] // FF_BLOCK,
        3,
        [n2, cot, widen, narrow],
        [rows, rows, WIDE_BLOCK, TALL_BLOCK],
        [
            ROW_F32,
            ROW_F32,
            jax.ShapeDtypeStruct(widen.shape, BF16),
            jax.ShapeDtypeStruct(narrow.shape, BF16),
        ],
        [rows, rows, WIDE_BLOCK, TALL_BLOCK],
        [pltpu.VMEM((3, ROW, FF_BLOCK), BF16)],
        comm=comm,
        key=key,
    )


def feed_end(n2, cot, h1, gain, result_part, back_part, widen, narrow, comm=None, key=0):
    rows = whole_block(ROW, WIDTH)
    line = whole_block(1, WIDTH)
    return call(
        "feed_end",
        feed_end_body,
        narrow.shape[0] // FF_BLOCK,
        3,
        [n2, cot, h1, gain, result_part, back_part, widen, narrow],
        [rows, rows, rows, line, ANY, ANY, WIDE_BLOCK, TALL_BLOCK],
        [
            ROW_F32,
            ROW_F32,
            ROW_BF16,
            jax.ShapeDtypeStruct((1, WIDTH), F32),
            jax.ShapeDtypeStruct(widen.shape, BF16),
            jax.ShapeDtypeStruct(narrow.shape, BF16),
        ],
        [rows, rows, rows, line, WIDE_BLOCK, TALL_BLOCK],
        [pltpu.VMEM((3, ROW, FF_BLOCK), BF16), pltpu.VMEM((ROW, WIDTH), F32), DMA((2,))],
        comm=comm,
        key=key,
    )


def front(attention_shard, gains_tile, feed_shards, tokens, cotangent, extras, key):
    comm = Gather((gains_tile, attention_shard, *feed_shards), (cotangent,), most=16, lag=2)
    points = [0] * 7 + [1] * 2
    rest = comm.ticks - len(points)
    points += [2 + tick * (5 * PAIRS - 2) // rest for tick in range(rest)]

    def body(
        pump, tokens_ref, mq_ref, mk_ref,
        turned_ref, row_ref, qkv_ref, o_ref, o_turned_ref, log_ref, h1_ref, n2_ref,
        normed, landed, parts, out_weights, o_all, gains, t_send, t_recv, part_sem, gains_sem,
    ):
        pair = pl.program_id(0)
        here = comm.here
        core = here.core
        across = remote(tokens_ref.at[1 - core], landed, t_send, t_recv, here.sibling())

        def fetch(p, slot):
            return pltpu.make_async_copy(
                comm.outs[1].at[:, :, :, :, pl.ds(128 * p, 128), :], parts.at[slot], part_sem.at[slot]
            )

        pump(0)

        @pl.when(pair == 0)
        def _():
            across.start()
            log_ref[...] = jnp.zeros_like(log_ref)
            row_ref[core] = tokens_ref[core]
            across.wait_recv()
            row_ref[1 - core] = landed[...]
            comm.arrived(0)
            copy = pltpu.make_async_copy(comm.outs[0], gains, gains_sem)
            copy.start()
            copy.wait()

        def gain_of(which):
            tiles = [
                gains[which * 2 + z, y, x, 0, 0:1, :] + gains[which * 2 + z, y, x, 1, 0:1, :]
                for z in range(2)
                for y in range(2)
                for x in range(2)
            ]
            return jnp.concatenate(tiles, axis=1).astype(F32)

        @pl.when(pair == 0)
        def _():
            gain = gain_of(0)
            for half in range(2):

                def tile(i, carry, half=half):
                    rows = pl.ds(pl.multiple_of(i * 64, 64), 64)
                    x = row_ref[half, rows, :].astype(F32)
                    scale = lax.rsqrt(jnp.mean(x * x, axis=-1, keepdims=True) + NORM_EPS)
                    normed[pl.ds(pl.multiple_of(half * HALF + i * 64, 64), 64), :] = (
                        x * scale * gain
                    ).astype(BF16)
                    return carry

                lax.fori_loop(0, HALF // 64, tile, 0)
            turned_ref[...] = normed[...].T

        pump(1)

        @pl.when(pair == 0)
        def _():
            comm.arrived(1)
            fetch(0, 0).start()

        slot = lax.rem(pair, 2)
        fetch(pair, slot).wait()
        weights = parts[slot].reshape(4, WIDTH, 128)
        three = dot(normed[...], jnp.concatenate([weights[0], weights[1], weights[2]], axis=1))
        for index in range(3):
            qkv_ref[index] = three[:, 128 * index : 128 * (index + 1)].astype(BF16)
        out_weights[pair] = weights[3]
        pump(2)
        for p in range(1, PAIRS):

            @pl.when(pair == p - 1)
            def _(p=p):
                comm.arrived(1 + p)
                fetch(p, p % 2).start()

        attend_tiles(
            lambda index: pump(3 + index),
            pair,
            qkv_ref.at[0],
            qkv_ref.at[1],
            qkv_ref.at[2],
            mq_ref,
            mk_ref,
            o_ref,
            log_ref,
        )
        mixed = o_ref[...]
        o_all[:, pl.ds(pl.multiple_of(pair * 128, 128), 128)] = mixed
        o_turned_ref[...] = mixed.T

        @pl.when(pair == PAIRS - 1)
        def _():
            across.wait_send()
            full = jnp.concatenate([out_weights[p] for p in range(PAIRS)], axis=1)
            gain = gain_of(1)
            h1_ref[...] = dot(o_all[...], full)
            for half in range(2):

                def tile(i, carry, half=half):
                    near = pl.ds(pl.multiple_of(i * 64, 64), 64)
                    rows = pl.ds(pl.multiple_of(half * HALF + i * 64, 64), 64)
                    h1 = row_ref[half, near, :].astype(F32) + h1_ref[rows, :]
                    h1_ref[rows, :] = h1
                    scale = lax.rsqrt(jnp.mean(h1 * h1, axis=-1, keepdims=True) + NORM_EPS)
                    n2_ref[rows, :] = (h1 * scale * gain).astype(BF16)
                    return carry

                lax.fori_loop(0, HALF // 64, tile, 0)

    whole = pl.BlockSpec((ROW, 128), lambda p: (0, 0))
    turned = jax.ShapeDtypeStruct((WIDTH, ROW), BF16)
    return call(
        "front",
        body,
        PAIRS,
        5,
        [tokens, *extras],
        [VMEM_WHOLE, whole, whole],
        [
            turned,
            jax.ShapeDtypeStruct((2, HALF, WIDTH), BF16),
            jax.ShapeDtypeStruct((3, ROW, WIDTH), BF16),
            ROW_BF16,
            turned,
            jax.ShapeDtypeStruct((ROW, 128), F32),
            ROW_F32,
            ROW_BF16,
        ],
        [
            whole_block(WIDTH, ROW),
            whole_block(2, HALF, WIDTH),
            pl.BlockSpec((3, ROW, 128), lambda p: (0, 0, p)),
            pl.BlockSpec((ROW, 128), lambda p: (0, p)),
            pl.BlockSpec((128, ROW), lambda p: (p, 0)),
            whole,
            whole_block(ROW, WIDTH),
            whole_block(ROW, WIDTH),
        ],
        [
            pltpu.VMEM((ROW, WIDTH), BF16),
            pltpu.VMEM((HALF, WIDTH), BF16),
            pltpu.VMEM((2, 4, 2, 2, 2, 128, 128), BF16),
            pltpu.VMEM((PAIRS, WIDTH, 128), BF16),
            pltpu.VMEM((ROW, WIDTH), BF16),
            pltpu.VMEM((4, 2, 2, 2, 16, 128), BF16),
            DMA,
            DMA,
            DMA((2,)),
            DMA,
        ],
        comm,
        key,
        points,
    )


PART = 96


def back(
    gradients, result, e, dh1, tokens_row, gain, projected, extras, mixed, log_rows,
    attention_parts, normed_turned, mixed_turned, key,
):
    starts = [0, 2, 4, 6, 8, 11, 13, 16] + [9, 9, 19, 19, 29, 29, 34, 39]
    lags = [3] * 14 + [2, 1]
    comm = Reduce(
        gradients, [(PAIRS * 128, 128)], (result,), most=16, starts=starts, lags=lags
    )
    inner, made, after, middle, rest = 8, 4, 5, 6, 7
    plan = [tick // 5 * inner + tick % 5 for tick in range(5 * PAIRS)]
    plan += [(PAIRS - 1) * inner + point for point in (after, middle, rest, rest)]

    def body(
        pump, q_ref, k_ref, v_ref, mq_ref, mk_ref, o_ref, log_ref, parts_ref, rows_ref,
        e_ref, n_turned_ref, o_turned_ref, gain_ref, tokens_ref, dh1_ref,
        da_ref, gain_grad_ref,
        do, three, dk, dv, x_part, dh1_part, x_sem, dh1_sem,
    ):
        pair = pl.program_id(0)
        odd = lax.rem(pair, 2)
        pump(0)

        @pl.when(odd == 0)
        def _():
            rows = [
                jnp.concatenate(
                    [rows_ref[0, 0, 0, c, 128 * p : 128 * (p + 1), :] for p in range(PAIRS)], axis=1
                )
                for c in range(2)
            ]
            two = dot(e_ref[...], jnp.concatenate(rows, axis=0), NT).astype(BF16)
            do[0] = two[:, :128]
            do[1] = two[:, 128:]

        attend_back_tiles(
            lambda index: pump(1 + index), pair, q_ref.at[0], k_ref.at[0], v_ref.at[0],
            mq_ref, mk_ref, o_ref, do.at[odd], log_ref, three.at[odd, :, 0:128], dk, dv,
        )
        three[odd, :, 128:256] = dk[...].astype(BF16)
        three[odd, :, 256:384] = dv[...].astype(BF16)
        made_ref = comm.own[comm.outside]
        late = pair >= PAIRS - 2
        cases = (
            ((odd == 1) & jnp.logical_not(late), (0, 1)),
            ((odd == 0) & late, (0,)),
            ((odd == 1) & late, (1,)),
        )

        def joined(halves):
            return jnp.concatenate([three[half] for half in halves], axis=1)

        def make(halves):
            first = pair - odd + halves[0]
            grads = dot(n_turned_ref[...], joined(halves)).astype(BF16)
            columns = pl.ds(pl.multiple_of(first * 128, 128), 128 * len(halves))
            out_grads = dot(o_turned_ref[...], e_ref[:, columns]).astype(BF16)
            for place in range(len(halves)):
                mine = pl.ds(pl.multiple_of((first + place) * 128, 128), 128)
                for index in range(3):
                    at = 384 * place + 128 * index
                    made_ref[index, :, :, :, mine, :] = grads[:, at : at + 128].reshape(
                        2, 2, 2, 128, 128
                    )
                made_ref[3, :, :, :, mine, :] = out_grads[
                    :, 128 * place : 128 * (place + 1)
                ].reshape(2, 2, 2, 128, 128)

        def down(halves):
            columns = jnp.concatenate(
                [
                    parts_ref[index, :, :, :, 128 * half : 128 * (half + 1), :].reshape(WIDTH, 128)
                    for half in halves
                    for index in range(3)
                ],
                axis=1,
            )
            da_ref[...] += dot(joined(halves), columns, NT)

        @pl.when(pair == 0)
        def _():
            da_ref[...] = jnp.zeros_like(da_ref)

        for case, halves in cases:

            @pl.when(case)
            def _(halves=halves):
                make(halves)

        pump(made)
        for case, halves in cases:

            @pl.when(case)
            def _(halves=halves):
                down(halves)

        pump(after)

        @pl.when(pair == PAIRS - 1)
        def _():
            def fetch(i):
                rows = pl.ds(i * PART, PART)
                slot = i % 2
                return (
                    pltpu.make_async_copy(tokens_ref.at[rows, :], x_part.at[slot], x_sem.at[slot]),
                    pltpu.make_async_copy(dh1_ref.at[rows, :], dh1_part.at[slot], dh1_sem.at[slot]),
                )

            gain_row = gain_ref[...]
            total = jnp.zeros((8, WIDTH), F32)
            for copy in fetch(0):
                copy.start()
            for i in range(ROW // PART):
                if i == ROW // PART // 2:
                    pump(middle)
                if i + 1 < ROW // PART:
                    for copy in fetch(i + 1):
                        copy.start()
                for copy in fetch(i):
                    copy.wait()

                def tile(j, total, i=i):
                    near = pl.ds(pl.multiple_of(j * 48, 16), 48)
                    rows = pl.ds(pl.multiple_of(i * PART + j * 48, 16), 48)
                    x = x_part[i % 2, near, :].astype(F32)
                    grad = da_ref[rows, :]
                    scale = lax.rsqrt(jnp.mean(x * x, axis=-1, keepdims=True) + NORM_EPS)
                    lifted = gain_row * grad
                    middle = jnp.mean(x * lifted, axis=-1, keepdims=True)
                    da_ref[rows, :] = (
                        dh1_part[i % 2, near, :]
                        + scale * lifted
                        - x * (scale * scale * scale * middle)
                    )
                    return total + jnp.sum((grad * x * scale).reshape(6, 8, WIDTH), axis=0)

                total = lax.fori_loop(0, PART // 48, tile, total)
            gain_grad_ref[...] = jnp.sum(total, axis=0, keepdims=True)

        pump(rest)

    extra = pl.BlockSpec((ROW, 128), lambda p: (0, 0), pipeline_mode=pl.Buffered(1))
    line = whole_block(1, WIDTH)
    return call(
        "back",
        body,
        PAIRS,
        inner,
        [projected, projected, projected, *extras, mixed, log_rows, attention_parts, attention_parts]
        + [e, normed_turned, mixed_turned, gain, tokens_row, dh1],
        [third(0), third(1), third(2), extra, extra]
        + [
            pl.BlockSpec((ROW, 128), lambda p: (0, p)),
            whole_block(2 * PAIRS, ROW),
            pl.BlockSpec((3, 2, 2, 2, 256, 128), lambda p: (0, 0, 0, 0, p // 2, 0)),
            pl.BlockSpec(
                (1, 1, 1, 2, WIDTH, 128), lambda p: (3, p // 4, lax.rem(p // 2, 2), 0, 0, 0)
            ),
            whole_block(ROW, WIDTH),
            whole_block(WIDTH, ROW),
            whole_block(WIDTH, ROW),
            line,
            ANY,
            ANY,
        ],
        [ROW_F32, jax.ShapeDtypeStruct((1, WIDTH), F32)],
        [whole_block(ROW, WIDTH), line],
        [
            pltpu.VMEM((2, ROW, 128), BF16),
            pltpu.VMEM((2, ROW, 384), BF16),
            pltpu.VMEM((ROW, 128), F32),
            pltpu.VMEM((ROW, 128), F32),
            pltpu.VMEM((2, PART, WIDTH), BF16),
            pltpu.VMEM((2, PART, WIDTH), F32),
            DMA((2,)),
            DMA((2,)),
        ],
        comm,
        key,
        plan,
    )


def rms_scale(values, gain_vector):
    return (
        values
        * lax.rsqrt(jnp.mean(values * values, axis=-1, keepdims=True) + NORM_EPS)
        * gain_vector
    )


def adam_update(master, first, second, gradient, factors, rate, decay):
    clip_factor, first_fix, second_fix = factors
    clipped = clip_factor * gradient
    first_new = BETA_FIRST * first + (1.0 - BETA_FIRST) * clipped
    second_new = BETA_SECOND * second + (1.0 - BETA_SECOND) * clipped * clipped
    master_new = master - rate * (
        first_new / first_fix / (jnp.sqrt(second_new / second_fix) + ADAM_EPS) + decay * master
    )
    return (master_new, first_new, second_new)


def swap_halves(parts):
    core = lax.axis_index("fsdp")
    got = lax.ppermute(parts[1 - core], "fsdp", [(0, 1), (1, 0)])
    return jnp.where(core == 0, jnp.stack([parts[0], got]), jnp.stack([got, parts[1]]))


def with_half(rows, got):
    own = rows.reshape(2, HALF, WIDTH)
    first = lax.axis_index("fsdp") == 0
    return jnp.where(first, jnp.stack([own[0], got]), jnp.stack([got, own[1]]))


def local(
    own_kernels,
    tokens,
    cotangent,
    images,
    attention_weight,
    attention_first,
    attention_second,
    widen_weight,
    widen_first,
    widen_second,
    narrow_weight,
    narrow_first,
    narrow_second,
    norm_gains,
    gains_first,
    gains_second,
):
    axes = ("dp", "fsdp")
    devices = lax.axis_size(axes)
    core = lax.axis_index("fsdp")
    position = lax.axis_index(axes)
    gain_count = norm_gains.shape[0]
    units = narrow_weight.shape[0]
    split = units * 6 // 11
    attention_low = attention_weight.astype(BF16)
    widen_low = widen_weight.astype(BF16).T.reshape(2, units, WIDTH)
    narrow_low = narrow_weight.astype(BF16)
    gains_low = norm_gains.astype(BF16)
    feed_low = [
        (widen_low[:, :split].reshape(-1, WIDTH), narrow_low[:split]),
        (widen_low[:, split:].reshape(-1, WIDTH), narrow_low[split:]),
    ]
    grid = (4, 2, 2, 2)

    def fetch(shards):
        return [lax.all_gather(shard, axes, axis=0, tiled=True) for shard in shards]

    def summed(gradients):
        return [
            lax.psum_scatter(
                g.astype(F32).reshape(-1, 128), axes, scatter_dimension=0, tiled=True
            ).reshape(-1, WIDTH)
            for g in gradients
        ]

    def other_half(parts):
        return lax.ppermute(
            lax.dynamic_index_in_dim(parts, 1 - core, 0, keepdims=False), "fsdp", [(0, 1), (1, 0)]
        )

    def as_feed(shards):
        return shards[0].reshape(2, -1, WIDTH), shards[1].reshape(-1, WIDTH)

    def as_shards(*gradients):
        return [g.reshape(grid + (-1, WIDTH)) for g in gradients]

    counts = lax.dynamic_index_in_dim(images[:, 0, :], core, 0, keepdims=False)
    extras = segment_lanes(counts)
    gather_b = None
    if own_kernels:
        places = lax.broadcasted_iota(jnp.int32, (16, 2, gain_count), 0) * 2
        places = places + lax.broadcasted_iota(jnp.int32, (16, 2, gain_count), 1)
        gains_tile = jnp.where(places == core, gains_low, jnp.zeros_like(gains_low)).reshape(16, -1)
        columns = attention_low.reshape(-1, PAIRS, 2 * HD).transpose(1, 0, 2).reshape(-1, 2 * HD)
        (
            (normed_turned, tokens_row, projected, mixed, mixed_turned, log_columns, h1, n2),
            (gains_full, attention_parts, *feed_a, cotangent_row),
        ) = front(columns, gains_tile, feed_low[0], tokens, cotangent, extras, 0)
        gains_full = gains_full[:, :, :, :, 0, :].sum(axis=3).reshape(-1)
        gather_b = Gather(feed_low[1])
        cot = cotangent_row.reshape(ROW, WIDTH)
        inputs = tokens_row.reshape(ROW, WIDTH).astype(F32)
        first_gain = gains_full[:WIDTH].astype(F32)
        second_gain = gains_full[WIDTH:].astype(F32)
    else:
        attention_full, gains_full = fetch((attention_low, gains_low))
        first = core == 0
        tokens_row, cotangent_row = (
            jnp.where(first, jnp.stack([a[0], got]), jnp.stack([got, a[1]]))
            for a, got in ((a, other_half(a)) for a in (tokens, cotangent))
        )
        attention = attention_full.reshape(4, WIDTH, WIDTH)
        cot = cotangent_row.reshape(ROW, WIDTH)
        inputs = tokens_row.reshape(ROW, WIDTH).astype(F32)
        first_gain = gains_full[:WIDTH].astype(F32)
        second_gain = gains_full[WIDTH:].astype(F32)
        normed = rms_scale(inputs, first_gain).astype(BF16)
        projected = jnp.einsum(
            "sd,jde->jse", normed, attention[:3], preferred_element_type=F32
        ).astype(BF16)
        (mixed, log_columns), _ = attend(projected, extras)
        h1 = inputs + dot(mixed, attention[3])
        n2 = rms_scale(h1, second_gain).astype(BF16)
    log_rows = log_columns[:, : WIDTH // HD].T
    widen_a, narrow_a = as_feed(feed_a if own_kernels else fetch(feed_low[0]))
    (result_part, back_part, *grads_a), feed_b = feed_start(
        n2, cot, widen_a, narrow_a, gather_b, 2
    )
    widen_b, narrow_b = as_feed(feed_b if own_kernels else fetch(feed_low[1]))
    (result, dh1, e, grad_gain_two, *grads_b), sums_a = feed_end(
        n2,
        cot,
        h1,
        second_gain[None],
        result_part,
        back_part,
        widen_b,
        narrow_b,
        Reduce(as_shards(*grads_a)) if own_kernels else None,
        3,
    )
    if own_kernels:
        (input_rows, grad_gain_one), (*sums_b, attention_sum, got_result) = back(
            as_shards(*grads_b),
            result.reshape(2, HALF, WIDTH),
            e,
            dh1,
            tokens_row.reshape(ROW, WIDTH),
            first_gain[None],
            projected,
            extras,
            mixed,
            log_rows,
            attention_parts,
            normed_turned,
            mixed_turned,
            4,
        )
        got_input, gains_total, square_total = settle(
            input_rows.reshape(2, HALF, WIDTH),
            jnp.concatenate([grad_gain_one, grad_gain_two]).reshape(16, 128),
            [*sums_a, *sums_b, attention_sum],
            5,
        )
        attention_sum = (
            attention_sum.reshape(PAIRS, -1, 128).transpose(1, 0, 2).reshape(-1, WIDTH)
        )
        gains_sum = lax.dynamic_slice_in_dim(
            gains_total.reshape(-1), position * gain_count, gain_count
        )
        squares = square_total[0, 0]
    else:
        grad_out = dot(mixed, e, TN).astype(BF16)
        grad_mixed = dot(e, attention[3], NT).astype(BF16)
        (grad_projected,), _ = attend_back(projected, extras, mixed, grad_mixed, log_rows)
        grad_qkv = jnp.einsum(
            "sd,jse->jde", normed, grad_projected, preferred_element_type=F32
        ).astype(BF16)
        grad_normed = jnp.einsum(
            "jse,jde->sd", grad_projected, attention[:3], preferred_element_type=F32
        )
        scale = lax.rsqrt(jnp.mean(inputs * inputs, axis=-1, keepdims=True) + NORM_EPS)
        lifted = first_gain * grad_normed
        inner = jnp.mean(inputs * lifted, axis=-1, keepdims=True)
        input_rows = dh1 + scale * lifted - inputs * (scale * scale * scale * inner)
        grad_gain_one = jnp.sum(grad_normed * inputs * scale, axis=0)
        grad_attention = jnp.concatenate([grad_qkv, grad_out[None]], axis=0)
        grad_gains = jnp.concatenate([grad_gain_one, grad_gain_two[0]])
        sums_a, sums_b, (attention_sum,) = summed(grads_a), summed(grads_b), summed([grad_attention])
        gains_sum = lax.psum_scatter(grad_gains, axes, scatter_dimension=0, tiled=True)
        squares = lax.psum(
            sum(jnp.sum(g * g) for g in (*sums_a, *sums_b, attention_sum, gains_sum)), axes
        )
        got_result = other_half(result.reshape(2, HALF, WIDTH))
        got_input = other_half(input_rows.reshape(2, HALF, WIDTH))
    widen_sum = jnp.concatenate(
        [sums_a[0].reshape(2, -1, WIDTH), sums_b[0].reshape(2, -1, WIDTH)], axis=1
    ).reshape(-1, WIDTH)
    narrow_sum = jnp.concatenate([sums_a[1], sums_b[1]], axis=0)
    grad_norm = jnp.sqrt(squares)
    clip_factor = jnp.minimum(1.0, CLIP_LIMIT / (grad_norm + 1e-06))
    step_value = jnp.float32(STEP_VALUE)
    factors = (
        clip_factor,
        1.0 - jnp.power(jnp.float32(BETA_FIRST), step_value),
        1.0 - jnp.power(jnp.float32(BETA_SECOND), step_value),
    )
    return (
        with_half(result, got_result),
        with_half(input_rows, got_input),
        *adam_update(
            attention_weight,
            attention_first,
            attention_second,
            attention_sum,
            factors,
            MATRIX_RATE,
            DECAY,
        ),
        *adam_update(
            widen_weight, widen_first, widen_second, widen_sum.T, factors, MATRIX_RATE, DECAY
        ),
        *adam_update(
            narrow_weight, narrow_first, narrow_second, narrow_sum, factors, MATRIX_RATE, DECAY
        ),
        *adam_update(norm_gains, gains_first, gains_second, gains_sum, factors, GAIN_RATE, 0.0),
        grad_norm,
    )


def solution(mesh):
    both = ("dp", "fsdp")
    rows = P(None, both, None)
    tall = P(both, None)
    wide = P(None, both)
    flat = P(both)
    weights = (tall, tall, tall, wide, wide, wide, tall, tall, tall, flat, flat, flat)
    own_kernels = dict(mesh.shape) == {"dp": 16, "fsdp": 2}
    return jax.shard_map(
        functools.partial(local, own_kernels),
        mesh=mesh,
        in_specs=(rows, rows, P(None, "dp", None)) + weights,
        out_specs=(rows, rows) + weights + (P(),),
        check_vma=False,
    )
```

```python
import functools

import jax
import jax.numpy as jnp
from jax import lax
from jax.experimental import pallas as pl
from jax.experimental.pallas import tpu as pltpu
from jax.sharding import PartitionSpec as P

HD = 64
TEXT = 128
PATCH = 256
ROW = 1152
WIDTH = 1024
HALF = ROW // 2
QUERY_TILE = 576
BACK_TILE = 384
FF_BLOCK = 256
GATHER_ROWS = 16
REDUCE_ROWS = 16

NORM_EPS = 1e-06
MASKED = -(2.0**30)
BETA_FIRST = 0.9
BETA_SECOND = 0.999
ADAM_EPS = 1e-08
MATRIX_RATE = 0.05
GAIN_RATE = 0.3
DECAY = 0.1
CLIP_LIMIT = 1.0
STEP_VALUE = 10.0
GELU_SCALE = 0.7978845608028654
GELU_CUBE = 0.044715

BF16 = jnp.bfloat16
F32 = jnp.float32
MESH = pl.DeviceIdType.MESH
ANY = pl.BlockSpec(memory_space=pl.ANY)
VMEM_WHOLE = pl.BlockSpec(memory_space=pltpu.VMEM)
DMA = pltpu.SemaphoreType.DMA
VMEM_LIMIT = 62 * 2**20

NT = (((1,), (1,)), ((), ()))
TN = (((0,), (0,)), ((), ()))


def dot(left, right, dims=(((1,), (0,)), ((), ()))):
    return lax.dot_general(left, right, dims, preferred_element_type=F32)


class Place:
    def __init__(self):
        self.dp = lax.axis_index("dp")
        self.core = lax.axis_index("fsdp")
        self.z = self.dp // 4
        self.y = lax.rem(self.dp // 2, 2)
        self.x = lax.rem(self.dp, 2)
        flip_y = 1 - self.y
        flip_x = 1 - self.x
        is_zero = self.core == 0
        self.own = (self.y, self.x)
        self.first = (jnp.where(is_zero, self.y, flip_y), jnp.where(is_zero, flip_x, self.x))
        self.second = (jnp.where(is_zero, flip_y, self.y), jnp.where(is_zero, self.x, flip_x))
        self.across = (flip_y, flip_x)

    def at(self, z, spot):
        return (z * 4 + spot[0] * 2 + spot[1], self.core)

    def above(self, step):
        return self.at(lax.rem(self.z + step, 4), self.own)

    def to_first(self):
        return self.at(self.z, self.first)

    def to_second(self):
        return self.at(self.z, self.second)

    def sibling(self):
        return (self.dp, 1 - self.core)

    def in_plane(self, step):
        y, x, core = ((1 - a) if step & bit else a for a, bit in ((self.y, 4), (self.x, 2), (self.core, 1)))
        return (self.z * 4 + y * 2 + x, core)

    def greet(self, plane=False):
        barrier = pltpu.get_barrier_semaphore()
        peers = [self.above(1), self.above(2), self.above(3)]
        if plane:
            peers += [self.in_plane(step) for step in range(1, 8)]
        else:
            peers += [self.to_first(), self.to_second(), self.sibling()]
        for peer in peers:
            pl.semaphore_signal(barrier, inc=1, device_id=peer, device_id_type=MESH)
        pl.semaphore_wait(barrier, len(peers))


def remote(source, target, send_sem, recv_sem, device):
    return pltpu.make_async_remote_copy(
        src_ref=source,
        dst_ref=target,
        send_sem=send_sem,
        recv_sem=recv_sem,
        device_id=device,
        device_id_type=MESH,
    )


def cut(index, rows, most):
    pieces = -(-rows // most)
    step = -(-rows // (pieces * 16)) * 16
    return [(index, at, min(step, rows - at)) for at in range(0, rows, step)]


class Gather:
    def __init__(self, shards, swaps=(), most=GATHER_ROWS, lag=3):
        self.arrays = [*shards, *swaps]
        self.shards, self.swaps = len(shards), len(swaps)
        self.chunks = []
        for index, shard in enumerate(shards):
            self.chunks += cut(index, shard.shape[0], most * WIDTH // shard.shape[1])
        count = len(self.chunks)
        self.lags = [lag] * count
        self.ticks = max(k + 3 * g for k, g in enumerate(self.lags)) + 1
        self.in_specs = [VMEM_WHOLE] * len(self.arrays)
        self.out_shapes = [jax.ShapeDtypeStruct((4, 2, 2, 2) + a.shape, a.dtype) for a in shards]
        self.out_shapes += [jax.ShapeDtypeStruct(a.shape, a.dtype) for a in swaps]
        self.out_specs = [ANY] * len(self.arrays)
        self.scratch = [
            DMA((count,)),
            DMA((count, 3)),
            DMA((count, 3)),
            DMA((count, 3)),
            DMA((count, 3)),
            DMA((count, 4)),
            DMA((count, 4)),
            DMA((max(self.swaps, 1),)),
            DMA((max(self.swaps, 1),)),
            DMA((max(self.swaps, 1),)),
        ]

    def bind(self, ins, outs, scratch):
        self.ins, self.outs = ins, outs
        (
            self.own_sem,
            self.z_send,
            self.z_recv,
            self.p_send,
            self.p_recv,
            self.c_send,
            self.c_recv,
            self.s_own,
            self.s_send,
            self.s_recv,
        ) = scratch
        self.claimed = set()
        self.here = Place()
        self.columns = (self.here.own, self.here.first, self.here.second, self.here.across)

    def spot(self, k, where):
        array, start, rows = self.chunks[k]
        return self.outs[array].at[:, where[0], where[1], self.here.core, pl.ds(start, rows), :]

    def mine(self, k):
        array, start, rows = self.chunks[k]
        here = self.here
        return (
            self.ins[array].at[pl.ds(start, rows), :],
            self.outs[array].at[here.z, here.y, here.x, here.core, pl.ds(start, rows), :],
        )

    def keep(self, k):
        source, target = self.mine(k)
        return pltpu.make_async_copy(source, target, self.own_sem.at[k])

    def along_z(self, k, step):
        source, target = self.mine(k)
        return remote(
            source,
            target,
            self.z_send.at[k, step - 1],
            self.z_recv.at[k, step - 1],
            self.here.above(step),
        )

    def plane(self, k, index):
        where = self.here.first if index == 2 else self.here.own
        device = self.here.to_first() if index == 0 else self.here.to_second()
        return remote(
            self.spot(k, where),
            self.spot(k, where),
            self.p_send.at[k, index],
            self.p_recv.at[k, index],
            device,
        )

    def to_sibling(self, k, index):
        where = self.columns[index]
        return remote(
            self.spot(k, where),
            self.spot(k, where),
            self.c_send.at[k, index],
            self.c_recv.at[k, index],
            self.here.sibling(),
        )

    def swap(self, index):
        source = self.ins[self.shards + index]
        target = self.outs[self.shards + index]
        core = self.here.core
        return (
            pltpu.make_async_copy(source.at[core], target.at[core], self.s_own.at[index]),
            remote(
                source.at[1 - core],
                target.at[core],
                self.s_send.at[index],
                self.s_recv.at[index],
                self.here.sibling(),
            ),
        )

    def tick(self, tick):
        for leg in (0, 3, 2, 1):
            for k in range(len(self.chunks)):
                if k + leg * self.lags[k] == tick:
                    self.leg(k, leg)
        if tick == self.ticks // 2:
            for index in range(self.swaps):
                for copy in self.swap(index):
                    copy.start()

    def leg(self, k, leg):
        if leg == 0:
            self.keep(k).start()
            for step in (2, 1, 3):
                self.along_z(k, step).start()
        elif leg == 1:
            self.keep(k).wait()
            for step in (1, 2, 3):
                self.along_z(k, step).wait_recv()
            self.plane(k, 1).start()
            self.plane(k, 0).start()
            self.to_sibling(k, 0).start()
        elif leg == 2:
            self.plane(k, 0).wait_recv()
            self.plane(k, 2).start()
            self.to_sibling(k, 1).start()
            self.plane(k, 1).wait_recv()
            self.to_sibling(k, 2).start()
        else:
            self.plane(k, 2).wait_recv()
            self.to_sibling(k, 3).start()

    def arrived(self, k):
        self.claimed.add(k)
        for index in range(4):
            self.to_sibling(k, index).wait_recv()

    def finish(self):
        for k in range(len(self.chunks)):
            for step in (1, 2, 3):
                self.along_z(k, step).wait_send()
            for index in range(3):
                self.plane(k, index).wait_send()
            for index in range(4):
                self.to_sibling(k, index).wait_send()
                if k not in self.claimed:
                    self.to_sibling(k, index).wait_recv()
        for index in range(self.swaps):
            for copy in self.swap(index):
                copy.wait()


class Reduce:
    def __init__(self, gradients, inside=(), swaps=(), most=REDUCE_ROWS, lag=2, starts=None, lags=None):
        self.arrays = [*gradients, *swaps]
        self.outside, self.inside, self.swaps = len(gradients), list(inside), len(swaps)
        self.chunks = []
        for index, gradient in enumerate(gradients):
            self.chunks += cut(index, gradient.shape[4], most)
        shapes = [g.shape[4:] for g in gradients] + self.inside
        for index, shape in enumerate(self.inside):
            self.chunks += cut(self.outside + index, shape[0], most * WIDTH // shape[1])
        count = len(self.chunks)
        self.starts = starts or list(range(count))
        self.lags = lags or [lag] * count
        self.ticks = max(s + 4 * g for s, g in zip(self.starts, self.lags)) + 1
        padded = [(-(-s[0] // 16) * 16, s[1]) for s in shapes]
        self.total_count = len(shapes)
        self.in_specs = [ANY] * len(self.arrays)
        self.out_shapes = [jax.ShapeDtypeStruct(s, F32) for s in shapes]
        self.out_shapes += [jax.ShapeDtypeStruct(a.shape[1:], a.dtype) for a in swaps]
        self.out_specs = [VMEM_WHOLE] * len(shapes) + [ANY] * len(swaps)
        self.scratch = [pltpu.VMEM((4, 2, 2) + s, BF16) for s in padded[: self.outside]]
        self.scratch += [pltpu.VMEM((4, 2, 2, 2) + s, BF16) for s in self.inside]
        for lead in ((4, 2, 2), (2, 4), (4,), (3,)):
            self.scratch += [pltpu.VMEM(lead + s, BF16) for s in padded]
        self.scratch += [
            DMA((count,)),
            DMA((count,)),
            DMA((count,)),
            DMA((count, 3)),
            DMA((count, 3)),
            DMA((count, 3)),
            DMA((count, 3)),
            DMA((max(self.swaps, 1),)),
            DMA((max(self.swaps, 1),)),
        ]

    def bind(self, ins, outs, scratch):
        n = self.total_count
        self.ins, self.outs = ins, outs
        self.own = scratch[:n]
        self.from_core, self.from_second, self.from_first, self.from_z = (
            scratch[i * n : (i + 1) * n] for i in range(1, 5)
        )
        (
            self.own_sem,
            self.c_send,
            self.c_recv,
            self.p_send,
            self.p_recv,
            self.z_send,
            self.z_recv,
            self.s_send,
            self.s_recv,
        ) = scratch[5 * n :]
        self.here = Place()

    def part(self, k):
        array, start, rows = self.chunks[k]
        return array, pl.ds(start, rows)

    def own_at(self, k, z, y, x):
        array, rows = self.part(k)
        if array < self.outside:
            return self.own[array].at[z, y, x, rows, :]
        return self.own[array].at[z, y, x, self.here.core, rows, :]

    def load(self, k):
        array, rows = self.part(k)
        return pltpu.make_async_copy(
            self.ins[array].at[:, :, :, self.here.core, rows, :],
            self.own[array].at[:, :, :, rows, :],
            self.own_sem.at[k],
        )

    def swap_core(self, k):
        array, rows = self.part(k)
        source = self.ins[array] if array < self.outside else self.own[array]
        return remote(
            source.at[:, :, :, 1 - self.here.core, rows, :],
            self.from_core[array].at[:, :, :, rows, :],
            self.c_send.at[k],
            self.c_recv.at[k],
            self.here.sibling(),
        )

    def send_second(self, k, index):
        array, rows = self.part(k)
        where = self.here.second if index == 0 else self.here.across
        return remote(
            self.own_at(k, slice(None), *where),
            self.from_second[array].at[index, :, rows, :],
            self.p_send.at[k, index],
            self.p_recv.at[k, index],
            self.here.to_second(),
        )

    def send_first(self, k):
        array, rows = self.part(k)
        return remote(
            self.own_at(k, slice(None), *self.here.first),
            self.from_first[array].at[:, rows, :],
            self.p_send.at[k, 2],
            self.p_recv.at[k, 2],
            self.here.to_first(),
        )

    def send_z(self, k, step):
        array, rows = self.part(k)
        here = self.here
        return remote(
            self.own_at(k, lax.rem(here.z + step, 4), *here.own),
            self.from_z[array].at[step - 1, rows, :],
            self.z_send.at[k, step - 1],
            self.z_recv.at[k, step - 1],
            here.above(step),
        )

    def swap(self, index):
        source = self.ins[self.outside + index]
        return remote(
            source.at[1 - self.here.core],
            self.outs[self.total_count + index],
            self.s_send.at[index],
            self.s_recv.at[index],
            self.here.sibling(),
        )

    def add_all(self, k):
        array, rows = self.part(k)
        every = slice(None)
        own = self.own_at(k, every, every, every)
        own[...] = own[...] + self.from_core[array][:, :, :, rows, :]

    def add_column(self, k, where, other):
        rows = self.part(k)[1]
        own = self.own_at(k, slice(None), *where)
        own[...] = own[...] + other[:, rows, :]

    def total(self, k):
        array, rows = self.part(k)
        total = self.own_at(k, self.here.z, *self.here.own)[...].astype(F32)
        for step in range(3):
            total = total + self.from_z[array][step, rows, :].astype(F32)
        self.outs[array][rows, :] = total

    def tick(self, tick):
        if tick == 1:
            for index in range(self.swaps):
                self.swap(index).start()
        for leg in (0, 4, 3, 2, 1):
            for k in range(len(self.chunks)):
                if self.starts[k] + leg * self.lags[k] == tick:
                    self.leg(k, leg)

    def leg(self, k, leg):
        array = self.chunks[k][0]
        if leg == 0:
            self.swap_core(k).start()
            if array < self.outside:
                self.load(k).start()
        elif leg == 1:
            if array < self.outside:
                self.load(k).wait()
            self.swap_core(k).wait_recv()
            self.add_all(k)
            for index in (1, 0):
                self.send_second(k, index).start()
        elif leg == 2:
            self.send_second(k, 1).wait_recv()
            self.add_column(k, self.here.first, self.from_second[array].at[1])
            self.send_first(k).start()
            self.send_second(k, 0).wait_recv()
            self.add_column(k, self.here.own, self.from_second[array].at[0])
        elif leg == 3:
            self.send_first(k).wait_recv()
            self.add_column(k, self.here.own, self.from_first[array])
            for step in (2, 1, 3):
                self.send_z(k, step).start()
        else:
            for step in (1, 2, 3):
                self.send_z(k, step).wait_recv()
            self.total(k)

    def finish(self):
        for k in range(len(self.chunks)):
            self.swap_core(k).wait_send()
            for index in (1, 0):
                self.send_second(k, index).wait_send()
            self.send_first(k).wait_send()
            for step in (1, 2, 3):
                self.send_z(k, step).wait_send()
        for index in range(self.swaps):
            self.swap(index).wait()


def everywhere(here, buffer, value, send, recv):
    me = here.y * 4 + here.x * 2 + here.core
    for base, slot, count, peer in (
        (0, me, 8, here.in_plane),
        (8, here.z, 4, here.above),
    ):
        buffer[base + slot] = value
        copies = [
            remote(
                buffer.at[base + slot],
                buffer.at[base + slot],
                send.at[base + step],
                recv.at[base + step],
                peer(step),
            )
            for step in range(1, count)
        ]
        for copy in copies:
            copy.start()
        for copy in copies:
            copy.wait()
        value = buffer[base]
        for index in range(1, count):
            value = value + buffer[base + index]
    return value


def call(name, body, grid, inner, ins, in_specs, out_shapes, out_specs, scratch=(), comm=None, key=0, plan=None):
    params = {"vmem_limit_bytes": VMEM_LIMIT}
    if comm is None:

        def kernel(*refs):
            body(lambda point: None, *refs)

        extra = ([], [], [], [], [])
    else:
        params.update(collective_id=key, has_side_effects=True)
        extra = (comm.arrays, comm.in_specs, comm.out_shapes, comm.out_specs, comm.scratch)
        sizes = (len(ins), len(extra[0]), len(out_shapes), len(extra[2]), len(scratch), len(extra[4]))

        def kernel(*refs):
            parts, at = [], 0
            for size in sizes:
                parts.append(refs[at : at + size])
                at += size
            comm.bind(parts[1], parts[3], parts[5])
            step = pl.program_id(0)

            def pump(point):
                for tick in range(comm.ticks):
                    slot = plan[tick] if plan else tick * grid * inner // comm.ticks
                    if slot % inner == point:

                        @pl.when(step == slot // inner)
                        def _(tick=tick):
                            if tick == 0:
                                comm.here.greet()
                            comm.tick(tick)

            body(pump, *parts[0], *parts[2], *parts[4])

            @pl.when(step == grid - 1)
            def _():
                comm.finish()

    results = pl.pallas_call(
        kernel,
        grid=(grid,),
        out_shape=[*out_shapes, *extra[2]],
        in_specs=[*in_specs, *extra[1]],
        out_specs=[*out_specs, *extra[3]],
        scratch_shapes=[*scratch, *extra[4]],
        compiler_params=pltpu.CompilerParams(**params),
        name=name,
    )(*ins, *extra[0])
    return results[: len(out_shapes)], results[len(out_shapes) :]


def settle(rows, gains, sums, key):
    def kernel(rows_ref, gains_ref, *refs):
        sums_refs = refs[: len(sums)]
        got_ref, gains_out, square_out, buffer, send, recv, s_send, s_recv = refs[len(sums) :]
        here = Place()
        here.greet(plane=True)
        swap = remote(rows_ref.at[1 - here.core], got_ref, s_send, s_recv, here.sibling())
        swap.start()
        squares = jnp.zeros((8, 128), F32)
        for ref in sums_refs:
            values = ref[...]
            squares = squares + jnp.sum((values * values).reshape(-1, 8, 128), axis=0)
        total = everywhere(
            here, buffer, jnp.concatenate([gains_ref[...], squares], axis=0), send, recv
        )
        gains_total = total[:16]
        gains_out[...] = gains_total
        square_out[...] = jnp.broadcast_to(
            jnp.sum(total[16:]) + jnp.sum(gains_total * gains_total), (8, 128)
        )
        swap.wait()

    return pl.pallas_call(
        kernel,
        out_shape=[
            jax.ShapeDtypeStruct(rows.shape[1:], F32),
            jax.ShapeDtypeStruct((16, 128), F32),
            jax.ShapeDtypeStruct((8, 128), F32),
        ],
        in_specs=[ANY, VMEM_WHOLE] + [VMEM_WHOLE] * len(sums),
        out_specs=[ANY, VMEM_WHOLE, VMEM_WHOLE],
        scratch_shapes=[pltpu.VMEM((12, 24, 128), F32), DMA((12,)), DMA((12,)), DMA, DMA],
        compiler_params=pltpu.CompilerParams(
            collective_id=key, has_side_effects=True, vmem_limit_bytes=VMEM_LIMIT
        ),
        name="settle",
    )(rows, gains, *sums)


def segment_lanes(counts):
    sizes = [jnp.where(counts[i] > 0, TEXT + PATCH * counts[i], 0) for i in range(3)]
    ends = (sizes[0], sizes[0] + sizes[1], sizes[0] + sizes[1] + sizes[2])
    places = jnp.arange(ROW, dtype=jnp.int32)[:, None]
    segment = sum((places >= end).astype(jnp.int32) for end in ends)
    lane = jnp.arange(2 * HD, dtype=jnp.int32)[None, :] % HD
    same = lane == segment
    queries = jnp.where((lane < 4) & ~same, MASKED, 0.0).astype(BF16)
    return queries, jnp.where(same, 1.0, 0.0).astype(BF16)


def lanes_of_heads():
    lane = lax.broadcasted_iota(jnp.int32, (1, 2 * HD), 1)
    return lane, (lane < HD, lane >= HD)


def attend_tiles(pump, pair, q_ref, k_ref, v_ref, mq_ref, mk_ref, o_ref, log_ref):
    lane, in_head = lanes_of_heads()
    key = jnp.concatenate([k_ref[...], mk_ref[...]], axis=1)
    value = v_ref[...]
    values = [jnp.where(mine, value, jnp.ones_like(value)) for mine in in_head]
    for index in range(ROW // QUERY_TILE):
        pump(index)
        rows = pl.ds(index * QUERY_TILE, QUERY_TILE)
        query, extra = q_ref[rows, :], mq_ref[rows, :]
        mixed = []
        logs = log_ref[rows, :]
        for head in range(2):
            masked = jnp.where(in_head[head], query, jnp.zeros_like(query))
            scores = dot(jnp.concatenate([masked, extra], axis=1), key, NT)
            top = jnp.max(scores, axis=-1, keepdims=True)
            weight = jnp.exp(scores - top).astype(BF16)
            both = dot(weight, values[head])
            other = pltpu.roll(both, HD, 1)
            mixed.append(both / other)
            total = jnp.where(in_head[head], other, both)
            logs = jnp.where(lane == 2 * pair + head, top + jnp.log(total), logs)
        log_ref[rows, :] = logs
        o_ref[rows, :] = jnp.where(in_head[0], mixed[0], mixed[1]).astype(BF16)


def attend_body(pump, q_ref, k_ref, v_ref, mq_ref, mk_ref, o_ref, log_ref):
    pair = pl.program_id(0)

    @pl.when(pair == 0)
    def _():
        log_ref[...] = jnp.zeros_like(log_ref)

    attend_tiles(
        pump, pair, q_ref.at[0], k_ref.at[0], v_ref.at[0], mq_ref, mk_ref, o_ref, log_ref
    )


PAIRS = WIDTH // (2 * HD)


def third(which):
    return pl.BlockSpec((1, ROW, 2 * HD), lambda p: (which, 0, p))


def attend(projected, extras):
    whole = pl.BlockSpec((ROW, 128), lambda p: (0, 0))
    return call(
        "attend",
        attend_body,
        PAIRS,
        ROW // QUERY_TILE,
        [projected, projected, projected, *extras],
        [third(0), third(1), third(2), whole, whole],
        [jax.ShapeDtypeStruct((ROW, WIDTH), BF16), jax.ShapeDtypeStruct((ROW, 128), F32)],
        [pl.BlockSpec((ROW, 2 * HD), lambda p: (0, p)), whole],
    )


def attend_back_tiles(
    pump, pair, q_ref, k_ref, v_ref, mq_ref, mk_ref, o_ref, do_ref, log_ref, dq_ref, dk, dv
):
    _, in_head = lanes_of_heads()
    pick = jnp.where(
        (lax.broadcasted_iota(jnp.int32, (8, 2 * HD), 1) < HD)
        == (lax.broadcasted_iota(jnp.int32, (8, 2 * HD), 0) == 0),
        jnp.ones((8, 2 * HD), F32),
        jnp.zeros((8, 2 * HD), F32),
    )

    def only(values, head):
        return jnp.where(in_head[head], values, jnp.zeros_like(values))

    dk[...] = jnp.zeros_like(dk)
    dv[...] = jnp.zeros_like(dv)
    for index in range(ROW // BACK_TILE):
        pump(index)
        rows = pl.ds(index * BACK_TILE, BACK_TILE)
        query, grad, extra = q_ref[rows, :], do_ref[rows, :], mq_ref[rows, :]
        key, value = k_ref[...], v_ref[...]
        inner = lax.dot_general(
            pick,
            grad.astype(F32) * o_ref[rows, :].astype(F32),
            NT,
            precision=lax.Precision.HIGHEST,
            preferred_element_type=F32,
        )
        dq = None
        for head in range(2):
            log_total = log_ref[
                pl.ds(2 * pair + head, 1), index * BACK_TILE : (index + 1) * BACK_TILE
            ]
            scores = dot(
                jnp.where(in_head[head], key, mk_ref[...]),
                jnp.where(in_head[head], query, extra),
                NT,
            )
            weight = jnp.exp(scores - log_total)
            down = dot(only(value, head), grad, NT)
            slope = (weight * (down - inner[head : head + 1, :])).astype(BF16)
            dv[...] += dot(weight.astype(BF16), only(grad, head))
            dk[...] += dot(slope, only(query, head))
            step = dot(slope, only(key, head), TN)
            dq = step if dq is None else dq + step
        dq_ref[rows, :] = dq.astype(BF16)


def attend_back_body(
    pump, q_ref, k_ref, v_ref, mq_ref, mk_ref, o_ref, do_ref, log_ref, out_ref, dk, dv
):
    attend_back_tiles(
        pump, pl.program_id(0), q_ref.at[0], k_ref.at[0], v_ref.at[0], mq_ref, mk_ref, o_ref,
        do_ref, log_ref, out_ref.at[0], dk, dv,
    )
    out_ref[1] = dk[...].astype(BF16)
    out_ref[2] = dv[...].astype(BF16)


def attend_back(projected, extras, mixed, grad_mixed, log_rows):
    whole = pl.BlockSpec((ROW, 128), lambda p: (0, 0))
    column = pl.BlockSpec((ROW, 2 * HD), lambda p: (0, p))
    return call(
        "attend_back",
        attend_back_body,
        PAIRS,
        ROW // BACK_TILE,
        [projected, projected, projected, *extras, mixed, grad_mixed, log_rows],
        [third(0), third(1), third(2), whole, whole, column, column]
        + [pl.BlockSpec((2 * PAIRS, ROW), lambda p: (0, 0))],
        [jax.ShapeDtypeStruct((3, ROW, WIDTH), BF16)],
        [pl.BlockSpec((3, ROW, 2 * HD), lambda p: (0, 0, p))],
        [pltpu.VMEM((ROW, 2 * HD), F32), pltpu.VMEM((ROW, 2 * HD), F32)],
    )


def feed_units(
    pump, n2_ref, cot_ref, widen_ref, narrow_ref, widen_grad_ref, narrow_grad_ref, units
):
    pump(0)
    n2, cot = n2_ref[...], cot_ref[...]
    gate = dot(n2, widen_ref[0], NT)
    up = dot(n2, widen_ref[1], NT)
    down = dot(cot, narrow_ref[...], NT)
    square = gate * gate
    bend = jnp.tanh(gate * (GELU_SCALE + (GELU_SCALE * GELU_CUBE) * square))
    half = 0.5 + 0.5 * bend
    curve = gate * half
    slope = half + 0.5 * gate * (1.0 - bend * bend) * (
        GELU_SCALE + (3.0 * GELU_SCALE * GELU_CUBE) * square
    )
    units[0] = (curve * up).astype(BF16)
    units[1] = (down * up * slope).astype(BF16)
    units[2] = (down * curve).astype(BF16)
    pump(1)
    narrow_grad_ref[...] = dot(units[0], cot, TN).astype(BF16)
    widen_grad_ref[0] = dot(units[1], n2, TN).astype(BF16)
    widen_grad_ref[1] = dot(units[2], n2, TN).astype(BF16)
    pump(2)
    return (
        lambda: dot(units[0], narrow_ref[...]),
        lambda: dot(units[1], widen_ref[0]) + dot(units[2], widen_ref[1]),
    )


def feed_start_body(
    pump, n2_ref, cot_ref, widen_ref, narrow_ref,
    result_ref, back_ref, widen_grad_ref, narrow_grad_ref, units,
):
    result, back = feed_units(
        pump, n2_ref, cot_ref, widen_ref, narrow_ref, widen_grad_ref, narrow_grad_ref, units
    )

    @pl.when(pl.program_id(0) == 0)
    def _():
        result_ref[...] = jnp.zeros_like(result_ref)
        back_ref[...] = jnp.zeros_like(back_ref)

    result_ref[...] += result()
    back_ref[...] += back()


def feed_end_body(
    pump, n2_ref, cot_ref, h1_ref, gain_ref, result_part, back_part, widen_ref, narrow_ref,
    result_ref, dh1_ref, e_ref, gain_grad_ref, widen_grad_ref, narrow_grad_ref,
    units, back_ref, part_sem,
):
    step = pl.program_id(0)
    parts = (
        pltpu.make_async_copy(result_part, result_ref, part_sem.at[0]),
        pltpu.make_async_copy(back_part, back_ref, part_sem.at[1]),
    )

    @pl.when(step == 0)
    def _():
        for part in parts:
            part.start()

    result, back = feed_units(
        pump, n2_ref, cot_ref, widen_ref, narrow_ref, widen_grad_ref, narrow_grad_ref, units
    )

    @pl.when(step == 0)
    def _():
        for part in parts:
            part.wait()

    result_ref[...] += result()
    back_ref[...] += back()

    @pl.when(step == pl.num_programs(0) - 1)
    def _():
        gain = gain_ref[...]

        def tile(i, total):
            rows = pl.ds(pl.multiple_of(i * 64, 64), 64)
            h1 = h1_ref[rows, :]
            grad = back_ref[rows, :]
            result_ref[rows, :] += h1
            scale = lax.rsqrt(jnp.mean(h1 * h1, axis=-1, keepdims=True) + NORM_EPS)
            lifted = gain * grad
            inner = jnp.mean(h1 * lifted, axis=-1, keepdims=True)
            dh1 = (
                cot_ref[rows, :].astype(F32)
                + scale * lifted
                - h1 * (scale * scale * scale * inner)
            )
            dh1_ref[rows, :] = dh1
            e_ref[rows, :] = dh1.astype(BF16)
            return total + jnp.sum((grad * h1 * scale).reshape(8, 8, WIDTH), axis=0)

        total = lax.fori_loop(0, ROW // 64, tile, jnp.zeros((8, WIDTH), F32))
        gain_grad_ref[...] = jnp.sum(total, axis=0, keepdims=True)


def whole_block(*shape):
    return pl.BlockSpec(shape, lambda j: (0,) * len(shape), pipeline_mode=pl.Buffered(1))


WIDE_BLOCK = pl.BlockSpec((2, FF_BLOCK, WIDTH), lambda j: (0, j, 0))
TALL_BLOCK = pl.BlockSpec((FF_BLOCK, WIDTH), lambda j: (j, 0))
ROW_F32 = jax.ShapeDtypeStruct((ROW, WIDTH), F32)
ROW_BF16 = jax.ShapeDtypeStruct((ROW, WIDTH), BF16)


def feed_start(n2, cot, widen, narrow, comm=None, key=0):
    rows = whole_block(ROW, WIDTH)
    return call(
        "feed_start",
        feed_start_body,
        narrow.shape[0] // FF_BLOCK,
        3,
        [n2, cot, widen, narrow],
        [rows, rows, WIDE_BLOCK, TALL_BLOCK],
        [
            ROW_F32,
            ROW_F32,
            jax.ShapeDtypeStruct(widen.shape, BF16),
            jax.ShapeDtypeStruct(narrow.shape, BF16),
        ],
        [rows, rows, WIDE_BLOCK, TALL_BLOCK],
        [pltpu.VMEM((3, ROW, FF_BLOCK), BF16)],
        comm=comm,
        key=key,
    )


def feed_end(n2, cot, h1, gain, result_part, back_part, widen, narrow, comm=None, key=0):
    rows = whole_block(ROW, WIDTH)
    line = whole_block(1, WIDTH)
    return call(
        "feed_end",
        feed_end_body,
        narrow.shape[0] // FF_BLOCK,
        3,
        [n2, cot, h1, gain, result_part, back_part, widen, narrow],
        [rows, rows, rows, line, ANY, ANY, WIDE_BLOCK, TALL_BLOCK],
        [
            ROW_F32,
            ROW_F32,
            ROW_BF16,
            jax.ShapeDtypeStruct((1, WIDTH), F32),
            jax.ShapeDtypeStruct(widen.shape, BF16),
            jax.ShapeDtypeStruct(narrow.shape, BF16),
        ],
        [rows, rows, rows, line, WIDE_BLOCK, TALL_BLOCK],
        [pltpu.VMEM((3, ROW, FF_BLOCK), BF16), pltpu.VMEM((ROW, WIDTH), F32), DMA((2,))],
        comm=comm,
        key=key,
    )


def front(attention_shard, gains_tile, feed_shards, tokens, cotangent, extras, key):
    comm = Gather((gains_tile, attention_shard, *feed_shards), (cotangent,), most=16, lag=2)
    points = [0] * 7 + [1] * 2
    rest = comm.ticks - len(points)
    points += [2 + tick * (6 * PAIRS - 2) // rest for tick in range(rest)]

    def body(
        pump, tokens_ref, mq_ref, mk_ref,
        turned_ref, row_ref, qkv_ref, o_ref, o_turned_ref, log_ref, h1_ref, n2_ref,
        normed, landed, parts, out_weights, o_all, gains, t_send, t_recv, part_sem, gains_sem,
    ):
        pair = pl.program_id(0)
        here = comm.here
        core = here.core
        across = remote(tokens_ref.at[1 - core], landed, t_send, t_recv, here.sibling())

        def fetch(p, slot):
            return pltpu.make_async_copy(
                comm.outs[1].at[:, :, :, :, pl.ds(128 * p, 128), :], parts.at[slot], part_sem.at[slot]
            )

        pump(0)

        @pl.when(pair == 0)
        def _():
            across.start()
            log_ref[...] = jnp.zeros_like(log_ref)
            row_ref[core] = tokens_ref[core]
            across.wait_recv()
            row_ref[1 - core] = landed[...]
            comm.arrived(0)
            copy = pltpu.make_async_copy(comm.outs[0], gains, gains_sem)
            copy.start()
            copy.wait()

        def gain_of(which):
            tiles = [
                gains[which * 2 + z, y, x, 0, 0:1, :] + gains[which * 2 + z, y, x, 1, 0:1, :]
                for z in range(2)
                for y in range(2)
                for x in range(2)
            ]
            return jnp.concatenate(tiles, axis=1).astype(F32)

        @pl.when(pair == 0)
        def _():
            gain = gain_of(0)
            for half in range(2):

                def tile(i, carry, half=half):
                    rows = pl.ds(pl.multiple_of(i * 64, 64), 64)
                    x = row_ref[half, rows, :].astype(F32)
                    scale = lax.rsqrt(jnp.mean(x * x, axis=-1, keepdims=True) + NORM_EPS)
                    normed[pl.ds(pl.multiple_of(half * HALF + i * 64, 64), 64), :] = (
                        x * scale * gain
                    ).astype(BF16)
                    return carry

                lax.fori_loop(0, HALF // 64, tile, 0)
            turned_ref[...] = normed[...].T

        pump(1)

        @pl.when(pair == 0)
        def _():
            comm.arrived(1)
            fetch(0, 0).start()

        slot = lax.rem(pair, 2)
        fetch(pair, slot).wait()
        weights = parts[slot].reshape(4, WIDTH, 128)
        three = dot(normed[...], jnp.concatenate([weights[0], weights[1], weights[2]], axis=1))
        for index in range(3):
            qkv_ref[index] = three[:, 128 * index : 128 * (index + 1)].astype(BF16)
        out_weights[pair] = weights[3]
        pump(2)
        for p in range(1, PAIRS):

            @pl.when(pair == p - 1)
            def _(p=p):
                comm.arrived(1 + p)
                fetch(p, p % 2).start()

        attend_tiles(
            lambda index: pump(3 + index),
            pair,
            qkv_ref.at[0],
            qkv_ref.at[1],
            qkv_ref.at[2],
            mq_ref,
            mk_ref,
            o_ref,
            log_ref,
        )
        mixed = o_ref[...]
        o_all[:, pl.ds(pl.multiple_of(pair * 128, 128), 128)] = mixed
        o_turned_ref[...] = mixed.T

        @pl.when(pair == PAIRS - 1)
        def _():
            across.wait_send()
            full = jnp.concatenate([out_weights[p] for p in range(PAIRS)], axis=1)
            gain = gain_of(1)
            h1_ref[...] = dot(o_all[...], full)
            for half in range(2):

                def tile(i, carry, half=half):
                    near = pl.ds(pl.multiple_of(i * 64, 64), 64)
                    rows = pl.ds(pl.multiple_of(half * HALF + i * 64, 64), 64)
                    h1 = row_ref[half, near, :].astype(F32) + h1_ref[rows, :]
                    h1_ref[rows, :] = h1
                    scale = lax.rsqrt(jnp.mean(h1 * h1, axis=-1, keepdims=True) + NORM_EPS)
                    n2_ref[rows, :] = (h1 * scale * gain).astype(BF16)
                    return carry

                lax.fori_loop(0, HALF // 64, tile, 0)

        pump(5)

    whole = pl.BlockSpec((ROW, 128), lambda p: (0, 0))
    turned = jax.ShapeDtypeStruct((WIDTH, ROW), BF16)
    return call(
        "front",
        body,
        PAIRS,
        6,
        [tokens, *extras],
        [VMEM_WHOLE, whole, whole],
        [
            turned,
            jax.ShapeDtypeStruct((2, HALF, WIDTH), BF16),
            jax.ShapeDtypeStruct((3, ROW, WIDTH), BF16),
            ROW_BF16,
            turned,
            jax.ShapeDtypeStruct((ROW, 128), F32),
            ROW_F32,
            ROW_BF16,
        ],
        [
            whole_block(WIDTH, ROW),
            whole_block(2, HALF, WIDTH),
            pl.BlockSpec((3, ROW, 128), lambda p: (0, 0, p)),
            pl.BlockSpec((ROW, 128), lambda p: (0, p)),
            pl.BlockSpec((128, ROW), lambda p: (p, 0)),
            whole,
            whole_block(ROW, WIDTH),
            whole_block(ROW, WIDTH),
        ],
        [
            pltpu.VMEM((ROW, WIDTH), BF16),
            pltpu.VMEM((HALF, WIDTH), BF16),
            pltpu.VMEM((2, 4, 2, 2, 2, 128, 128), BF16),
            pltpu.VMEM((PAIRS, WIDTH, 128), BF16),
            pltpu.VMEM((ROW, WIDTH), BF16),
            pltpu.VMEM((4, 2, 2, 2, 16, 128), BF16),
            DMA,
            DMA,
            DMA((2,)),
            DMA,
        ],
        comm,
        key,
        points,
    )


PART = 96


def back(
    gradients, result, e, dh1, tokens_row, gain, projected, extras, mixed, log_rows,
    attention_parts, normed_turned, mixed_turned, key,
):
    starts = [0, 3, 6, 11, 14, 17, 21, 24] + [9, 9, 19, 19, 29, 29, 34, 39]
    lags = [4] * 12 + [3, 3, 2, 1]
    comm = Reduce(
        gradients, [(PAIRS * 128, 128)], (result,), most=16, starts=starts, lags=lags
    )
    inner, made, after, middle, rest = 8, 4, 5, 6, 7
    plan = [tick // 5 * inner + tick % 5 for tick in range(5 * PAIRS)]
    plan += [(PAIRS - 1) * inner + point for point in (after, middle, rest, rest)]

    def body(
        pump, q_ref, k_ref, v_ref, mq_ref, mk_ref, o_ref, log_ref, parts_ref, rows_ref,
        e_ref, n_turned_ref, o_turned_ref, gain_ref, tokens_ref, dh1_ref,
        da_ref, gain_grad_ref,
        do, three, dk, dv, x_part, dh1_part, x_sem, dh1_sem,
    ):
        pair = pl.program_id(0)
        odd = lax.rem(pair, 2)
        pump(0)

        @pl.when(odd == 0)
        def _():
            rows = [
                jnp.concatenate(
                    [rows_ref[0, 0, 0, c, 128 * p : 128 * (p + 1), :] for p in range(PAIRS)], axis=1
                )
                for c in range(2)
            ]
            two = dot(e_ref[...], jnp.concatenate(rows, axis=0), NT).astype(BF16)
            do[0] = two[:, :128]
            do[1] = two[:, 128:]

        attend_back_tiles(
            lambda index: pump(1 + index), pair, q_ref.at[0], k_ref.at[0], v_ref.at[0],
            mq_ref, mk_ref, o_ref, do.at[odd], log_ref, three.at[odd, :, 0:128], dk, dv,
        )
        three[odd, :, 128:256] = dk[...].astype(BF16)
        three[odd, :, 256:384] = dv[...].astype(BF16)
        made_ref = comm.own[comm.outside]
        late = pair >= PAIRS - 2
        cases = (
            ((odd == 1) & jnp.logical_not(late), (0, 1)),
            ((odd == 0) & late, (0,)),
            ((odd == 1) & late, (1,)),
        )

        def joined(halves):
            return jnp.concatenate([three[half] for half in halves], axis=1)

        def make(halves):
            first = pair - odd + halves[0]
            grads = dot(n_turned_ref[...], joined(halves)).astype(BF16)
            columns = pl.ds(pl.multiple_of(first * 128, 128), 128 * len(halves))
            out_grads = dot(o_turned_ref[...], e_ref[:, columns]).astype(BF16)
            for place in range(len(halves)):
                mine = pl.ds(pl.multiple_of((first + place) * 128, 128), 128)
                for index in range(3):
                    at = 384 * place + 128 * index
                    made_ref[index, :, :, :, mine, :] = grads[:, at : at + 128].reshape(
                        2, 2, 2, 128, 128
                    )
                made_ref[3, :, :, :, mine, :] = out_grads[
                    :, 128 * place : 128 * (place + 1)
                ].reshape(2, 2, 2, 128, 128)

        def down(halves):
            columns = jnp.concatenate(
                [
                    parts_ref[index, :, :, :, 128 * half : 128 * (half + 1), :].reshape(WIDTH, 128)
                    for half in halves
                    for index in range(3)
                ],
                axis=1,
            )
            da_ref[...] += dot(joined(halves), columns, NT)

        @pl.when(pair == 0)
        def _():
            da_ref[...] = jnp.zeros_like(da_ref)

        for case, halves in cases:

            @pl.when(case)
            def _(halves=halves):
                make(halves)

        pump(made)
        for case, halves in cases:

            @pl.when(case)
            def _(halves=halves):
                down(halves)

        pump(after)

        @pl.when(pair == PAIRS - 1)
        def _():
            def fetch(i):
                rows = pl.ds(i * PART, PART)
                slot = i % 2
                return (
                    pltpu.make_async_copy(tokens_ref.at[rows, :], x_part.at[slot], x_sem.at[slot]),
                    pltpu.make_async_copy(dh1_ref.at[rows, :], dh1_part.at[slot], dh1_sem.at[slot]),
                )

            gain_row = gain_ref[...]
            total = jnp.zeros((8, WIDTH), F32)
            for copy in fetch(0):
                copy.start()
            for i in range(ROW // PART):
                if i == ROW // PART // 2:
                    pump(middle)
                if i + 1 < ROW // PART:
                    for copy in fetch(i + 1):
                        copy.start()
                for copy in fetch(i):
                    copy.wait()

                def tile(j, total, i=i):
                    near = pl.ds(pl.multiple_of(j * 48, 16), 48)
                    rows = pl.ds(pl.multiple_of(i * PART + j * 48, 16), 48)
                    x = x_part[i % 2, near, :].astype(F32)
                    grad = da_ref[rows, :]
                    scale = lax.rsqrt(jnp.mean(x * x, axis=-1, keepdims=True) + NORM_EPS)
                    lifted = gain_row * grad
                    middle = jnp.mean(x * lifted, axis=-1, keepdims=True)
                    da_ref[rows, :] = (
                        dh1_part[i % 2, near, :]
                        + scale * lifted
                        - x * (scale * scale * scale * middle)
                    )
                    return total + jnp.sum((grad * x * scale).reshape(6, 8, WIDTH), axis=0)

                total = lax.fori_loop(0, PART // 48, tile, total)
            gain_grad_ref[...] = jnp.sum(total, axis=0, keepdims=True)

        pump(rest)

    extra = pl.BlockSpec((ROW, 128), lambda p: (0, 0), pipeline_mode=pl.Buffered(1))
    line = whole_block(1, WIDTH)
    return call(
        "back",
        body,
        PAIRS,
        inner,
        [projected, projected, projected, *extras, mixed, log_rows, attention_parts, attention_parts]
        + [e, normed_turned, mixed_turned, gain, tokens_row, dh1],
        [third(0), third(1), third(2), extra, extra]
        + [
            pl.BlockSpec((ROW, 128), lambda p: (0, p)),
            whole_block(2 * PAIRS, ROW),
            pl.BlockSpec((3, 2, 2, 2, 256, 128), lambda p: (0, 0, 0, 0, p // 2, 0)),
            pl.BlockSpec(
                (1, 1, 1, 2, WIDTH, 128), lambda p: (3, p // 4, lax.rem(p // 2, 2), 0, 0, 0)
            ),
            whole_block(ROW, WIDTH),
            whole_block(WIDTH, ROW),
            whole_block(WIDTH, ROW),
            line,
            ANY,
            ANY,
        ],
        [ROW_F32, jax.ShapeDtypeStruct((1, WIDTH), F32)],
        [whole_block(ROW, WIDTH), line],
        [
            pltpu.VMEM((2, ROW, 128), BF16),
            pltpu.VMEM((2, ROW, 384), BF16),
            pltpu.VMEM((ROW, 128), F32),
            pltpu.VMEM((ROW, 128), F32),
            pltpu.VMEM((2, PART, WIDTH), BF16),
            pltpu.VMEM((2, PART, WIDTH), F32),
            DMA((2,)),
            DMA((2,)),
        ],
        comm,
        key,
        plan,
    )


def rms_scale(values, gain_vector):
    return (
        values
        * lax.rsqrt(jnp.mean(values * values, axis=-1, keepdims=True) + NORM_EPS)
        * gain_vector
    )


def adam_update(master, first, second, gradient, factors, rate, decay):
    clip_factor, first_fix, second_fix = factors
    clipped = clip_factor * gradient
    first_new = BETA_FIRST * first + (1.0 - BETA_FIRST) * clipped
    second_new = BETA_SECOND * second + (1.0 - BETA_SECOND) * clipped * clipped
    master_new = master - rate * (
        first_new / first_fix / (jnp.sqrt(second_new / second_fix) + ADAM_EPS) + decay * master
    )
    return (master_new, first_new, second_new)


def swap_halves(parts):
    core = lax.axis_index("fsdp")
    got = lax.ppermute(parts[1 - core], "fsdp", [(0, 1), (1, 0)])
    return jnp.where(core == 0, jnp.stack([parts[0], got]), jnp.stack([got, parts[1]]))


def with_half(rows, got):
    own = rows.reshape(2, HALF, WIDTH)
    first = lax.axis_index("fsdp") == 0
    return jnp.where(first, jnp.stack([own[0], got]), jnp.stack([got, own[1]]))


def local(
    own_kernels,
    tokens,
    cotangent,
    images,
    attention_weight,
    attention_first,
    attention_second,
    widen_weight,
    widen_first,
    widen_second,
    narrow_weight,
    narrow_first,
    narrow_second,
    norm_gains,
    gains_first,
    gains_second,
):
    axes = ("dp", "fsdp")
    devices = lax.axis_size(axes)
    core = lax.axis_index("fsdp")
    position = lax.axis_index(axes)
    gain_count = norm_gains.shape[0]
    units = narrow_weight.shape[0]
    split = units * 6 // 11
    attention_low = attention_weight.astype(BF16)
    widen_rows = widen_weight.T.reshape(2, units, WIDTH)
    gains_low = norm_gains.astype(BF16)
    feed_low = [
        (
            widen_rows[:, part].astype(BF16).reshape(-1, WIDTH),
            narrow_weight[part].astype(BF16),
        )
        for part in (slice(None, split), slice(split, None))
    ]
    grid = (4, 2, 2, 2)

    def fetch(shards):
        return [lax.all_gather(shard, axes, axis=0, tiled=True) for shard in shards]

    def summed(gradients):
        return [
            lax.psum_scatter(
                g.astype(F32).reshape(-1, 128), axes, scatter_dimension=0, tiled=True
            ).reshape(-1, WIDTH)
            for g in gradients
        ]

    def other_half(parts):
        return lax.ppermute(
            lax.dynamic_index_in_dim(parts, 1 - core, 0, keepdims=False), "fsdp", [(0, 1), (1, 0)]
        )

    def as_feed(shards):
        return shards[0].reshape(2, -1, WIDTH), shards[1].reshape(-1, WIDTH)

    def as_shards(*gradients):
        return [g.reshape(grid + (-1, WIDTH)) for g in gradients]

    counts = lax.dynamic_index_in_dim(images[:, 0, :], core, 0, keepdims=False)
    extras = segment_lanes(counts)
    gather_b = None
    if own_kernels:
        places = lax.broadcasted_iota(jnp.int32, (16, 2, gain_count), 0) * 2
        places = places + lax.broadcasted_iota(jnp.int32, (16, 2, gain_count), 1)
        gains_tile = jnp.where(places == core, gains_low, jnp.zeros_like(gains_low)).reshape(16, -1)
        columns = attention_low.reshape(-1, PAIRS, 2 * HD).transpose(1, 0, 2).reshape(-1, 2 * HD)
        (
            (normed_turned, tokens_row, projected, mixed, mixed_turned, log_columns, h1, n2),
            (gains_full, attention_parts, *feed_a, cotangent_row),
        ) = front(columns, gains_tile, feed_low[0], tokens, cotangent, extras, 0)
        gains_full = gains_full[:, :, :, :, 0, :].sum(axis=3).reshape(-1)
        gather_b = Gather(feed_low[1])
        cot = cotangent_row.reshape(ROW, WIDTH)
        inputs = tokens_row.reshape(ROW, WIDTH).astype(F32)
        first_gain = gains_full[:WIDTH].astype(F32)
        second_gain = gains_full[WIDTH:].astype(F32)
    else:
        attention_full, gains_full = fetch((attention_low, gains_low))
        first = core == 0
        tokens_row, cotangent_row = (
            jnp.where(first, jnp.stack([a[0], got]), jnp.stack([got, a[1]]))
            for a, got in ((a, other_half(a)) for a in (tokens, cotangent))
        )
        attention = attention_full.reshape(4, WIDTH, WIDTH)
        cot = cotangent_row.reshape(ROW, WIDTH)
        inputs = tokens_row.reshape(ROW, WIDTH).astype(F32)
        first_gain = gains_full[:WIDTH].astype(F32)
        second_gain = gains_full[WIDTH:].astype(F32)
        normed = rms_scale(inputs, first_gain).astype(BF16)
        projected = jnp.einsum(
            "sd,jde->jse", normed, attention[:3], preferred_element_type=F32
        ).astype(BF16)
        (mixed, log_columns), _ = attend(projected, extras)
        h1 = inputs + dot(mixed, attention[3])
        n2 = rms_scale(h1, second_gain).astype(BF16)
    log_rows = log_columns[:, : WIDTH // HD].T
    widen_a, narrow_a = as_feed(feed_a if own_kernels else fetch(feed_low[0]))
    (result_part, back_part, *grads_a), feed_b = feed_start(
        n2, cot, widen_a, narrow_a, gather_b, 2
    )
    widen_b, narrow_b = as_feed(feed_b if own_kernels else fetch(feed_low[1]))
    (result, dh1, e, grad_gain_two, *grads_b), sums_a = feed_end(
        n2,
        cot,
        h1,
        second_gain[None],
        result_part,
        back_part,
        widen_b,
        narrow_b,
        Reduce(as_shards(*grads_a)) if own_kernels else None,
        3,
    )
    if own_kernels:
        (input_rows, grad_gain_one), (*sums_b, attention_sum, got_result) = back(
            as_shards(*grads_b),
            result.reshape(2, HALF, WIDTH),
            e,
            dh1,
            tokens_row.reshape(ROW, WIDTH),
            first_gain[None],
            projected,
            extras,
            mixed,
            log_rows,
            attention_parts,
            normed_turned,
            mixed_turned,
            4,
        )
        got_input, gains_total, square_total = settle(
            input_rows.reshape(2, HALF, WIDTH),
            jnp.concatenate([grad_gain_one, grad_gain_two]).reshape(16, 128),
            [*sums_a, *sums_b, attention_sum],
            5,
        )
        attention_sum = (
            attention_sum.reshape(PAIRS, -1, 128).transpose(1, 0, 2).reshape(-1, WIDTH)
        )
        gains_sum = lax.dynamic_slice_in_dim(
            gains_total.reshape(-1), position * gain_count, gain_count
        )
        squares = square_total[0, 0]
    else:
        grad_out = dot(mixed, e, TN).astype(BF16)
        grad_mixed = dot(e, attention[3], NT).astype(BF16)
        (grad_projected,), _ = attend_back(projected, extras, mixed, grad_mixed, log_rows)
        grad_qkv = jnp.einsum(
            "sd,jse->jde", normed, grad_projected, preferred_element_type=F32
        ).astype(BF16)
        grad_normed = jnp.einsum(
            "jse,jde->sd", grad_projected, attention[:3], preferred_element_type=F32
        )
        scale = lax.rsqrt(jnp.mean(inputs * inputs, axis=-1, keepdims=True) + NORM_EPS)
        lifted = first_gain * grad_normed
        inner = jnp.mean(inputs * lifted, axis=-1, keepdims=True)
        input_rows = dh1 + scale * lifted - inputs * (scale * scale * scale * inner)
        grad_gain_one = jnp.sum(grad_normed * inputs * scale, axis=0)
        grad_attention = jnp.concatenate([grad_qkv, grad_out[None]], axis=0)
        grad_gains = jnp.concatenate([grad_gain_one, grad_gain_two[0]])
        sums_a, sums_b, (attention_sum,) = summed(grads_a), summed(grads_b), summed([grad_attention])
        gains_sum = lax.psum_scatter(grad_gains, axes, scatter_dimension=0, tiled=True)
        squares = lax.psum(
            sum(jnp.sum(g * g) for g in (*sums_a, *sums_b, attention_sum, gains_sum)), axes
        )
        got_result = other_half(result.reshape(2, HALF, WIDTH))
        got_input = other_half(input_rows.reshape(2, HALF, WIDTH))
    widen_sum = jnp.concatenate(
        [sums_a[0].reshape(2, -1, WIDTH), sums_b[0].reshape(2, -1, WIDTH)], axis=1
    ).reshape(-1, WIDTH)
    narrow_sum = jnp.concatenate([sums_a[1], sums_b[1]], axis=0)
    grad_norm = jnp.sqrt(squares)
    clip_factor = jnp.minimum(1.0, CLIP_LIMIT / (grad_norm + 1e-06))
    step_value = jnp.float32(STEP_VALUE)
    factors = (
        clip_factor,
        1.0 - jnp.power(jnp.float32(BETA_FIRST), step_value),
        1.0 - jnp.power(jnp.float32(BETA_SECOND), step_value),
    )
    return (
        with_half(result, got_result),
        with_half(input_rows, got_input),
        *adam_update(
            attention_weight,
            attention_first,
            attention_second,
            attention_sum,
            factors,
            MATRIX_RATE,
            DECAY,
        ),
        *adam_update(
            widen_weight, widen_first, widen_second, widen_sum.T, factors, MATRIX_RATE, DECAY
        ),
        *adam_update(
            narrow_weight, narrow_first, narrow_second, narrow_sum, factors, MATRIX_RATE, DECAY
        ),
        *adam_update(norm_gains, gains_first, gains_second, gains_sum, factors, GAIN_RATE, 0.0),
        grad_norm,
    )


def solution(mesh):
    both = ("dp", "fsdp")
    rows = P(None, both, None)
    tall = P(both, None)
    wide = P(None, both)
    flat = P(both)
    weights = (tall, tall, tall, wide, wide, wide, tall, tall, tall, flat, flat, flat)
    own_kernels = dict(mesh.shape) == {"dp": 16, "fsdp": 2}
    return jax.shard_map(
        functools.partial(local, own_kernels),
        mesh=mesh,
        in_specs=(rows, rows, P(None, "dp", None)) + weights,
        out_specs=(rows, rows) + weights + (P(),),
        check_vma=False,
    )
```

```python
import functools

import jax
import jax.numpy as jnp
from jax import lax
from jax.experimental import pallas as pl
from jax.experimental.pallas import tpu as pltpu
from jax.sharding import PartitionSpec as P

HD = 64
TEXT = 128
PATCH = 256
ROW = 1152
WIDTH = 1024
HALF = ROW // 2
QUERY_TILE = 576
BACK_TILE = 384
FF_BLOCK = 256
GATHER_ROWS = 16
REDUCE_ROWS = 16

NORM_EPS = 1e-06
MASKED = -(2.0**30)
BETA_FIRST = 0.9
BETA_SECOND = 0.999
ADAM_EPS = 1e-08
MATRIX_RATE = 0.05
GAIN_RATE = 0.3
DECAY = 0.1
CLIP_LIMIT = 1.0
STEP_VALUE = 10.0
GELU_SCALE = 0.7978845608028654
GELU_CUBE = 0.044715

BF16 = jnp.bfloat16
F32 = jnp.float32
MESH = pl.DeviceIdType.MESH
ANY = pl.BlockSpec(memory_space=pl.ANY)
VMEM_WHOLE = pl.BlockSpec(memory_space=pltpu.VMEM)
DMA = pltpu.SemaphoreType.DMA
VMEM_LIMIT = 62 * 2**20

NT = (((1,), (1,)), ((), ()))
TN = (((0,), (0,)), ((), ()))


def dot(left, right, dims=(((1,), (0,)), ((), ()))):
    return lax.dot_general(left, right, dims, preferred_element_type=F32)


class Place:
    def __init__(self):
        self.dp = lax.axis_index("dp")
        self.core = lax.axis_index("fsdp")
        self.z = self.dp // 4
        self.y = lax.rem(self.dp // 2, 2)
        self.x = lax.rem(self.dp, 2)
        flip_y = 1 - self.y
        flip_x = 1 - self.x
        is_zero = self.core == 0
        self.own = (self.y, self.x)
        self.first = (jnp.where(is_zero, self.y, flip_y), jnp.where(is_zero, flip_x, self.x))
        self.second = (jnp.where(is_zero, flip_y, self.y), jnp.where(is_zero, self.x, flip_x))
        self.across = (flip_y, flip_x)

    def at(self, z, spot):
        return (z * 4 + spot[0] * 2 + spot[1], self.core)

    def above(self, step):
        return self.at(lax.rem(self.z + step, 4), self.own)

    def to_first(self):
        return self.at(self.z, self.first)

    def to_second(self):
        return self.at(self.z, self.second)

    def sibling(self):
        return (self.dp, 1 - self.core)

    def in_plane(self, step):
        y, x, core = ((1 - a) if step & bit else a for a, bit in ((self.y, 4), (self.x, 2), (self.core, 1)))
        return (self.z * 4 + y * 2 + x, core)

    def greet(self, plane=False):
        barrier = pltpu.get_barrier_semaphore()
        peers = [self.above(1), self.above(2), self.above(3)]
        if plane:
            peers += [self.in_plane(step) for step in range(1, 8)]
        else:
            peers += [self.to_first(), self.to_second(), self.sibling()]
        for peer in peers:
            pl.semaphore_signal(barrier, inc=1, device_id=peer, device_id_type=MESH)
        pl.semaphore_wait(barrier, len(peers))


def remote(source, target, send_sem, recv_sem, device):
    return pltpu.make_async_remote_copy(
        src_ref=source,
        dst_ref=target,
        send_sem=send_sem,
        recv_sem=recv_sem,
        device_id=device,
        device_id_type=MESH,
    )


def cut(index, rows, most):
    pieces = -(-rows // most)
    step = -(-rows // (pieces * 16)) * 16
    return [(index, at, min(step, rows - at)) for at in range(0, rows, step)]


class Gather:
    def __init__(self, shards, swaps=(), most=GATHER_ROWS, lag=3):
        self.arrays = [*shards, *swaps]
        self.shards, self.swaps = len(shards), len(swaps)
        self.chunks = []
        for index, shard in enumerate(shards):
            self.chunks += cut(index, shard.shape[0], most * WIDTH // shard.shape[1])
        count = len(self.chunks)
        self.lags = [lag] * count
        self.ticks = max(k + 3 * g for k, g in enumerate(self.lags)) + 1
        self.in_specs = [VMEM_WHOLE] * len(self.arrays)
        self.out_shapes = [jax.ShapeDtypeStruct((4, 2, 2, 2) + a.shape, a.dtype) for a in shards]
        self.out_shapes += [jax.ShapeDtypeStruct(a.shape, a.dtype) for a in swaps]
        self.out_specs = [ANY] * len(self.arrays)
        self.scratch = [
            DMA((count,)),
            DMA((count, 3)),
            DMA((count, 3)),
            DMA((count, 3)),
            DMA((count, 3)),
            DMA((count, 4)),
            DMA((count, 4)),
            DMA((max(self.swaps, 1),)),
            DMA((max(self.swaps, 1),)),
            DMA((max(self.swaps, 1),)),
        ]

    def bind(self, ins, outs, scratch):
        self.ins, self.outs = ins, outs
        (
            self.own_sem,
            self.z_send,
            self.z_recv,
            self.p_send,
            self.p_recv,
            self.c_send,
            self.c_recv,
            self.s_own,
            self.s_send,
            self.s_recv,
        ) = scratch
        self.claimed = set()
        self.here = Place()
        self.columns = (self.here.own, self.here.first, self.here.second, self.here.across)

    def spot(self, k, where):
        array, start, rows = self.chunks[k]
        return self.outs[array].at[:, where[0], where[1], self.here.core, pl.ds(start, rows), :]

    def mine(self, k):
        array, start, rows = self.chunks[k]
        here = self.here
        return (
            self.ins[array].at[pl.ds(start, rows), :],
            self.outs[array].at[here.z, here.y, here.x, here.core, pl.ds(start, rows), :],
        )

    def keep(self, k):
        source, target = self.mine(k)
        return pltpu.make_async_copy(source, target, self.own_sem.at[k])

    def along_z(self, k, step):
        source, target = self.mine(k)
        return remote(
            source,
            target,
            self.z_send.at[k, step - 1],
            self.z_recv.at[k, step - 1],
            self.here.above(step),
        )

    def plane(self, k, index):
        where = self.here.first if index == 2 else self.here.own
        device = self.here.to_first() if index == 0 else self.here.to_second()
        return remote(
            self.spot(k, where),
            self.spot(k, where),
            self.p_send.at[k, index],
            self.p_recv.at[k, index],
            device,
        )

    def to_sibling(self, k, index):
        where = self.columns[index]
        return remote(
            self.spot(k, where),
            self.spot(k, where),
            self.c_send.at[k, index],
            self.c_recv.at[k, index],
            self.here.sibling(),
        )

    def swap(self, index):
        source = self.ins[self.shards + index]
        target = self.outs[self.shards + index]
        core = self.here.core
        return (
            pltpu.make_async_copy(source.at[core], target.at[core], self.s_own.at[index]),
            remote(
                source.at[1 - core],
                target.at[core],
                self.s_send.at[index],
                self.s_recv.at[index],
                self.here.sibling(),
            ),
        )

    def tick(self, tick):
        for leg in (0, 3, 2, 1):
            for k in range(len(self.chunks)):
                if k + leg * self.lags[k] == tick:
                    self.leg(k, leg)
        if tick == self.ticks // 2:
            for index in range(self.swaps):
                for copy in self.swap(index):
                    copy.start()

    def leg(self, k, leg):
        if leg == 0:
            self.keep(k).start()
            for step in (2, 1, 3):
                self.along_z(k, step).start()
        elif leg == 1:
            self.keep(k).wait()
            for step in (1, 2, 3):
                self.along_z(k, step).wait_recv()
            self.plane(k, 1).start()
            self.plane(k, 0).start()
            self.to_sibling(k, 0).start()
        elif leg == 2:
            self.plane(k, 0).wait_recv()
            self.plane(k, 2).start()
            self.to_sibling(k, 1).start()
            self.plane(k, 1).wait_recv()
            self.to_sibling(k, 2).start()
        else:
            self.plane(k, 2).wait_recv()
            self.to_sibling(k, 3).start()

    def arrived(self, k):
        self.claimed.add(k)
        for index in range(4):
            self.to_sibling(k, index).wait_recv()

    def finish(self):
        for k in range(len(self.chunks)):
            for step in (1, 2, 3):
                self.along_z(k, step).wait_send()
            for index in range(3):
                self.plane(k, index).wait_send()
            for index in range(4):
                self.to_sibling(k, index).wait_send()
                if k not in self.claimed:
                    self.to_sibling(k, index).wait_recv()
        for index in range(self.swaps):
            for copy in self.swap(index):
                copy.wait()


class Reduce:
    def __init__(self, gradients, inside=(), swaps=(), most=REDUCE_ROWS, lag=2, starts=None, lags=None):
        self.arrays = [*gradients, *swaps]
        self.outside, self.inside, self.swaps = len(gradients), list(inside), len(swaps)
        self.chunks = []
        for index, gradient in enumerate(gradients):
            self.chunks += cut(index, gradient.shape[4], most)
        shapes = [g.shape[4:] for g in gradients] + self.inside
        for index, shape in enumerate(self.inside):
            self.chunks += cut(self.outside + index, shape[0], most * WIDTH // shape[1])
        count = len(self.chunks)
        self.starts = starts or list(range(count))
        self.lags = lags or [lag] * count
        self.ticks = max(s + 4 * g for s, g in zip(self.starts, self.lags)) + 1
        padded = [(-(-s[0] // 16) * 16, s[1]) for s in shapes]
        self.total_count = len(shapes)
        self.in_specs = [ANY] * len(self.arrays)
        self.out_shapes = [jax.ShapeDtypeStruct(s, F32) for s in shapes]
        self.out_shapes += [jax.ShapeDtypeStruct(a.shape[1:], a.dtype) for a in swaps]
        self.out_specs = [VMEM_WHOLE] * len(shapes) + [ANY] * len(swaps)
        self.scratch = [pltpu.VMEM((4, 2, 2) + s, BF16) for s in padded[: self.outside]]
        self.scratch += [pltpu.VMEM((4, 2, 2, 2) + s, BF16) for s in self.inside]
        for lead in ((4, 2, 2), (2, 4), (4,), (3,)):
            self.scratch += [pltpu.VMEM(lead + s, BF16) for s in padded]
        self.scratch += [
            DMA((count,)),
            DMA((count,)),
            DMA((count,)),
            DMA((count, 3)),
            DMA((count, 3)),
            DMA((count, 3)),
            DMA((count, 3)),
            DMA((max(self.swaps, 1),)),
            DMA((max(self.swaps, 1),)),
        ]

    def bind(self, ins, outs, scratch):
        n = self.total_count
        self.ins, self.outs = ins, outs
        self.own = scratch[:n]
        self.from_core, self.from_second, self.from_first, self.from_z = (
            scratch[i * n : (i + 1) * n] for i in range(1, 5)
        )
        (
            self.own_sem,
            self.c_send,
            self.c_recv,
            self.p_send,
            self.p_recv,
            self.z_send,
            self.z_recv,
            self.s_send,
            self.s_recv,
        ) = scratch[5 * n :]
        self.here = Place()

    def part(self, k):
        array, start, rows = self.chunks[k]
        return array, pl.ds(start, rows)

    def own_at(self, k, z, y, x):
        array, rows = self.part(k)
        if array < self.outside:
            return self.own[array].at[z, y, x, rows, :]
        return self.own[array].at[z, y, x, self.here.core, rows, :]

    def load(self, k):
        array, rows = self.part(k)
        return pltpu.make_async_copy(
            self.ins[array].at[:, :, :, self.here.core, rows, :],
            self.own[array].at[:, :, :, rows, :],
            self.own_sem.at[k],
        )

    def swap_core(self, k):
        array, rows = self.part(k)
        source = self.ins[array] if array < self.outside else self.own[array]
        return remote(
            source.at[:, :, :, 1 - self.here.core, rows, :],
            self.from_core[array].at[:, :, :, rows, :],
            self.c_send.at[k],
            self.c_recv.at[k],
            self.here.sibling(),
        )

    def send_second(self, k, index):
        array, rows = self.part(k)
        where = self.here.second if index == 0 else self.here.across
        return remote(
            self.own_at(k, slice(None), *where),
            self.from_second[array].at[index, :, rows, :],
            self.p_send.at[k, index],
            self.p_recv.at[k, index],
            self.here.to_second(),
        )

    def send_first(self, k):
        array, rows = self.part(k)
        return remote(
            self.own_at(k, slice(None), *self.here.first),
            self.from_first[array].at[:, rows, :],
            self.p_send.at[k, 2],
            self.p_recv.at[k, 2],
            self.here.to_first(),
        )

    def send_z(self, k, step):
        array, rows = self.part(k)
        here = self.here
        return remote(
            self.own_at(k, lax.rem(here.z + step, 4), *here.own),
            self.from_z[array].at[step - 1, rows, :],
            self.z_send.at[k, step - 1],
            self.z_recv.at[k, step - 1],
            here.above(step),
        )

    def swap(self, index):
        source = self.ins[self.outside + index]
        return remote(
            source.at[1 - self.here.core],
            self.outs[self.total_count + index],
            self.s_send.at[index],
            self.s_recv.at[index],
            self.here.sibling(),
        )

    def add_all(self, k):
        array, rows = self.part(k)
        every = slice(None)
        own = self.own_at(k, every, every, every)
        own[...] = own[...] + self.from_core[array][:, :, :, rows, :]

    def add_column(self, k, where, other):
        rows = self.part(k)[1]
        own = self.own_at(k, slice(None), *where)
        own[...] = own[...] + other[:, rows, :]

    def total(self, k):
        array, rows = self.part(k)
        total = self.own_at(k, self.here.z, *self.here.own)[...].astype(F32)
        for step in range(3):
            total = total + self.from_z[array][step, rows, :].astype(F32)
        self.outs[array][rows, :] = total

    def tick(self, tick):
        if tick == 1:
            for index in range(self.swaps):
                self.swap(index).start()
        for leg in (0, 4, 3, 2, 1):
            for k in range(len(self.chunks)):
                if self.starts[k] + leg * self.lags[k] == tick:
                    self.leg(k, leg)

    def leg(self, k, leg):
        array = self.chunks[k][0]
        if leg == 0:
            self.swap_core(k).start()
            if array < self.outside:
                self.load(k).start()
        elif leg == 1:
            if array < self.outside:
                self.load(k).wait()
            self.swap_core(k).wait_recv()
            self.add_all(k)
            for index in (1, 0):
                self.send_second(k, index).start()
        elif leg == 2:
            self.send_second(k, 1).wait_recv()
            self.add_column(k, self.here.first, self.from_second[array].at[1])
            self.send_first(k).start()
            self.send_second(k, 0).wait_recv()
            self.add_column(k, self.here.own, self.from_second[array].at[0])
        elif leg == 3:
            self.send_first(k).wait_recv()
            self.add_column(k, self.here.own, self.from_first[array])
            for step in (2, 1, 3):
                self.send_z(k, step).start()
        else:
            for step in (1, 2, 3):
                self.send_z(k, step).wait_recv()
            self.total(k)

    def finish(self):
        for k in range(len(self.chunks)):
            self.swap_core(k).wait_send()
            for index in (1, 0):
                self.send_second(k, index).wait_send()
            self.send_first(k).wait_send()
            for step in (1, 2, 3):
                self.send_z(k, step).wait_send()
        for index in range(self.swaps):
            self.swap(index).wait()


def everywhere(here, buffer, value, send, recv):
    me = here.y * 4 + here.x * 2 + here.core
    for base, slot, count, peer in (
        (0, me, 8, here.in_plane),
        (8, here.z, 4, here.above),
    ):
        buffer[base + slot] = value
        copies = [
            remote(
                buffer.at[base + slot],
                buffer.at[base + slot],
                send.at[base + step],
                recv.at[base + step],
                peer(step),
            )
            for step in range(1, count)
        ]
        for copy in copies:
            copy.start()
        for copy in copies:
            copy.wait()
        value = buffer[base]
        for index in range(1, count):
            value = value + buffer[base + index]
    return value


def call(name, body, grid, inner, ins, in_specs, out_shapes, out_specs, scratch=(), comm=None, key=0, plan=None):
    params = {"vmem_limit_bytes": VMEM_LIMIT}
    if comm is None:

        def kernel(*refs):
            body(lambda point: None, *refs)

        extra = ([], [], [], [], [])
    else:
        params.update(collective_id=key, has_side_effects=True)
        extra = (comm.arrays, comm.in_specs, comm.out_shapes, comm.out_specs, comm.scratch)
        sizes = (len(ins), len(extra[0]), len(out_shapes), len(extra[2]), len(scratch), len(extra[4]))

        def kernel(*refs):
            parts, at = [], 0
            for size in sizes:
                parts.append(refs[at : at + size])
                at += size
            comm.bind(parts[1], parts[3], parts[5])
            step = pl.program_id(0)

            def pump(point):
                for tick in range(comm.ticks):
                    slot = plan[tick] if plan else tick * grid * inner // comm.ticks
                    if slot % inner == point:

                        @pl.when(step == slot // inner)
                        def _(tick=tick):
                            if tick == 0:
                                comm.here.greet()
                            comm.tick(tick)

            body(pump, *parts[0], *parts[2], *parts[4])

            @pl.when(step == grid - 1)
            def _():
                comm.finish()

    results = pl.pallas_call(
        kernel,
        grid=(grid,),
        out_shape=[*out_shapes, *extra[2]],
        in_specs=[*in_specs, *extra[1]],
        out_specs=[*out_specs, *extra[3]],
        scratch_shapes=[*scratch, *extra[4]],
        compiler_params=pltpu.CompilerParams(**params),
        name=name,
    )(*ins, *extra[0])
    return results[: len(out_shapes)], results[len(out_shapes) :]


def settle(rows, gains, sums, key):
    def kernel(rows_ref, gains_ref, *refs):
        sums_refs = refs[: len(sums)]
        got_ref, gains_out, square_out, buffer, send, recv, s_send, s_recv = refs[len(sums) :]
        here = Place()
        here.greet(plane=True)
        swap = remote(rows_ref.at[1 - here.core], got_ref, s_send, s_recv, here.sibling())
        swap.start()
        squares = jnp.zeros((8, 128), F32)
        for ref in sums_refs:
            values = ref[...]
            squares = squares + jnp.sum((values * values).reshape(-1, 8, 128), axis=0)
        total = everywhere(
            here, buffer, jnp.concatenate([gains_ref[...], squares], axis=0), send, recv
        )
        gains_total = total[:16]
        gains_out[...] = gains_total
        square_out[...] = jnp.broadcast_to(
            jnp.sum(total[16:]) + jnp.sum(gains_total * gains_total), (8, 128)
        )
        swap.wait()

    return pl.pallas_call(
        kernel,
        out_shape=[
            jax.ShapeDtypeStruct(rows.shape[1:], F32),
            jax.ShapeDtypeStruct((16, 128), F32),
            jax.ShapeDtypeStruct((8, 128), F32),
        ],
        in_specs=[ANY, VMEM_WHOLE] + [VMEM_WHOLE] * len(sums),
        out_specs=[ANY, VMEM_WHOLE, VMEM_WHOLE],
        scratch_shapes=[pltpu.VMEM((12, 24, 128), F32), DMA((12,)), DMA((12,)), DMA, DMA],
        compiler_params=pltpu.CompilerParams(
            collective_id=key, has_side_effects=True, vmem_limit_bytes=VMEM_LIMIT
        ),
        name="settle",
    )(rows, gains, *sums)


def segment_lanes(counts):
    sizes = [jnp.where(counts[i] > 0, TEXT + PATCH * counts[i], 0) for i in range(3)]
    ends = (sizes[0], sizes[0] + sizes[1], sizes[0] + sizes[1] + sizes[2])
    places = jnp.arange(ROW, dtype=jnp.int32)[:, None]
    segment = sum((places >= end).astype(jnp.int32) for end in ends)
    lane = jnp.arange(2 * HD, dtype=jnp.int32)[None, :] % HD
    same = lane == segment
    queries = jnp.where((lane < 4) & ~same, MASKED, 0.0).astype(BF16)
    return queries, jnp.where(same, 1.0, 0.0).astype(BF16)


def lanes_of_heads():
    lane = lax.broadcasted_iota(jnp.int32, (1, 2 * HD), 1)
    return lane, (lane < HD, lane >= HD)


def attend_tiles(pump, pair, q_ref, k_ref, v_ref, mq_ref, mk_ref, o_ref, log_ref):
    lane, in_head = lanes_of_heads()
    key = jnp.concatenate([k_ref[...], mk_ref[...]], axis=1)
    value = v_ref[...]
    values = [jnp.where(mine, value, jnp.ones_like(value)) for mine in in_head]
    for index in range(ROW // QUERY_TILE):
        pump(index)
        rows = pl.ds(index * QUERY_TILE, QUERY_TILE)
        query, extra = q_ref[rows, :], mq_ref[rows, :]
        mixed = []
        logs = log_ref[rows, :]
        for head in range(2):
            masked = jnp.where(in_head[head], query, jnp.zeros_like(query))
            scores = dot(jnp.concatenate([masked, extra], axis=1), key, NT)
            top = jnp.max(scores, axis=-1, keepdims=True)
            weight = jnp.exp(scores - top).astype(BF16)
            both = dot(weight, values[head])
            other = pltpu.roll(both, HD, 1)
            mixed.append(both / other)
            total = jnp.where(in_head[head], other, both)
            logs = jnp.where(lane == 2 * pair + head, top + jnp.log(total), logs)
        log_ref[rows, :] = logs
        o_ref[rows, :] = jnp.where(in_head[0], mixed[0], mixed[1]).astype(BF16)


def attend_body(pump, q_ref, k_ref, v_ref, mq_ref, mk_ref, o_ref, log_ref):
    pair = pl.program_id(0)

    @pl.when(pair == 0)
    def _():
        log_ref[...] = jnp.zeros_like(log_ref)

    attend_tiles(
        pump, pair, q_ref.at[0], k_ref.at[0], v_ref.at[0], mq_ref, mk_ref, o_ref, log_ref
    )


PAIRS = WIDTH // (2 * HD)


def third(which):
    return pl.BlockSpec((1, ROW, 2 * HD), lambda p: (which, 0, p))


def attend(projected, extras):
    whole = pl.BlockSpec((ROW, 128), lambda p: (0, 0))
    return call(
        "attend",
        attend_body,
        PAIRS,
        ROW // QUERY_TILE,
        [projected, projected, projected, *extras],
        [third(0), third(1), third(2), whole, whole],
        [jax.ShapeDtypeStruct((ROW, WIDTH), BF16), jax.ShapeDtypeStruct((ROW, 128), F32)],
        [pl.BlockSpec((ROW, 2 * HD), lambda p: (0, p)), whole],
    )


def attend_back_tiles(
    pump, pair, q_ref, k_ref, v_ref, mq_ref, mk_ref, o_ref, do_ref, log_ref, dq_ref, dk, dv
):
    _, in_head = lanes_of_heads()
    pick = jnp.where(
        (lax.broadcasted_iota(jnp.int32, (8, 2 * HD), 1) < HD)
        == (lax.broadcasted_iota(jnp.int32, (8, 2 * HD), 0) == 0),
        jnp.ones((8, 2 * HD), F32),
        jnp.zeros((8, 2 * HD), F32),
    )

    def only(values, head):
        return jnp.where(in_head[head], values, jnp.zeros_like(values))

    dk[...] = jnp.zeros_like(dk)
    dv[...] = jnp.zeros_like(dv)
    for index in range(ROW // BACK_TILE):
        pump(index)
        rows = pl.ds(index * BACK_TILE, BACK_TILE)
        query, grad, extra = q_ref[rows, :], do_ref[rows, :], mq_ref[rows, :]
        key, value = k_ref[...], v_ref[...]
        inner = lax.dot_general(
            pick,
            grad.astype(F32) * o_ref[rows, :].astype(F32),
            NT,
            precision=lax.Precision.HIGHEST,
            preferred_element_type=F32,
        )
        dq = None
        for head in range(2):
            log_total = log_ref[
                pl.ds(2 * pair + head, 1), index * BACK_TILE : (index + 1) * BACK_TILE
            ]
            scores = dot(
                jnp.where(in_head[head], key, mk_ref[...]),
                jnp.where(in_head[head], query, extra),
                NT,
            )
            weight = jnp.exp(scores - log_total)
            down = dot(only(value, head), grad, NT)
            slope = (weight * (down - inner[head : head + 1, :])).astype(BF16)
            dv[...] += dot(weight.astype(BF16), only(grad, head))
            dk[...] += dot(slope, only(query, head))
            step = dot(slope, only(key, head), TN)
            dq = step if dq is None else dq + step
        dq_ref[rows, :] = dq.astype(BF16)


def attend_back_body(
    pump, q_ref, k_ref, v_ref, mq_ref, mk_ref, o_ref, do_ref, log_ref, out_ref, dk, dv
):
    attend_back_tiles(
        pump, pl.program_id(0), q_ref.at[0], k_ref.at[0], v_ref.at[0], mq_ref, mk_ref, o_ref,
        do_ref, log_ref, out_ref.at[0], dk, dv,
    )
    out_ref[1] = dk[...].astype(BF16)
    out_ref[2] = dv[...].astype(BF16)


def attend_back(projected, extras, mixed, grad_mixed, log_rows):
    whole = pl.BlockSpec((ROW, 128), lambda p: (0, 0))
    column = pl.BlockSpec((ROW, 2 * HD), lambda p: (0, p))
    return call(
        "attend_back",
        attend_back_body,
        PAIRS,
        ROW // BACK_TILE,
        [projected, projected, projected, *extras, mixed, grad_mixed, log_rows],
        [third(0), third(1), third(2), whole, whole, column, column]
        + [pl.BlockSpec((2 * PAIRS, ROW), lambda p: (0, 0))],
        [jax.ShapeDtypeStruct((3, ROW, WIDTH), BF16)],
        [pl.BlockSpec((3, ROW, 2 * HD), lambda p: (0, 0, p))],
        [pltpu.VMEM((ROW, 2 * HD), F32), pltpu.VMEM((ROW, 2 * HD), F32)],
    )


def feed_units(
    pump, n2_ref, cot_ref, widen_ref, narrow_ref, widen_grad_ref, narrow_grad_ref, units
):
    pump(0)
    n2, cot = n2_ref[...], cot_ref[...]
    gate = dot(n2, widen_ref[0], NT)
    up = dot(n2, widen_ref[1], NT)
    down = dot(cot, narrow_ref[...], NT)
    square = gate * gate
    bend = jnp.tanh(gate * (GELU_SCALE + (GELU_SCALE * GELU_CUBE) * square))
    half = 0.5 + 0.5 * bend
    curve = gate * half
    slope = half + 0.5 * gate * (1.0 - bend * bend) * (
        GELU_SCALE + (3.0 * GELU_SCALE * GELU_CUBE) * square
    )
    units[0] = (curve * up).astype(BF16)
    units[1] = (down * up * slope).astype(BF16)
    units[2] = (down * curve).astype(BF16)
    pump(1)
    narrow_grad_ref[...] = dot(units[0], cot, TN).astype(BF16)
    widen_grad_ref[0] = dot(units[1], n2, TN).astype(BF16)
    widen_grad_ref[1] = dot(units[2], n2, TN).astype(BF16)
    pump(2)
    return (
        lambda: dot(units[0], narrow_ref[...]),
        lambda: dot(units[1], widen_ref[0]) + dot(units[2], widen_ref[1]),
    )


def feed_start_body(
    pump, n2_ref, cot_ref, widen_ref, narrow_ref,
    result_ref, back_ref, widen_grad_ref, narrow_grad_ref, units,
):
    result, back = feed_units(
        pump, n2_ref, cot_ref, widen_ref, narrow_ref, widen_grad_ref, narrow_grad_ref, units
    )

    @pl.when(pl.program_id(0) == 0)
    def _():
        result_ref[...] = jnp.zeros_like(result_ref)
        back_ref[...] = jnp.zeros_like(back_ref)

    result_ref[...] += result()
    back_ref[...] += back()


def feed_end_body(
    pump, n2_ref, cot_ref, h1_ref, gain_ref, result_part, back_part, widen_ref, narrow_ref,
    result_ref, dh1_ref, e_ref, gain_grad_ref, widen_grad_ref, narrow_grad_ref,
    units, back_ref, part_sem,
):
    step = pl.program_id(0)
    parts = (
        pltpu.make_async_copy(result_part, result_ref, part_sem.at[0]),
        pltpu.make_async_copy(back_part, back_ref, part_sem.at[1]),
    )

    @pl.when(step == 0)
    def _():
        for part in parts:
            part.start()

    result, back = feed_units(
        pump, n2_ref, cot_ref, widen_ref, narrow_ref, widen_grad_ref, narrow_grad_ref, units
    )

    @pl.when(step == 0)
    def _():
        for part in parts:
            part.wait()

    result_ref[...] += result()
    back_ref[...] += back()

    @pl.when(step == pl.num_programs(0) - 1)
    def _():
        gain = gain_ref[...]

        def tile(i, total):
            rows = pl.ds(pl.multiple_of(i * 32, 32), 32)
            h1 = h1_ref[rows, :]
            grad = back_ref[rows, :]
            result_ref[rows, :] += h1
            scale = lax.rsqrt(jnp.mean(h1 * h1, axis=-1, keepdims=True) + NORM_EPS)
            lifted = gain * grad
            inner = jnp.mean(h1 * lifted, axis=-1, keepdims=True)
            dh1 = (
                cot_ref[rows, :].astype(F32)
                + scale * lifted
                - h1 * (scale * scale * scale * inner)
            )
            dh1_ref[rows, :] = dh1
            e_ref[rows, :] = dh1.astype(BF16)
            return total + jnp.sum((grad * h1 * scale).reshape(4, 8, WIDTH), axis=0)

        total = lax.fori_loop(0, ROW // 32, tile, jnp.zeros((8, WIDTH), F32), unroll=2)
        gain_grad_ref[...] = jnp.sum(total, axis=0, keepdims=True)


def whole_block(*shape):
    return pl.BlockSpec(shape, lambda j: (0,) * len(shape), pipeline_mode=pl.Buffered(1))


WIDE_BLOCK = pl.BlockSpec((2, FF_BLOCK, WIDTH), lambda j: (0, j, 0))
TALL_BLOCK = pl.BlockSpec((FF_BLOCK, WIDTH), lambda j: (j, 0))
ROW_F32 = jax.ShapeDtypeStruct((ROW, WIDTH), F32)
ROW_BF16 = jax.ShapeDtypeStruct((ROW, WIDTH), BF16)


def feed_start(n2, cot, widen, narrow, comm=None, key=0):
    rows = whole_block(ROW, WIDTH)
    return call(
        "feed_start",
        feed_start_body,
        narrow.shape[0] // FF_BLOCK,
        3,
        [n2, cot, widen, narrow],
        [rows, rows, WIDE_BLOCK, TALL_BLOCK],
        [
            ROW_F32,
            ROW_F32,
            jax.ShapeDtypeStruct(widen.shape, BF16),
            jax.ShapeDtypeStruct(narrow.shape, BF16),
        ],
        [rows, rows, WIDE_BLOCK, TALL_BLOCK],
        [pltpu.VMEM((3, ROW, FF_BLOCK), BF16)],
        comm=comm,
        key=key,
    )


def feed_end(n2, cot, h1, gain, result_part, back_part, widen, narrow, comm=None, key=0):
    rows = whole_block(ROW, WIDTH)
    line = whole_block(1, WIDTH)
    return call(
        "feed_end",
        feed_end_body,
        narrow.shape[0] // FF_BLOCK,
        3,
        [n2, cot, h1, gain, result_part, back_part, widen, narrow],
        [rows, rows, rows, line, ANY, ANY, WIDE_BLOCK, TALL_BLOCK],
        [
            ROW_F32,
            ROW_F32,
            ROW_BF16,
            jax.ShapeDtypeStruct((1, WIDTH), F32),
            jax.ShapeDtypeStruct(widen.shape, BF16),
            jax.ShapeDtypeStruct(narrow.shape, BF16),
        ],
        [rows, rows, rows, line, WIDE_BLOCK, TALL_BLOCK],
        [pltpu.VMEM((3, ROW, FF_BLOCK), BF16), pltpu.VMEM((ROW, WIDTH), F32), DMA((2,))],
        comm=comm,
        key=key,
    )


def front(attention_shard, gains_tile, feed_shards, tokens, cotangent, extras, key):
    comm = Gather((gains_tile, attention_shard, *feed_shards), (cotangent,), most=16, lag=2)
    points = [0] * 7 + [1] * 2
    rest = comm.ticks - len(points)
    points += [2 + tick * (6 * PAIRS - 2) // rest for tick in range(rest)]

    def body(
        pump, tokens_ref, mq_ref, mk_ref,
        turned_ref, row_ref, qkv_ref, o_ref, o_turned_ref, log_ref, h1_ref, n2_ref,
        normed, landed, parts, out_weights, o_all, gains, t_send, t_recv, part_sem, gains_sem,
    ):
        pair = pl.program_id(0)
        here = comm.here
        core = here.core
        across = remote(tokens_ref.at[1 - core], landed, t_send, t_recv, here.sibling())

        def fetch(p, slot):
            return pltpu.make_async_copy(
                comm.outs[1].at[:, :, :, :, pl.ds(128 * p, 128), :], parts.at[slot], part_sem.at[slot]
            )

        pump(0)

        @pl.when(pair == 0)
        def _():
            across.start()
            log_ref[...] = jnp.zeros_like(log_ref)
            row_ref[core] = tokens_ref[core]
            across.wait_recv()
            row_ref[1 - core] = landed[...]
            comm.arrived(0)
            copy = pltpu.make_async_copy(comm.outs[0], gains, gains_sem)
            copy.start()
            copy.wait()

        def gain_of(which):
            tiles = [
                gains[which * 2 + z, y, x, 0, 0:1, :] + gains[which * 2 + z, y, x, 1, 0:1, :]
                for z in range(2)
                for y in range(2)
                for x in range(2)
            ]
            return jnp.concatenate(tiles, axis=1).astype(F32)

        @pl.when(pair == 0)
        def _():
            gain = gain_of(0)
            for half in range(2):

                def tile(i, carry, half=half):
                    rows = pl.ds(pl.multiple_of(i * 32, 32), 32)
                    x = row_ref[half, rows, :].astype(F32)
                    scale = lax.rsqrt(jnp.mean(x * x, axis=-1, keepdims=True) + NORM_EPS)
                    normed[pl.ds(pl.multiple_of(half * HALF + i * 32, 32), 32), :] = (
                        x * scale * gain
                    ).astype(BF16)
                    return carry

                lax.fori_loop(0, HALF // 32, tile, 0, unroll=2)
            turned_ref[...] = normed[...].T

        pump(1)

        @pl.when(pair == 0)
        def _():
            comm.arrived(1)
            fetch(0, 0).start()

        slot = lax.rem(pair, 2)
        fetch(pair, slot).wait()
        weights = parts[slot].reshape(4, WIDTH, 128)
        three = dot(normed[...], jnp.concatenate([weights[0], weights[1], weights[2]], axis=1))
        for index in range(3):
            qkv_ref[index] = three[:, 128 * index : 128 * (index + 1)].astype(BF16)
        out_weights[pair] = weights[3]
        pump(2)
        for p in range(1, PAIRS):

            @pl.when(pair == p - 1)
            def _(p=p):
                comm.arrived(1 + p)
                fetch(p, p % 2).start()

        attend_tiles(
            lambda index: pump(3 + index),
            pair,
            qkv_ref.at[0],
            qkv_ref.at[1],
            qkv_ref.at[2],
            mq_ref,
            mk_ref,
            o_ref,
            log_ref,
        )
        mixed = o_ref[...]
        o_all[:, pl.ds(pl.multiple_of(pair * 128, 128), 128)] = mixed
        o_turned_ref[...] = mixed.T

        @pl.when(pair == PAIRS - 1)
        def _():
            across.wait_send()
            full = jnp.concatenate([out_weights[p] for p in range(PAIRS)], axis=1)
            gain = gain_of(1)
            h1_ref[...] = dot(o_all[...], full)
            for half in range(2):

                def tile(i, carry, half=half):
                    near = pl.ds(pl.multiple_of(i * 32, 32), 32)
                    rows = pl.ds(pl.multiple_of(half * HALF + i * 32, 32), 32)
                    h1 = row_ref[half, near, :].astype(F32) + h1_ref[rows, :]
                    h1_ref[rows, :] = h1
                    scale = lax.rsqrt(jnp.mean(h1 * h1, axis=-1, keepdims=True) + NORM_EPS)
                    n2_ref[rows, :] = (h1 * scale * gain).astype(BF16)
                    return carry

                lax.fori_loop(0, HALF // 32, tile, 0, unroll=2)

        pump(5)

    whole = pl.BlockSpec((ROW, 128), lambda p: (0, 0))
    turned = jax.ShapeDtypeStruct((WIDTH, ROW), BF16)
    return call(
        "front",
        body,
        PAIRS,
        6,
        [tokens, *extras],
        [VMEM_WHOLE, whole, whole],
        [
            turned,
            jax.ShapeDtypeStruct((2, HALF, WIDTH), BF16),
            jax.ShapeDtypeStruct((3, ROW, WIDTH), BF16),
            ROW_BF16,
            turned,
            jax.ShapeDtypeStruct((ROW, 128), F32),
            ROW_F32,
            ROW_BF16,
        ],
        [
            whole_block(WIDTH, ROW),
            whole_block(2, HALF, WIDTH),
            pl.BlockSpec((3, ROW, 128), lambda p: (0, 0, p)),
            pl.BlockSpec((ROW, 128), lambda p: (0, p)),
            pl.BlockSpec((128, ROW), lambda p: (p, 0)),
            whole,
            whole_block(ROW, WIDTH),
            whole_block(ROW, WIDTH),
        ],
        [
            pltpu.VMEM((ROW, WIDTH), BF16),
            pltpu.VMEM((HALF, WIDTH), BF16),
            pltpu.VMEM((2, 4, 2, 2, 2, 128, 128), BF16),
            pltpu.VMEM((PAIRS, WIDTH, 128), BF16),
            pltpu.VMEM((ROW, WIDTH), BF16),
            pltpu.VMEM((4, 2, 2, 2, 16, 128), BF16),
            DMA,
            DMA,
            DMA((2,)),
            DMA,
        ],
        comm,
        key,
        points,
    )


PART = 96


def back(
    gradients, result, e, dh1, tokens_row, gain, projected, extras, mixed, log_rows,
    attention_parts, normed_turned, mixed_turned, key,
):
    starts = [0, 3, 6, 11, 14, 17, 21, 24] + [9, 9, 19, 19, 29, 29, 34, 39]
    lags = [4] * 12 + [3, 3, 2, 1]
    comm = Reduce(
        gradients, [(PAIRS * 128, 128)], (result,), most=16, starts=starts, lags=lags
    )
    inner, made, after, middle, rest = 8, 4, 5, 6, 7
    plan = [tick // 5 * inner + tick % 5 for tick in range(5 * PAIRS)]
    plan += [(PAIRS - 1) * inner + point for point in (after, middle, rest, rest)]

    def body(
        pump, q_ref, k_ref, v_ref, mq_ref, mk_ref, o_ref, log_ref, parts_ref, rows_ref,
        e_ref, n_turned_ref, o_turned_ref, gain_ref, tokens_ref, dh1_ref,
        da_ref, gain_grad_ref,
        do, three, dk, dv, x_part, dh1_part, x_sem, dh1_sem,
    ):
        pair = pl.program_id(0)
        odd = lax.rem(pair, 2)
        pump(0)

        @pl.when(odd == 0)
        def _():
            rows = [
                jnp.concatenate(
                    [rows_ref[0, 0, 0, c, 128 * p : 128 * (p + 1), :] for p in range(PAIRS)], axis=1
                )
                for c in range(2)
            ]
            two = dot(e_ref[...], jnp.concatenate(rows, axis=0), NT).astype(BF16)
            do[0] = two[:, :128]
            do[1] = two[:, 128:]

        attend_back_tiles(
            lambda index: pump(1 + index), pair, q_ref.at[0], k_ref.at[0], v_ref.at[0],
            mq_ref, mk_ref, o_ref, do.at[odd], log_ref, three.at[odd, :, 0:128], dk, dv,
        )
        three[odd, :, 128:256] = dk[...].astype(BF16)
        three[odd, :, 256:384] = dv[...].astype(BF16)
        made_ref = comm.own[comm.outside]
        late = pair >= PAIRS - 2
        cases = (
            ((odd == 1) & jnp.logical_not(late), (0, 1)),
            ((odd == 0) & late, (0,)),
            ((odd == 1) & late, (1,)),
        )

        def joined(halves):
            return jnp.concatenate([three[half] for half in halves], axis=1)

        def make(halves):
            first = pair - odd + halves[0]
            grads = dot(n_turned_ref[...], joined(halves)).astype(BF16)
            columns = pl.ds(pl.multiple_of(first * 128, 128), 128 * len(halves))
            out_grads = dot(o_turned_ref[...], e_ref[:, columns]).astype(BF16)
            for place in range(len(halves)):
                mine = pl.ds(pl.multiple_of((first + place) * 128, 128), 128)
                for index in range(3):
                    at = 384 * place + 128 * index
                    made_ref[index, :, :, :, mine, :] = grads[:, at : at + 128].reshape(
                        2, 2, 2, 128, 128
                    )
                made_ref[3, :, :, :, mine, :] = out_grads[
                    :, 128 * place : 128 * (place + 1)
                ].reshape(2, 2, 2, 128, 128)

        def down(halves):
            columns = jnp.concatenate(
                [
                    parts_ref[index, :, :, :, 128 * half : 128 * (half + 1), :].reshape(WIDTH, 128)
                    for half in halves
                    for index in range(3)
                ],
                axis=1,
            )
            da_ref[...] += dot(joined(halves), columns, NT)

        @pl.when(pair == 0)
        def _():
            da_ref[...] = jnp.zeros_like(da_ref)

        for case, halves in cases:

            @pl.when(case)
            def _(halves=halves):
                make(halves)

        pump(made)
        for case, halves in cases:

            @pl.when(case)
            def _(halves=halves):
                down(halves)

        pump(after)

        @pl.when(pair == PAIRS - 1)
        def _():
            def fetch(i):
                rows = pl.ds(i * PART, PART)
                slot = i % 2
                return (
                    pltpu.make_async_copy(tokens_ref.at[rows, :], x_part.at[slot], x_sem.at[slot]),
                    pltpu.make_async_copy(dh1_ref.at[rows, :], dh1_part.at[slot], dh1_sem.at[slot]),
                )

            gain_row = gain_ref[...]
            total = jnp.zeros((8, WIDTH), F32)
            for copy in fetch(0):
                copy.start()
            for i in range(ROW // PART):
                if i == ROW // PART // 2:
                    pump(middle)
                if i + 1 < ROW // PART:
                    for copy in fetch(i + 1):
                        copy.start()
                for copy in fetch(i):
                    copy.wait()

                def tile(j, total, i=i):
                    near = pl.ds(pl.multiple_of(j * 32, 32), 32)
                    rows = pl.ds(pl.multiple_of(i * PART + j * 32, 32), 32)
                    x = x_part[i % 2, near, :].astype(F32)
                    grad = da_ref[rows, :]
                    scale = lax.rsqrt(jnp.mean(x * x, axis=-1, keepdims=True) + NORM_EPS)
                    lifted = gain_row * grad
                    middle = jnp.mean(x * lifted, axis=-1, keepdims=True)
                    da_ref[rows, :] = (
                        dh1_part[i % 2, near, :]
                        + scale * lifted
                        - x * (scale * scale * scale * middle)
                    )
                    return total + jnp.sum((grad * x * scale).reshape(4, 8, WIDTH), axis=0)

                total = lax.fori_loop(0, PART // 32, tile, total)
            gain_grad_ref[...] = jnp.sum(total, axis=0, keepdims=True)

        pump(rest)

    extra = pl.BlockSpec((ROW, 128), lambda p: (0, 0), pipeline_mode=pl.Buffered(1))
    line = whole_block(1, WIDTH)
    return call(
        "back",
        body,
        PAIRS,
        inner,
        [projected, projected, projected, *extras, mixed, log_rows, attention_parts, attention_parts]
        + [e, normed_turned, mixed_turned, gain, tokens_row, dh1],
        [third(0), third(1), third(2), extra, extra]
        + [
            pl.BlockSpec((ROW, 128), lambda p: (0, p)),
            whole_block(2 * PAIRS, ROW),
            pl.BlockSpec((3, 2, 2, 2, 256, 128), lambda p: (0, 0, 0, 0, p // 2, 0)),
            pl.BlockSpec(
                (1, 1, 1, 2, WIDTH, 128), lambda p: (3, p // 4, lax.rem(p // 2, 2), 0, 0, 0)
            ),
            whole_block(ROW, WIDTH),
            whole_block(WIDTH, ROW),
            whole_block(WIDTH, ROW),
            line,
            ANY,
            ANY,
        ],
        [ROW_F32, jax.ShapeDtypeStruct((1, WIDTH), F32)],
        [whole_block(ROW, WIDTH), line],
        [
            pltpu.VMEM((2, ROW, 128), BF16),
            pltpu.VMEM((2, ROW, 384), BF16),
            pltpu.VMEM((ROW, 128), F32),
            pltpu.VMEM((ROW, 128), F32),
            pltpu.VMEM((2, PART, WIDTH), BF16),
            pltpu.VMEM((2, PART, WIDTH), F32),
            DMA((2,)),
            DMA((2,)),
        ],
        comm,
        key,
        plan,
    )


def rms_scale(values, gain_vector):
    return (
        values
        * lax.rsqrt(jnp.mean(values * values, axis=-1, keepdims=True) + NORM_EPS)
        * gain_vector
    )


def adam_update(master, first, second, gradient, factors, rate, decay):
    clip_factor, first_fix, second_fix = factors
    clipped = clip_factor * gradient
    first_new = BETA_FIRST * first + (1.0 - BETA_FIRST) * clipped
    second_new = BETA_SECOND * second + (1.0 - BETA_SECOND) * clipped * clipped
    master_new = master - rate * (
        first_new / first_fix / (jnp.sqrt(second_new / second_fix) + ADAM_EPS) + decay * master
    )
    return (master_new, first_new, second_new)


def swap_halves(parts):
    core = lax.axis_index("fsdp")
    got = lax.ppermute(parts[1 - core], "fsdp", [(0, 1), (1, 0)])
    return jnp.where(core == 0, jnp.stack([parts[0], got]), jnp.stack([got, parts[1]]))


def with_half(rows, got):
    own = rows.reshape(2, HALF, WIDTH)
    first = lax.axis_index("fsdp") == 0
    return jnp.where(first, jnp.stack([own[0], got]), jnp.stack([got, own[1]]))


def local(
    own_kernels,
    tokens,
    cotangent,
    images,
    attention_weight,
    attention_first,
    attention_second,
    widen_weight,
    widen_first,
    widen_second,
    narrow_weight,
    narrow_first,
    narrow_second,
    norm_gains,
    gains_first,
    gains_second,
):
    axes = ("dp", "fsdp")
    devices = lax.axis_size(axes)
    core = lax.axis_index("fsdp")
    position = lax.axis_index(axes)
    gain_count = norm_gains.shape[0]
    units = narrow_weight.shape[0]
    split = units * 6 // 11
    attention_low = attention_weight.astype(BF16)
    widen_rows = widen_weight.T.reshape(2, units, WIDTH)
    gains_low = norm_gains.astype(BF16)
    feed_low = [
        (
            widen_rows[:, part].astype(BF16).reshape(-1, WIDTH),
            narrow_weight[part].astype(BF16),
        )
        for part in (slice(None, split), slice(split, None))
    ]
    grid = (4, 2, 2, 2)

    def fetch(shards):
        return [lax.all_gather(shard, axes, axis=0, tiled=True) for shard in shards]

    def summed(gradients):
        return [
            lax.psum_scatter(
                g.astype(F32).reshape(-1, 128), axes, scatter_dimension=0, tiled=True
            ).reshape(-1, WIDTH)
            for g in gradients
        ]

    def other_half(parts):
        return lax.ppermute(
            lax.dynamic_index_in_dim(parts, 1 - core, 0, keepdims=False), "fsdp", [(0, 1), (1, 0)]
        )

    def as_feed(shards):
        return shards[0].reshape(2, -1, WIDTH), shards[1].reshape(-1, WIDTH)

    def as_shards(*gradients):
        return [g.reshape(grid + (-1, WIDTH)) for g in gradients]

    counts = lax.dynamic_index_in_dim(images[:, 0, :], core, 0, keepdims=False)
    extras = segment_lanes(counts)
    gather_b = None
    if own_kernels:
        places = lax.broadcasted_iota(jnp.int32, (16, 2, gain_count), 0) * 2
        places = places + lax.broadcasted_iota(jnp.int32, (16, 2, gain_count), 1)
        gains_tile = jnp.where(places == core, gains_low, jnp.zeros_like(gains_low)).reshape(16, -1)
        columns = attention_low.reshape(-1, PAIRS, 2 * HD).transpose(1, 0, 2).reshape(-1, 2 * HD)
        (
            (normed_turned, tokens_row, projected, mixed, mixed_turned, log_columns, h1, n2),
            (gains_full, attention_parts, *feed_a, cotangent_row),
        ) = front(columns, gains_tile, feed_low[0], tokens, cotangent, extras, 0)
        gains_full = gains_full[:, :, :, :, 0, :].sum(axis=3).reshape(-1)
        gather_b = Gather(feed_low[1])
        cot = cotangent_row.reshape(ROW, WIDTH)
        inputs = tokens_row.reshape(ROW, WIDTH).astype(F32)
        first_gain = gains_full[:WIDTH].astype(F32)
        second_gain = gains_full[WIDTH:].astype(F32)
    else:
        attention_full, gains_full = fetch((attention_low, gains_low))
        first = core == 0
        tokens_row, cotangent_row = (
            jnp.where(first, jnp.stack([a[0], got]), jnp.stack([got, a[1]]))
            for a, got in ((a, other_half(a)) for a in (tokens, cotangent))
        )
        attention = attention_full.reshape(4, WIDTH, WIDTH)
        cot = cotangent_row.reshape(ROW, WIDTH)
        inputs = tokens_row.reshape(ROW, WIDTH).astype(F32)
        first_gain = gains_full[:WIDTH].astype(F32)
        second_gain = gains_full[WIDTH:].astype(F32)
        normed = rms_scale(inputs, first_gain).astype(BF16)
        projected = jnp.einsum(
            "sd,jde->jse", normed, attention[:3], preferred_element_type=F32
        ).astype(BF16)
        (mixed, log_columns), _ = attend(projected, extras)
        h1 = inputs + dot(mixed, attention[3])
        n2 = rms_scale(h1, second_gain).astype(BF16)
    log_rows = log_columns[:, : WIDTH // HD].T
    widen_a, narrow_a = as_feed(feed_a if own_kernels else fetch(feed_low[0]))
    (result_part, back_part, *grads_a), feed_b = feed_start(
        n2, cot, widen_a, narrow_a, gather_b, 2
    )
    widen_b, narrow_b = as_feed(feed_b if own_kernels else fetch(feed_low[1]))
    (result, dh1, e, grad_gain_two, *grads_b), sums_a = feed_end(
        n2,
        cot,
        h1,
        second_gain[None],
        result_part,
        back_part,
        widen_b,
        narrow_b,
        Reduce(as_shards(*grads_a)) if own_kernels else None,
        3,
    )
    if own_kernels:
        (input_rows, grad_gain_one), (*sums_b, attention_sum, got_result) = back(
            as_shards(*grads_b),
            result.reshape(2, HALF, WIDTH),
            e,
            dh1,
            tokens_row.reshape(ROW, WIDTH),
            first_gain[None],
            projected,
            extras,
            mixed,
            log_rows,
            attention_parts,
            normed_turned,
            mixed_turned,
            4,
        )
        got_input, gains_total, square_total = settle(
            input_rows.reshape(2, HALF, WIDTH),
            jnp.concatenate([grad_gain_one, grad_gain_two]).reshape(16, 128),
            [*sums_a, *sums_b, attention_sum],
            5,
        )
        attention_sum = (
            attention_sum.reshape(PAIRS, -1, 128).transpose(1, 0, 2).reshape(-1, WIDTH)
        )
        gains_sum = lax.dynamic_slice_in_dim(
            gains_total.reshape(-1), position * gain_count, gain_count
        )
        squares = square_total[0, 0]
    else:
        grad_out = dot(mixed, e, TN).astype(BF16)
        grad_mixed = dot(e, attention[3], NT).astype(BF16)
        (grad_projected,), _ = attend_back(projected, extras, mixed, grad_mixed, log_rows)
        grad_qkv = jnp.einsum(
            "sd,jse->jde", normed, grad_projected, preferred_element_type=F32
        ).astype(BF16)
        grad_normed = jnp.einsum(
            "jse,jde->sd", grad_projected, attention[:3], preferred_element_type=F32
        )
        scale = lax.rsqrt(jnp.mean(inputs * inputs, axis=-1, keepdims=True) + NORM_EPS)
        lifted = first_gain * grad_normed
        inner = jnp.mean(inputs * lifted, axis=-1, keepdims=True)
        input_rows = dh1 + scale * lifted - inputs * (scale * scale * scale * inner)
        grad_gain_one = jnp.sum(grad_normed * inputs * scale, axis=0)
        grad_attention = jnp.concatenate([grad_qkv, grad_out[None]], axis=0)
        grad_gains = jnp.concatenate([grad_gain_one, grad_gain_two[0]])
        sums_a, sums_b, (attention_sum,) = summed(grads_a), summed(grads_b), summed([grad_attention])
        gains_sum = lax.psum_scatter(grad_gains, axes, scatter_dimension=0, tiled=True)
        squares = lax.psum(
            sum(jnp.sum(g * g) for g in (*sums_a, *sums_b, attention_sum, gains_sum)), axes
        )
        got_result = other_half(result.reshape(2, HALF, WIDTH))
        got_input = other_half(input_rows.reshape(2, HALF, WIDTH))
    widen_sum = jnp.concatenate(
        [sums_a[0].reshape(2, -1, WIDTH), sums_b[0].reshape(2, -1, WIDTH)], axis=1
    ).reshape(-1, WIDTH)
    narrow_sum = jnp.concatenate([sums_a[1], sums_b[1]], axis=0)
    grad_norm = jnp.sqrt(squares)
    clip_factor = jnp.minimum(1.0, CLIP_LIMIT / (grad_norm + 1e-06))
    step_value = jnp.float32(STEP_VALUE)
    factors = (
        clip_factor,
        1.0 - jnp.power(jnp.float32(BETA_FIRST), step_value),
        1.0 - jnp.power(jnp.float32(BETA_SECOND), step_value),
    )
    return (
        with_half(result, got_result),
        with_half(input_rows, got_input),
        *adam_update(
            attention_weight,
            attention_first,
            attention_second,
            attention_sum,
            factors,
            MATRIX_RATE,
            DECAY,
        ),
        *adam_update(
            widen_weight, widen_first, widen_second, widen_sum.T, factors, MATRIX_RATE, DECAY
        ),
        *adam_update(
            narrow_weight, narrow_first, narrow_second, narrow_sum, factors, MATRIX_RATE, DECAY
        ),
        *adam_update(norm_gains, gains_first, gains_second, gains_sum, factors, GAIN_RATE, 0.0),
        grad_norm,
    )


def solution(mesh):
    both = ("dp", "fsdp")
    rows = P(None, both, None)
    tall = P(both, None)
    wide = P(None, both)
    flat = P(both)
    weights = (tall, tall, tall, wide, wide, wide, tall, tall, tall, flat, flat, flat)
    own_kernels = dict(mesh.shape) == {"dp": 16, "fsdp": 2}
    return jax.shard_map(
        functools.partial(local, own_kernels),
        mesh=mesh,
        in_specs=(rows, rows, P(None, "dp", None)) + weights,
        out_specs=(rows, rows) + weights + (P(),),
        check_vma=False,
    )
```
